32 devices in a mesh: dp: 8 (over y, x, core), tensor: 4 (over z).
Axes of the slice: x: 2, y: 2, z: 4, core: 2. Of those that a mesh axis runs over, the one named last changes fastest.
Arguments:
- inputs: bfloat16 [8192, 1024], P(('dp', 'tensor')), may hold values from -6 to 6
- segments: int32 [8, 1024], P('dp'), may hold values from 0 to 3, never falling along the last dimension, each value on 1 to 512 neighbouring positions
- query_weight: bfloat16 [1024, 1024], P(None, 'tensor'), may hold values from -0.1875 to 0.1875
- key_weight: bfloat16 [1024, 1024], P(None, 'tensor'), may hold values from -0.1875 to 0.1875
- value_weight: bfloat16 [1024, 1024], P(None, 'tensor'), may hold values from -0.1875 to 0.1875
- gate_weight: bfloat16 [1024, 1024], P(None, 'tensor'), may hold values from -0.1875 to 0.1875
- out_weight: bfloat16 [1024, 1024], P('tensor'), may hold values from -0.1875 to 0.1875
- left_weight: bfloat16 [1024, 2816], P(None, 'tensor'), may hold values from -0.1875 to 0.1875
- right_weight: bfloat16 [1024, 2816], P(None, 'tensor'), may hold values from -0.1875 to 0.1875
- down_weight: bfloat16 [2816, 1024], P('tensor'), may hold values from -0.109375 to 0.109375
- norm_first: float32 [1024], replicated, may hold values from 0.1 to 1.9
- norm_second: float32 [1024], replicated, may hold values from 0.1 to 1.9
- cotangent: bfloat16 [8192, 1024], P(('dp', 'tensor')), may hold values from -6 to 6
Outputs:
- block_out: bfloat16 [8192, 1024], P(('dp', 'tensor'))
- block_grad: bfloat16 [8192, 1024], P(('dp', 'tensor'))
- query_grad: float32 [1024, 1024], P(None, 'tensor')
- key_grad: float32 [1024, 1024], P(None, 'tensor')
- value_grad: float32 [1024, 1024], P(None, 'tensor')
- gate_grad: float32 [1024, 1024], P(None, 'tensor')
- out_grad: float32 [1024, 1024], P('tensor')
- left_grad: float32 [1024, 2816], P(None, 'tensor')
- right_grad: float32 [1024, 2816], P(None, 'tensor')
- down_grad: float32 [2816, 1024], P('tensor')
- first_grad: float32 [1024], replicated
- second_grad: float32 [1024], replicated
The draws below stay inside these ranges and needn't reach their ends.
Inputs may be any that keep to these rules, and one draw needn't show every extreme that they name: `segments`: each row holds 4 documents; numbers never fall along a row; each document has 1 to 512 tokens and one of each row exactly 512.
All inputs are finite; a program needn't handle non-finite values.
Results may differ from the reference program's by a relative error of at most 0.02.
Values may be sent and summed in bfloat16 or wider, within the bound.
A program may use at most 128 MiB of HBM per device.

```python
import math
import jax
import jax.numpy as jnp
import numpy as np
from jax import lax

D = 1024
HEADS = 16
FF = 2816
LEN = 1024
DOCS = 4
MOST = 512
ROWS = 8
TOKENS = 8192


def steps_of(own_key, dims, shards, low, high):
    factor_of, own = 1.0, jax.random.fold_in(own_key, 6)
    for axis_at, parts in shards:
        steps = jnp.exp(jax.random.uniform(jax.random.fold_in(own, axis_at), (parts,), jnp.float32, low / len(shards), high / len(shards)))
        factor_of = factor_of * jnp.repeat(steps, dims[axis_at] // parts).reshape([-1 if axis == axis_at else 1 for axis in range(len(dims))])
    return factor_of


def split_up(amount, total, limit, skew):
    portions = [(1 << 20) // math.isqrt(grade ** skew) + 1 for grade in range(2, amount + 1)]
    rest, holding = total - limit - (amount - 1), [1] * (amount - 1)
    while rest > 0:
        movable = [i for i in range(amount - 1) if holding[i] < limit]
        mass, left = sum([portions[i] for i in movable]), rest
        for i in movable:
            more = min(limit - holding[i], max(1, left * portions[i] // mass), rest)
            holding[i] = holding[i] + more
            rest = rest - more
    return np.array([limit] + holding)


def uneven_parts(key, count, total, most, slope):
    if count == 2:
        one = jax.random.randint(key, (), max(1, total - most), min(most, total - 1) + 1)
        return jnp.stack([one, total - one])
    sizes = jnp.asarray(split_up(count, total, most, slope), jnp.int32)
    twos = (count - 1) // 2
    source_of, sink = sizes[1:1 + 2 * twos:2], sizes[2:2 + 2 * twos:2]
    room = jnp.minimum(source_of - 1, most - sink)
    shifted = jax.random.randint(jax.random.fold_in(key, 1), (twos,), 0, 1 << 20) % (room + 1)
    sizes = sizes.at[1:1 + 2 * twos:2].set(source_of - shifted).at[2:2 + 2 * twos:2].set(sink + shifted)
    return sizes[jax.random.permutation(jax.random.fold_in(key, 2), count)]


def gaussian(key, dims, deviation, reach, cuts=(), held_as=jnp.bfloat16):
    values = jax.random.normal(key, dims, jnp.float32) * deviation
    if len(cuts) > 0:
        values = steps_of(key, dims, cuts, -0.22, 0.18) * values
    return jnp.clip(values, min=-reach, max=reach).astype(held_as)


def setup_inputs(seed: int = 0) -> dict:
    key_list = jax.random.split(jax.random.key(seed), 14)
    return {
        "inputs": gaussian(key_list[0], (TOKENS, D), 1.0, 6.0, ((0, 32),)),
        "segments": jax.vmap(lambda own: jnp.searchsorted(jnp.cumsum(uneven_parts(own, DOCS, LEN, MOST, 1)), jnp.arange(LEN), side="right"))(jax.random.split(key_list[1], ROWS)).reshape((ROWS, LEN)).astype(jnp.int32),
        "query_weight": gaussian(key_list[2], (D, D), D ** -0.5, 0.1875, ((1, 4),)),
        "key_weight": gaussian(key_list[3], (D, D), D ** -0.5, 0.1875, ((1, 4),)),
        "value_weight": gaussian(key_list[4], (D, D), D ** -0.5, 0.1875, ((1, 4),)),
        "gate_weight": gaussian(key_list[5], (D, D), D ** -0.5, 0.1875, ((1, 4),)),
        "out_weight": gaussian(key_list[6], (D, D), D ** -0.5, 0.1875, ((0, 4),)),
        "left_weight": gaussian(key_list[7], (D, FF), D ** -0.5, 0.1875, ((1, 4),)),
        "right_weight": gaussian(key_list[8], (D, FF), D ** -0.5, 0.1875, ((1, 4),)),
        "down_weight": gaussian(key_list[9], (FF, D), FF ** -0.5, 0.109375, ((0, 4),)),
        "norm_first": jnp.clip(1.0 + 0.18 * jax.random.normal(key_list[10], (D,), jnp.float32), 0.1, 1.9),
        "norm_second": jnp.clip(1.0 + 0.18 * jax.random.normal(key_list[11], (D,), jnp.float32), 0.1, 1.9),
        "cotangent": gaussian(key_list[12], (TOKENS, D), 1.0, 6.0, ((0, 32),)),
    }


@jax.custom_vjp
def low(v):
    return lax.optimization_barrier(v.astype(jnp.bfloat16)).astype(jnp.float32)

@jax.custom_vjp
def low_back(v):
    return v

def low_keep(v):
    return (low(v), None)

def low_pass(kept, grad):
    return (grad,)

def back_keep(v):
    return (v, None)

def back_low(kept, grad):
    return (low(grad),)
low.defvjp(low_keep, low_pass)
low_back.defvjp(back_keep, back_low)
EPS = 1e-05
HIGH = lax.Precision.HIGHEST

def matmul(left_side, right_side):
    return jnp.dot(left_side, right_side, precision=HIGH)

def simple_norm(values, gain):
    return values * lax.rsqrt(lax.optimization_barrier(jnp.mean(values * values, axis=-1, keepdims=True)) + EPS) * gain

def layer(row_in, row_seg, query_weight, key_weight, value_weight, gate_weight, out_weight, left_weight, right_weight, down_weight, norm_first, norm_second):
    length = row_in.shape[0]
    head_size = D // HEADS
    normed = low(simple_norm(row_in, norm_first))
    query_raw = low_back(matmul(normed, query_weight))
    key_raw = low_back(matmul(normed, key_weight))
    value_raw = low(low_back(matmul(normed, value_weight)))
    gate_raw = low_back(matmul(normed, gate_weight))
    query_pos = low(jax.nn.softplus(query_raw)).reshape(length, HEADS, head_size)
    key_pos = low(jax.nn.softplus(key_raw)).reshape(length, HEADS, head_size)
    value_pos = value_raw.reshape(length, HEADS, head_size)
    positions = jnp.arange(length)
    doc_mask = (row_seg[:, None] == row_seg[None, :]) & (positions[:, None] >= positions[None, :])
    raw_scores = jnp.einsum('thd,shd->hts', query_pos, key_pos, precision=HIGH)
    raw_scores = jnp.where(doc_mask[None], raw_scores, jnp.zeros_like(raw_scores))
    scores = low(low_back(raw_scores))
    mixed_heads = low_back(jnp.einsum('hts,shd->thd', scores, value_pos, precision=HIGH))
    head_norm = mixed_heads * lax.rsqrt(lax.optimization_barrier(jnp.mean(mixed_heads * mixed_heads, axis=-1, keepdims=True)) + EPS)
    gated = low(head_norm.reshape(length, D) * jax.nn.sigmoid(gate_raw))
    branch = low_back(matmul(gated, out_weight))
    residual = row_in + branch
    second = low(simple_norm(residual, norm_second))
    left_out = low_back(matmul(second, left_weight))
    right_out = low_back(matmul(second, right_weight))
    product = low(left_out * right_out)
    return residual + low_back(matmul(product, down_weight))

def reference(inputs, segments, query_weight, key_weight, value_weight, gate_weight, out_weight, left_weight, right_weight, down_weight, norm_first, norm_second, cotangent):
    weights = tuple((w.astype(jnp.float32) for w in (query_weight, key_weight, value_weight, gate_weight, out_weight, left_weight, right_weight, down_weight, norm_first, norm_second)))
    rows_in = inputs.astype(jnp.float32).reshape(ROWS, LEN, D)
    rows_ct = cotangent.astype(jnp.float32).reshape(ROWS, LEN, D)

    def one_row(totals, item):
        row_in, row_seg, row_ct = item

        def forward(values, *params):
            return layer(values, row_seg, *params)
        result, pull = jax.vjp(forward, row_in, *weights)
        grads = pull(row_ct)
        summed = tuple((a + b for a, b in zip(totals, grads[1:])))
        return (summed, (result, grads[0]))
    zeros = tuple((jnp.zeros(w.shape, jnp.float32) for w in weights))
    totals, (results, in_grads) = lax.scan(one_row, zeros, (rows_in, segments, rows_ct))
    block_out = results.reshape(TOKENS, D).astype(jnp.bfloat16)
    block_grad = in_grads.reshape(TOKENS, D).astype(jnp.bfloat16)
    return (block_out, block_grad, totals[0], totals[1], totals[2], totals[3], totals[4], totals[5], totals[6], totals[7], totals[8], totals[9])
```

```python
import jax
import jax.numpy as jnp
from jax import lax
from jax.sharding import PartitionSpec as P

D = 1024
HEADS = 16


EPS = 1e-05


def rms_scale(values):
    return lax.rsqrt(jnp.mean(values * values, axis=-1, keepdims=True) + EPS)


def norm_back(grad_normed, values, scale, gain):
    weighted = grad_normed * gain
    return scale * weighted - values * scale * scale * scale * jnp.mean(
        weighted * values, axis=-1, keepdims=True
    )


def attention_scores(query_pos, key_pos, doc_mask):
    raw_scores = jnp.einsum(
        "rthd,rshd->rhts", query_pos, key_pos, preferred_element_type=jnp.float32
    )
    return jnp.where(doc_mask[:, None], raw_scores, 0.0).astype(jnp.bfloat16)


def per_device(
    inputs,
    segments,
    query_weight,
    key_weight,
    value_weight,
    gate_weight,
    out_weight,
    left_weight,
    right_weight,
    down_weight,
    norm_first,
    norm_second,
    cotangent,
):
    own_rows = inputs.astype(jnp.float32)
    rows_here, length = segments.shape
    all_tokens = rows_here * length
    local_width = query_weight.shape[1]
    head_size = D // HEADS
    heads_here = local_width // head_size
    four_shape = (rows_here, length, heads_here, head_size)
    scale_one = rms_scale(own_rows)
    normed_own = (own_rows * scale_one * norm_first).astype(jnp.bfloat16)
    normed_all = lax.all_gather(normed_own, "tensor", axis=0, tiled=True)
    joined_weight = jnp.concatenate((query_weight, key_weight, value_weight, gate_weight), axis=1)
    projected = jnp.dot(normed_all, joined_weight, preferred_element_type=jnp.float32)
    query_raw = projected[:, :local_width]
    key_raw = projected[:, local_width : 2 * local_width]
    value_raw = projected[:, 2 * local_width : 3 * local_width]
    gate_raw = projected[:, 3 * local_width :]
    query_pos = jax.nn.softplus(query_raw).astype(jnp.bfloat16).reshape(four_shape)
    key_pos = jax.nn.softplus(key_raw).astype(jnp.bfloat16).reshape(four_shape)
    value_pos = value_raw.astype(jnp.bfloat16).reshape(four_shape)
    later = lax.broadcasted_iota(jnp.int32, (length, length), 0) >= lax.broadcasted_iota(
        jnp.int32, (length, length), 1
    )
    doc_mask = (segments[:, :, None] == segments[:, None, :]) & later[None]
    scores = attention_scores(query_pos, key_pos, doc_mask)
    mixed_heads = jnp.einsum(
        "rhts,rshd->rthd", scores, value_pos, preferred_element_type=jnp.float32
    )
    head_scale = rms_scale(mixed_heads)
    head_norm = (mixed_heads * head_scale).reshape(all_tokens, local_width)
    gate_open = jax.nn.sigmoid(gate_raw)
    gated = (head_norm * gate_open).astype(jnp.bfloat16)
    branch = lax.psum_scatter(
        jnp.dot(gated, out_weight, preferred_element_type=jnp.float32).astype(jnp.bfloat16),
        "tensor",
        scatter_dimension=0,
        tiled=True,
    ).astype(jnp.float32)
    residual = own_rows + branch
    scale_two = rms_scale(residual)
    second_own = (residual * scale_two * norm_second).astype(jnp.bfloat16)
    second_all = lax.all_gather(second_own, "tensor", axis=0, tiled=True)
    left_out = jnp.dot(second_all, left_weight, preferred_element_type=jnp.float32)
    right_out = jnp.dot(second_all, right_weight, preferred_element_type=jnp.float32)
    product = (left_out * right_out).astype(jnp.bfloat16)
    ffn_share = lax.psum_scatter(
        jnp.dot(product, down_weight, preferred_element_type=jnp.float32).astype(jnp.bfloat16),
        "tensor",
        scatter_dimension=0,
        tiled=True,
    ).astype(jnp.float32)
    block_out = (residual + ffn_share).astype(jnp.bfloat16)
    upstream = cotangent.astype(jnp.float32)
    down_in = lax.all_gather(cotangent, "tensor", axis=0, tiled=True)
    down_grad = jnp.einsum("tf,td->fd", product, down_in, preferred_element_type=jnp.float32)
    prod_grad = jnp.einsum("td,fd->tf", down_in, down_weight, preferred_element_type=jnp.float32)
    left_back = (prod_grad * right_out).astype(jnp.bfloat16)
    right_back = (prod_grad * left_out).astype(jnp.bfloat16)
    left_grad = jnp.einsum("tc,tf->cf", second_all, left_back, preferred_element_type=jnp.float32)
    right_grad = jnp.einsum("tc,tf->cf", second_all, right_back, preferred_element_type=jnp.float32)
    second_back = lax.psum_scatter(
        (
            jnp.einsum("tf,cf->tc", left_back, left_weight, preferred_element_type=jnp.float32)
            + jnp.einsum("tf,cf->tc", right_back, right_weight, preferred_element_type=jnp.float32)
        ).astype(jnp.bfloat16),
        "tensor",
        scatter_dimension=0,
        tiled=True,
    ).astype(jnp.float32)
    second_part = jnp.sum(second_back * residual * scale_two, axis=0)
    resid_grad = upstream + norm_back(second_back, residual, scale_two, norm_second)
    mixer_in = lax.all_gather(resid_grad.astype(jnp.bfloat16), "tensor", axis=0, tiled=True)
    out_grad = jnp.einsum("tc,td->cd", gated, mixer_in, preferred_element_type=jnp.float32)
    gated_back = jnp.einsum("td,cd->tc", mixer_in, out_weight, preferred_element_type=jnp.float32)
    gate_back = (gated_back * head_norm * gate_open * (1.0 - gate_open)).astype(jnp.bfloat16)
    norm_grad = (gated_back * gate_open).reshape(four_shape)
    mixed_back = (
        head_scale * norm_grad
        - mixed_heads
        * head_scale
        * head_scale
        * head_scale
        * jnp.mean(norm_grad * mixed_heads, axis=-1, keepdims=True)
    ).astype(jnp.bfloat16)
    scores_again = attention_scores(query_pos, key_pos, doc_mask)
    value_back = jnp.einsum(
        "rhts,rthd->rshd", scores_again, mixed_back, preferred_element_type=jnp.float32
    ).astype(jnp.bfloat16)
    score_back = jnp.einsum(
        "rthd,rshd->rhts", mixed_back, value_pos, preferred_element_type=jnp.float32
    )
    score_back = jnp.where(doc_mask[:, None], score_back, 0.0).astype(jnp.bfloat16)
    query_back = jnp.einsum(
        "rhts,rshd->rthd", score_back, key_pos, preferred_element_type=jnp.float32
    )
    query_back = (query_back * jax.nn.sigmoid(query_raw.reshape(four_shape))).astype(jnp.bfloat16)
    key_back = jnp.einsum(
        "rhts,rthd->rshd", score_back, query_pos, preferred_element_type=jnp.float32
    )
    key_back = (key_back * jax.nn.sigmoid(key_raw.reshape(four_shape))).astype(jnp.bfloat16)
    back_all = jnp.concatenate(
        (
            query_back.reshape(all_tokens, local_width),
            key_back.reshape(all_tokens, local_width),
            value_back.reshape(all_tokens, local_width),
            gate_back,
        ),
        axis=1,
    )
    joined_grad = jnp.einsum("tc,tq->cq", normed_all, back_all, preferred_element_type=jnp.float32)
    query_grad = joined_grad[:, :local_width]
    key_grad = joined_grad[:, local_width : 2 * local_width]
    value_grad = joined_grad[:, 2 * local_width : 3 * local_width]
    gate_grad = joined_grad[:, 3 * local_width :]
    first_back = lax.psum_scatter(
        jnp.einsum("tq,cq->tc", back_all, joined_weight, preferred_element_type=jnp.float32).astype(
            jnp.bfloat16
        ),
        "tensor",
        scatter_dimension=0,
        tiled=True,
    ).astype(jnp.float32)
    first_part = jnp.sum(first_back * own_rows * scale_one, axis=0)
    block_grad = (resid_grad + norm_back(first_back, own_rows, scale_one, norm_first)).astype(
        jnp.bfloat16
    )
    query_grad, key_grad, value_grad, gate_grad, out_grad, left_grad, right_grad, down_grad = (
        total.astype(jnp.float32)
        for total in lax.psum(
            tuple(
                part.astype(jnp.bfloat16)
                for part in (
                    query_grad,
                    key_grad,
                    value_grad,
                    gate_grad,
                    out_grad,
                    left_grad,
                    right_grad,
                    down_grad,
                )
            ),
            "dp",
        )
    )
    first_grad, second_grad = lax.psum((first_part, second_part), ("dp", "tensor"))
    return (
        block_out,
        block_grad,
        query_grad,
        key_grad,
        value_grad,
        gate_grad,
        out_grad,
        left_grad,
        right_grad,
        down_grad,
        first_grad,
        second_grad,
    )


def solution(mesh):
    return jax.shard_map(
        per_device,
        mesh=mesh,
        in_specs=(
            P(("dp", "tensor"), None),
            P("dp", None),
            P(None, "tensor"),
            P(None, "tensor"),
            P(None, "tensor"),
            P(None, "tensor"),
            P("tensor", None),
            P(None, "tensor"),
            P(None, "tensor"),
            P("tensor", None),
            P(),
            P(),
            P(("dp", "tensor"), None),
        ),
        out_specs=(
            P(("dp", "tensor"), None),
            P(("dp", "tensor"), None),
            P(None, "tensor"),
            P(None, "tensor"),
            P(None, "tensor"),
            P(None, "tensor"),
            P("tensor", None),
            P(None, "tensor"),
            P(None, "tensor"),
            P("tensor", None),
            P(),
            P(),
        ),
        check_vma=False,
    )
```

```python
import functools

import jax
import jax.numpy as jnp
from jax import lax
from jax.experimental import pallas as pl
from jax.experimental.pallas import tpu as pltpu
from jax.sharding import PartitionSpec as P

EPS = 1e-05
HEAD = 64
BF = jnp.bfloat16
F32 = jnp.float32
MESH = pl.DeviceIdType.MESH
ANY = pl.BlockSpec(memory_space=pl.ANY)
INNER = pl.BlockSpec(memory_space=pltpu.VMEM)
PIECE_BITS = 3


def dot(a, b):
    return lax.dot_general(a, b, (((1,), (0,)), ((), ())), preferred_element_type=F32)


def dot_t(a, b):
    return lax.dot_general(a, b, (((1,), (1,)), ((), ())), preferred_element_type=F32)


class Place:
    def __init__(self, dp_size):
        self.i = lax.axis_index("dp")
        self.t = lax.axis_index("tensor")
        self.half = lax.rem(self.t, 2)
        self.pair = self.t // 2
        self.bits = dp_size.bit_length() - 1
        self.mate = {"tensor": self.t + 1 - 2 * self.half}
        self.twin = {"tensor": self.t + 2 - 4 * self.pair}

    def bit(self, b):
        return lax.rem(self.i // (1 << b), 2)

    def over(self, b):
        return {"dp": self.i + (1 << b) * (1 - 2 * self.bit(b))}

    def greet(self):
        barrier = pltpu.get_barrier_semaphore()
        peers = [self.mate, self.twin] + [self.over(b) for b in range(self.bits)]
        for peer in peers:
            pl.semaphore_signal(barrier, inc=1, device_id=peer, device_id_type=MESH)
        pl.semaphore_wait(barrier, len(peers))


class Links:
    def __init__(self, send_sem, recv_sem):
        self.send_sem, self.recv_sem, self.count, self.open = send_sem, recv_sem, 0, []

    def start(self, source, target, peer):
        copy = pltpu.make_async_remote_copy(
            src_ref=source,
            dst_ref=target,
            send_sem=self.send_sem.at[self.count],
            recv_sem=self.recv_sem.at[self.count],
            device_id=peer,
            device_id_type=MESH,
        )
        self.count += 1
        copy.start()
        self.open.append(copy)
        return copy

    def finish(self):
        for copy in self.open:
            copy.wait_send()


class Moves:
    def __init__(self, sem):
        self.sem, self.count, self.open = sem, 0, []

    def start(self, source, target):
        copy = pltpu.make_async_copy(source, target, self.sem.at[self.count])
        self.count += 1
        copy.start()
        self.open.append(copy)
        return copy

    def wait(self, copy):
        copy.wait()
        self.open = [other for other in self.open if other is not copy]

    def finish(self):
        for copy in list(self.open):
            self.wait(copy)


def part(ref, lead, axis, first, count):
    window = pl.ds(first, count)
    return ref.at[lead + ((window, slice(None)) if axis == 0 else (slice(None), window))]


def piece_of(place, order):
    total = 0
    for b in order:
        total = 2 * total + place.bit(b)
    return total


class Gather:
    def __init__(self, place, links, ref, lead, axis, order):
        self.place, self.links, self.ref, self.lead, self.axis, self.order = place, links, ref, lead, axis, order
        self.size = ref.shape[len(ref.shape) - 2 + axis] // (1 << len(order))
        self.piece = piece_of(place, order)
        self.copy, self.stage = None, 0

    def block(self, shard, width):
        first = (self.piece // width) * (width * self.size)
        return part(self.ref, (shard,) + self.lead, self.axis, pl.multiple_of(first, self.size), width * self.size)

    def begin(self):
        self.copy = self.links.start(self.block(0, 1), self.block(1, 1), self.place.twin)

    def advance(self):
        self.copy.wait_recv()
        if self.stage < len(self.order):
            block = self.block(1, 1 << self.stage)
            self.copy = self.links.start(block, block, self.place.over(self.order[-1 - self.stage]))
        self.stage += 1

    def complete(self):
        while self.stage <= len(self.order):
            self.advance()


def rows_loop(count, size, body):
    def step(k, carry):
        body(pl.multiple_of(k * size, size))
        return carry

    lax.fori_loop(0, count // size, step, 0)


def softplus_and_slope(values):
    tail = jnp.exp(-jnp.abs(values))
    soft = jnp.maximum(values, 0.0) + jnp.log1p(tail)
    slope = jnp.where(values >= 0, 1.0, tail) / (1.0 + tail)
    return soft, slope


def sigmoid(values):
    tail = jnp.exp(-jnp.abs(values))
    return jnp.where(values >= 0, 1.0, tail) / (1.0 + tail)


def head_of(shape, axis):
    return lax.broadcasted_iota(jnp.int32, shape, axis) // HEAD


def same_head(width):
    return head_of((width, width), 0) == head_of((width, width), 1)


def head_mean(values):
    ones = jnp.where(same_head(values.shape[-1]), 1.0 / HEAD, 0.0).astype(BF)
    return dot(values.astype(BF), ones)


def fold(state):
    width = state.shape[-1]
    state = jnp.where(same_head(width), state, 0.0)
    return (state[:, : width // 2] + state[:, width // 2 :]).astype(BF)


def unfold(state):
    both = jnp.concatenate((state, state), axis=1)
    return jnp.where(same_head(both.shape[-1]), both, jnp.zeros_like(both))


def only_head(values, head):
    return jnp.where(head_of(values.shape, 1) == head, values, jnp.zeros_like(values))


def near_marks(place, segc_ref, tokens):
    own = segc_ref[pl.ds(pl.multiple_of(place.pair * tokens, tokens), tokens), :]
    return own == segc_ref[tokens - 1 : tokens, :]


def doc_mask(place, segr_ref, segc_ref, mask_ref, tokens, later):
    offset = pl.multiple_of(place.pair * tokens, tokens)
    across = segr_ref[:, pl.ds(offset, tokens)]

    def body(first):
        down = segc_ref[pl.ds(pl.multiple_of(offset + first, 64), 64), :]
        at = first + lax.broadcasted_iota(jnp.int32, (64, tokens), 0)
        col = lax.broadcasted_iota(jnp.int32, (64, tokens), 1)
        order = col >= at if later else col <= at
        mask_ref[pl.ds(first, 64), :] = jnp.where((down == across) & order, 1.0, 0.0).astype(BF)

    rows_loop(tokens, 64, body)


def forward_kernel(
    dp_size,
    x_hbm, segr_ref, segc_ref, wq, wk, wv, wz, wo, wl, wr, wd, g1_ref, g2_ref, cot_hbm,
    normed_t_out, second_t_out, gated_t_out, product_t_out, dleft_out, dright_out, cot_out,
    qp_out, kp_out, vl_out, sq_out, sk_out, hn_out, rr_out, sz_out, state_out,
    joined_out, ow_out, dres_out, block_out, gain_out,
    x_ref, normed, normed_t, joined, ow, lw, rw, dw, qp, kp, vl, sq, sk, hn, rr, sz, gated, gated_t, mask,
    state_send, state_recv, branch_send, branch_recv, resid, own_sum, second, second_t, cot,
    product, product_t, dleft, dright, ffn_send, ffn_recv, ffn_own, back_send, back_recv, dres, blk, gain,
    send_sem, recv_sem, move_sem,
):
    place = Place(dp_size)
    links, moves = Links(send_sem, recv_sem), Moves(move_sem)
    own, width = x_ref.shape
    tokens = 2 * own
    mine = pl.multiple_of(place.half * own, own)
    theirs = pl.multiple_of((1 - place.half) * own, own)

    x_in = moves.start(x_hbm, x_ref)
    joined_in = [moves.start(w, joined.at[0, j]) for j, w in enumerate((wq, wk, wv, wz))]
    ow_in = moves.start(wo, ow.at[0])
    ffn_in = [moves.start(w, v.at[0]) for w, v in ((wl, lw), (wr, rw), (wd, dw))]
    cot_in = moves.start(cot_hbm, cot.at[pl.ds(mine, own), :])
    place.greet()

    def norm(first, source, gain_row):
        values = source[pl.ds(first, 32), :].astype(F32)
        scale = lax.rsqrt(jnp.mean(values * values, axis=-1, keepdims=True) + EPS)
        return values, scale, values * scale * gain_row

    moves.wait(x_in)

    def first_norm(first):
        normed[pl.ds(mine + first, 32), :] = norm(first, x_ref, g1_ref[...])[2].astype(BF)

    rows_loop(own, 32, first_norm)
    block = normed.at[pl.ds(mine, own), :]
    normed_copy = links.start(block, block, place.mate)

    first_order, second_order = (0, 1, 2), (0, 2, 1)
    gather_joined = [
        Gather(place, links, joined, (pl.ds(0, 2),), 0, first_order),
        Gather(place, links, joined, (pl.ds(2, 2),), 0, second_order),
    ]
    gather_ow = Gather(place, links, ow, (), 0, second_order)
    gather_ffn = [
        Gather(place, links, lw, (), 0, first_order),
        Gather(place, links, rw, (), 0, second_order),
        Gather(place, links, dw, (), 1, first_order),
    ]
    for copy in joined_in:
        moves.wait(copy)
    for unit in gather_joined:
        unit.begin()
    moves.wait(ow_in)
    gather_ow.begin()
    attn_units = gather_joined + [gather_ow]

    def project(shard, first):
        rows = normed[pl.ds(first, own), :]
        at = pl.ds(first, own)
        soft, slope = softplus_and_slope(dot(rows, joined[shard, 0]))
        qp[shard, at, :] = soft.astype(BF)
        sq[shard, at, :] = slope.astype(BF)
        soft, slope = softplus_and_slope(dot(rows, joined[shard, 1]))
        kp[shard, at, :] = soft.astype(BF)
        sk[shard, at, :] = slope.astype(BF)
        vl[shard, at, :] = dot(rows, joined[shard, 2]).astype(BF)
        sz[shard, at, :] = sigmoid(dot(rows, joined[shard, 3]))

    project(0, mine)
    doc_mask(place, segr_ref, segc_ref, mask, tokens, False)
    for unit in attn_units:
        unit.advance()
    for copy in ffn_in:
        moves.wait(copy)
    normed_copy.wait_recv()
    for unit in gather_ffn:
        unit.begin()
    moves.wait(cot_in)
    cot_block = cot.at[pl.ds(mine, own), :]
    cot_copy = links.start(cot_block, cot_block, place.mate)

    project(0, theirs)
    near = near_marks(place, segc_ref, tokens)
    state_copy = [None, None]

    def send_state(shard):
        keys = jnp.where(near, kp[shard].astype(F32), 0.0).astype(BF)
        state_send[shard] = fold(dot(keys.T, vl[shard]))
        state_copy[shard] = links.start(state_send.at[shard], state_recv.at[1 - shard], place.twin)

    def mix(shard):
        def one(head, carry):
            for r in range(2):
                seen = (r + 1) * own
                at = slice(r * own, (r + 1) * own)
                query = only_head(qp[shard, at, :], head)
                raw = dot_t(query, kp[shard, :seen, :])
                scores = raw.astype(BF) * mask[at, :seen]
                hn[shard, at, :] += dot(scores, only_head(vl[shard, :seen, :], head))
            return carry

        hn[shard] = jnp.zeros(hn.shape[1:], F32)
        lax.fori_loop(0, hn.shape[-1] // HEAD, one, 0)

    send_state(0)
    for unit in attn_units:
        unit.advance()
    mix(0)
    for unit in attn_units:
        unit.advance()
    for unit in gather_ffn:
        unit.advance()
    for unit in attn_units:
        unit.complete()
    project(1, mine)
    project(1, theirs)
    send_state(1)
    for unit in gather_ffn:
        unit.advance()
    mix(1)
    for unit in gather_ffn:
        unit.advance()

    second_half = place.pair == 1

    def open_gate(shard):
        state_copy[1 - shard].wait_recv()
        marks = near & second_half
        query = jnp.where(marks, qp[shard].astype(F32), 0.0).astype(BF)
        mixed = hn[shard] + dot(query, unfold(state_recv[shard]))
        scale = lax.rsqrt(head_mean(mixed * mixed) + EPS)
        rr[shard] = scale
        hn[shard] = mixed * scale
        gated[shard] = (mixed * scale * sz[shard]).astype(BF)

    open_gate(0)
    open_gate(1)

    def branch(first):
        at = pl.ds(first, own)
        return dot(gated[0, at, :], ow[0]) + dot(gated[1, at, :], ow[1])

    branch_send[...] = branch(theirs).astype(BF)
    branch_copy = links.start(branch_send, branch_recv, place.mate)
    own_sum[...] = branch(mine)
    for shard in range(2):
        gated_t[shard] = gated[shard].T
    for unit in gather_ffn:
        unit.complete()
    outs = [
        (joined.at[1], joined_out), (ow.at[1], ow_out), (qp, qp_out), (kp, kp_out), (vl, vl_out), (sq, sq_out),
        (sk, sk_out), (hn, hn_out), (rr, rr_out), (sz, sz_out), (state_recv, state_out), (gated_t, gated_t_out),
    ]
    for source, target in outs:
        moves.start(source, target)
    branch_copy.wait_recv()

    def second_norm(first):
        at = pl.ds(first, 32)
        values = x_ref[at, :].astype(F32) + own_sum[at, :] + branch_recv[at, :].astype(F32)
        resid[at, :] = values
        scale = lax.rsqrt(jnp.mean(values * values, axis=-1, keepdims=True) + EPS)
        second[pl.ds(mine + first, 32), :] = (values * scale * g2_ref[...]).astype(BF)

    rows_loop(own, 32, second_norm)
    block = second.at[pl.ds(mine, own), :]
    second_copy = links.start(block, block, place.mate)
    cot_copy.wait_recv()
    moves.start(cot, cot_out)

    def unit_rows(first):
        at = pl.ds(first, own)

        def one(shard, carry):
            left = dot(second[at, :], lw[shard])
            right = dot(second[at, :], rw[shard])
            product[shard, at, :] = (left * right).astype(BF)
            grad = dot_t(cot[at, :], dw[shard])
            dleft[shard, at, :] = (grad * right).astype(BF)
            dright[shard, at, :] = (grad * left).astype(BF)
            return carry

        lax.fori_loop(0, 2, one, 0)

    unit_rows(mine)
    for c in range(0, width, 256):
        normed_t[c : c + 256, :] = normed[:, c : c + 256].T
    moves.start(normed_t, normed_t_out)
    second_copy.wait_recv()
    unit_rows(theirs)

    def back(first):
        at = pl.ds(first, own)
        return (
            dot_t(dleft[0, at, :], lw[0])
            + dot_t(dright[0, at, :], rw[0])
            + dot_t(dleft[1, at, :], lw[1])
            + dot_t(dright[1, at, :], rw[1])
        )

    def ffn(first):
        at = pl.ds(first, own)
        return dot(product[0, at, :], dw[0]) + dot(product[1, at, :], dw[1])

    back_send[...] = back(theirs).astype(BF)
    back_copy = links.start(back_send, back_recv, place.mate)
    moves.start(dleft, dleft_out)
    moves.start(dright, dright_out)
    ffn_send[...] = ffn(theirs).astype(BF)
    ffn_copy = links.start(ffn_send, ffn_recv, place.mate)
    own_sum[...] = back(mine)
    ffn_own[...] = ffn(mine)
    for c in range(0, width, 256):
        second_t[c : c + 256, :] = second[:, c : c + 256].T
    moves.start(second_t, second_t_out)
    for shard in range(2):
        product_t[shard] = product[shard].T
    moves.start(product_t, product_t_out)
    gain[...] = jnp.zeros(gain.shape, F32)
    back_copy.wait_recv()

    def residual_back(first):
        at = pl.ds(first, 32)
        values = resid[at, :]
        scale = lax.rsqrt(jnp.mean(values * values, axis=-1, keepdims=True) + EPS)
        grad = own_sum[at, :] + back_recv[at, :].astype(F32)
        gain[0:1, :] += jnp.sum(grad * values * scale, axis=0, keepdims=True)
        weighted = grad * g2_ref[...]
        inner = jnp.mean(weighted * values, axis=-1, keepdims=True)
        upstream = cot[pl.ds(mine + first, 32), :].astype(F32)
        dres[at, :] = upstream + scale * weighted - values * (scale * scale * scale * inner)

    rows_loop(own, 32, residual_back)
    moves.start(dres, dres_out)
    moves.start(gain, gain_out)
    ffn_copy.wait_recv()

    def finish_block(first):
        at = pl.ds(first, 32)
        blk[at, :] = (resid[at, :] + ffn_own[at, :] + ffn_recv[at, :].astype(F32)).astype(BF)

    rows_loop(own, 32, finish_block)
    moves.start(blk, block_out)
    moves.finish()
    links.finish()


class Reduce:
    def __init__(self, place, links, moves, grad, axis, order, halves, extra, twin_recv, done, out):
        self.place, self.links, self.moves = place, links, moves
        self.grad, self.axis, self.order = grad, axis, order
        self.halves, self.extra, self.twin_recv, self.done, self.out = halves, extra, twin_recv, done, out
        self.size = grad.shape[1 + axis] // (1 << len(order))
        self.piece = piece_of(place, order)
        self.stage, self.copy, self.local = 0, None, None
        self.steps = len(order) + len(extra) + 1 + len(order)

    def first_of(self, width):
        return pl.multiple_of((self.piece // width) * (width * self.size), self.size)

    def grad_part(self, lead, first, width):
        return part(self.grad, lead, self.axis, pl.multiple_of(first, self.size), width * self.size)

    def out_part(self, width):
        return part(self.out, (), self.axis, self.first_of(width), width * self.size)

    def begin(self):
        shards, folds = (slice(None),), len(self.order)
        k = self.stage
        if k < folds:
            width = 1 << (folds - 1 - k)
            bit = self.place.bit(self.order[k])
            away = self.first_of(width) + (1 - 2 * bit) * (width * self.size)
            self.copy = self.links.start(
                self.grad_part(shards, away, width), self.halves[k], self.place.over(self.order[k])
            )
            return
        k -= folds
        if k < len(self.extra):
            source = self.grad_part(shards, self.first_of(1), 1)
            self.copy = self.links.start(source, self.extra[k], self.place.over(folds + k))
            return
        k -= len(self.extra)
        if k == 0:
            source = self.grad_part((1,), self.first_of(1), 1)
            self.copy = self.links.start(source, self.twin_recv, self.place.twin)
            return
        k -= 1
        block = self.out_part(1 << k)
        source = self.done if k == 0 else block
        self.copy = self.links.start(source, block, self.place.over(self.order[folds - 1 - k]))
        if k == 0:
            self.local = self.moves.start(self.done, block)

    def add(self, recv, width, target=None):
        rows = recv.shape[-2]
        chunk = 32
        first = self.first_of(width)
        shards = 1 if target is not None else 2

        def body(at):
            for shard in range(shards):
                lead = (shard,)
                if self.axis == 0:
                    where = lead + (pl.ds(pl.multiple_of(first + at, chunk), chunk), slice(None))
                else:
                    where = lead + (pl.ds(at, chunk), pl.ds(first, width * self.size))
                if target is None:
                    self.grad[where] = self.grad[where] + recv[shard, pl.ds(at, chunk), :]
                else:
                    target[pl.ds(at, chunk), :] = self.grad[where] + recv[pl.ds(at, chunk), :]

        rows_loop(rows, chunk, body)

    def advance(self):
        if self.stage >= self.steps:
            return
        folds = len(self.order)
        self.copy.wait_recv()
        k = self.stage
        if k < folds:
            self.add(self.halves[k], 1 << (folds - 1 - k))
        elif k < folds + len(self.extra):
            self.copy.wait_send()
            self.links.open = [other for other in self.links.open if other is not self.copy]
            self.add(self.extra[k - folds], 1)
        elif k == folds + len(self.extra):
            self.add(self.twin_recv, 1, self.done)
        elif self.local is not None:
            self.moves.wait(self.local)
            self.local = None
        self.stage += 1
        if self.stage < self.steps:
            self.begin()

    def over(self):
        return self.stage >= self.steps


def backward_kernel(
    dp_size, extras, unit_shapes,
    normed_t_in, second_t_in, gated_t_in, product_t_in, dleft_in, dright_in, cot_in,
    qp_in, kp_in, vl_in, sq_in, sk_in, hn_in, rr_in, sz_in, state_in,
    wq, wk, wv, wz, joined_in, wo, ow_in, dres_in, gain_in, x_hbm, segr_ref, segc_ref, g1_ref,
    *rest,
):
    count = len(unit_shapes)
    outs, rest = rest[:count], rest[count:]
    block_out, gains_out = rest[:2]
    rest = rest[2:]
    grads, rest = rest[:count], rest[count:]
    received, rest = rest[: count * (PIECE_BITS + extras + 2)], rest[count * (PIECE_BITS + extras + 2) :]
    (
        second_t, gated_t, product_t, dleft, dright, cot, qp, kp, vl, sq, sk, hn, rr, sz, state,
        joined, ow, dres, gains, gains_recv, x_ref, dres_all, dm, djoined, mask, mask_t,
        dq, dk, dv, meet_send, meet_recv, back_send, back_recv, own_sum, blk,
        send_sem, recv_sem, move_sem,
    ) = rest
    place = Place(dp_size)
    links, moves = Links(send_sem, recv_sem), Moves(move_sem)
    own, width = x_ref.shape
    tokens = 2 * own
    mine = pl.multiple_of(place.half * own, own)
    theirs = pl.multiple_of((1 - place.half) * own, own)

    loads = {}
    for name, source, target in (
        ("dres", dres_in, dres), ("product", product_t_in, product_t), ("cot", cot_in, cot),
        ("second", second_t_in, second_t), ("left", dleft_in, dleft), ("right", dright_in, dright),
        ("ow0", wo, ow.at[0]), ("ow1", ow_in, ow.at[1]), ("sz", sz_in, sz), ("hn", hn_in, hn), ("rr", rr_in, rr),
        ("gated", gated_t_in, gated_t), ("qp", qp_in, qp), ("kp", kp_in, kp),
        ("vl", vl_in, vl), ("sq", sq_in, sq), ("sk", sk_in, sk), ("state", state_in, state),
        ("j0", wq, joined.at[0, 0]), ("j1", wk, joined.at[0, 1]), ("j2", wv, joined.at[0, 2]),
        ("j3", wz, joined.at[0, 3]), ("joined", joined_in, joined.at[1]), ("x", x_hbm, x_ref),
        ("gain", gain_in, gains.at[0]),
    ):
        loads[name] = moves.start(source, target)

    def ready(*names):
        for name in names:
            moves.wait(loads[name])

    place.greet()
    ready("dres")

    def round_dres(first):
        dres_all[pl.ds(mine + first, 32), :] = dres[pl.ds(first, 32), :].astype(BF)

    rows_loop(own, 32, round_dres)
    block = dres_all.at[pl.ds(mine, own), :]
    dres_copy = links.start(block, block, place.mate)

    per_unit = PIECE_BITS + extras + 2
    units = []
    for n, (_, axis, order) in enumerate(unit_shapes):
        bufs = received[n * per_unit : (n + 1) * per_unit]
        units.append(
            Reduce(
                place, links, moves, grads[n], axis, order, bufs[:PIECE_BITS],
                bufs[PIECE_BITS : PIECE_BITS + extras], bufs[-2], bufs[-1], outs[n],
            )
        )
    down_unit, left_unit, right_unit, ow_unit, q_unit, k_unit, v_unit, z_unit = units
    live = []

    def launch(unit):
        unit.begin()
        live.append(unit)

    def step_all():
        for unit in live:
            unit.advance()

    def outer(unit, left_of, right_of, chunk):
        rows = unit.grad.shape[1]

        def body(first):
            def one(shard, carry):
                unit.grad[shard, pl.ds(first, chunk), :] = dot(left_of(shard, first), right_of(shard)).astype(BF)
                return carry

            lax.fori_loop(0, 2, one, 0)

        rows_loop(rows, chunk, body)
        launch(unit)

    ready("product", "cot")
    down_chunk = product_t.shape[1] // 2
    outer(down_unit, lambda g, f: product_t[g, pl.ds(f, down_chunk), :], lambda g: cot[...], down_chunk)
    ready("second", "left")
    outer(left_unit, lambda g, f: second_t[pl.ds(f, 256), :], lambda g: dleft[g], 256)
    ready("right")
    outer(right_unit, lambda g, f: second_t[pl.ds(f, 256), :], lambda g: dright[g], 256)
    normed_t = second_t
    loads["normed"] = moves.start(normed_t_in, normed_t)
    doc_mask(place, segr_ref, segc_ref, mask, tokens, False)
    doc_mask(place, segr_ref, segc_ref, mask_t, tokens, True)
    near = near_marks(place, segc_ref, tokens)
    ready("ow0", "ow1", "sz", "hn", "rr", "qp")
    dres_copy.wait_recv()

    def gate_back(shard, carry):
        grad = dot_t(dres_all[...], ow[shard])
        opened, norm = sz[shard], hn[shard]
        djoined[shard, 3] = (grad * norm * opened * (1.0 - opened)).astype(BF)
        inner = grad * opened
        dm[shard] = (rr[shard] * (inner - norm * head_mean(inner * norm))).astype(BF)
        return carry

    lax.fori_loop(0, 2, gate_back, 0)
    meets = []
    for shard in range(2):
        query = jnp.where(near, qp[shard].astype(F32), 0.0).astype(BF)
        meet_send[shard] = fold(dot(query.T, dm[shard]))
        meets.append(links.start(meet_send.at[shard], meet_recv.at[1 - shard], place.twin))
    ready("gated", "normed")
    outer(ow_unit, lambda g, f: gated_t[g, pl.ds(f, 256), :], lambda g: dres_all[...], 256)

    def project_back(unit, j):
        outer(unit, lambda g, f: normed_t[pl.ds(f, 256), :], lambda g: djoined[g, j], 256)

    project_back(z_unit, 3)
    step_all()
    ready("kp", "vl", "sq", "sk", "state")
    first_half, second_half = place.pair == 0, place.pair == 1

    def mix_back(shard):
        dq[...] = jnp.where(near & second_half, dot_t(dm[shard], unfold(state[shard])), 0.0)
        dk[...] = jnp.zeros(dk.shape, F32)
        dv[...] = jnp.zeros(dv.shape, F32)

        def one(head, carry):
            for r in range(2):
                seen = (r + 1) * own
                at = slice(r * own, (r + 1) * own)
                grad_r, query_r = dm[shard, at, :], qp[shard, at, :]
                grad_h, query_h = only_head(grad_r, head), only_head(query_r, head)
                keys_h = only_head(kp[shard, :seen, :], head)
                vals_h = only_head(vl[shard, :seen, :], head)
                ds = dot_t(grad_r, vals_h).astype(BF) * mask[at, :seen]
                dq[at, :] += dot(ds, keys_h)
                st = dot_t(keys_h, query_r).astype(BF) * mask_t[:seen, at]
                dv[:seen, :] += dot(st, grad_h)
                dst = dot_t(vals_h, grad_r).astype(BF) * mask_t[:seen, at]
                dk[:seen, :] += dot(dst, query_h)
            return carry

        lax.fori_loop(0, dq.shape[-1] // HEAD, one, 0)

    for shard in range(2):
        mix_back(shard)
        if shard == 0:
            step_all()
        meets[1 - shard].wait_recv()
        meet = unfold(meet_recv[shard])
        marks = near & first_half
        djoined[shard, 2] = (dv[...] + jnp.where(marks, dot(kp[shard], meet), 0.0)).astype(BF)
        from_meet = jnp.where(marks, dot_t(vl[shard], meet), 0.0)
        djoined[shard, 1] = ((dk[...] + from_meet) * sk[shard].astype(F32)).astype(BF)
        djoined[shard, 0] = (dq[...] * sq[shard].astype(F32)).astype(BF)

    step_all()
    ready("j0", "j1", "j2", "j3", "joined")

    def normed_back(first):
        at = pl.ds(first, own)
        own_sum[...] = jnp.zeros(own_sum.shape, F32)

        def one(k, carry):
            own_sum[...] += dot_t(djoined[k // 4, lax.rem(k, 4), at, :], joined[k // 4, lax.rem(k, 4)])
            return carry

        lax.fori_loop(0, 8, one, 0)

    project_back(q_unit, 0)
    project_back(k_unit, 1)
    project_back(v_unit, 2)
    step_all()
    normed_back(theirs)
    back_send[...] = own_sum[...].astype(BF)
    back_copy = links.start(back_send, back_recv, place.mate)
    step_all()
    normed_back(mine)
    ready("x", "gain")
    step_all()
    back_copy.wait_recv()

    def finish_block(first):
        at = pl.ds(first, 32)
        values = x_ref[at, :].astype(F32)
        scale = lax.rsqrt(jnp.mean(values * values, axis=-1, keepdims=True) + EPS)
        grad = own_sum[at, :] + back_recv[at, :].astype(F32)
        gains[0, 1:2, :] += jnp.sum(grad * values * scale, axis=0, keepdims=True)
        weighted = grad * g1_ref[...]
        inner = jnp.mean(weighted * values, axis=-1, keepdims=True)
        blk[at, :] = (dres[at, :] + scale * weighted - values * (scale * scale * scale * inner)).astype(BF)

    rows_loop(own, 32, finish_block)
    moves.start(blk, block_out)

    peers = [place.over(b) for b in range(place.bits)] + [place.mate, place.twin]
    for n, peer in enumerate(peers):
        copy = links.start(gains.at[n], gains_recv.at[n], peer)
        step_all()
        copy.wait_recv()
        gains[n + 1] = gains[n] + gains_recv[n]
    moves.start(gains.at[len(peers)], gains_out)
    while not all(unit.over() for unit in live):
        step_all()
    moves.finish()
    links.finish()


def vmem(shape, dtype=BF):
    return pltpu.VMEM(shape, dtype)


def per_device(
    dp_size,
    inputs, segments, query_weight, key_weight, value_weight, gate_weight, out_weight, left_weight, right_weight,
    down_weight, norm_first, norm_second, cotangent,
):
    own, width = inputs.shape
    tokens = 2 * own
    local = query_weight.shape[1]
    hidden = left_weight.shape[1]
    bits = dp_size.bit_length() - 1
    extras = bits - PIECE_BITS
    shape = jax.ShapeDtypeStruct
    heads = (2, tokens, local)
    segr, segc = segments, segments.reshape(-1, 1)
    gain_one, gain_two = norm_first.reshape(1, -1), norm_second.reshape(1, -1)
    saved = [
        shape((width, tokens), BF), shape((width, tokens), BF), shape((2, local, tokens), BF),
        shape((2, hidden, tokens), BF), shape((2, tokens, hidden), BF), shape((2, tokens, hidden), BF),
        shape((tokens, width), BF), shape(heads, BF), shape(heads, BF), shape(heads, BF), shape(heads, BF),
        shape(heads, BF), shape(heads, F32), shape(heads, F32), shape(heads, F32), shape((2, local, local // 2), BF),
    ]
    results = pl.pallas_call(
        functools.partial(forward_kernel, dp_size),
        out_shape=saved
        + [
            shape((4, width, local), BF), shape((local, width), BF), shape((own, width), F32),
            shape((own, width), BF), shape((8, width), F32),
        ],
        in_specs=[ANY, INNER, INNER] + [ANY] * 8 + [INNER, INNER, ANY],
        out_specs=[ANY] * 21,
        scratch_shapes=[
            vmem((own, width)), vmem((tokens, width)), vmem((width, tokens)), vmem((2, 4, width, local)),
            vmem((2, local, width)), vmem((2, width, hidden)), vmem((2, width, hidden)), vmem((2, hidden, width)),
            vmem(heads), vmem(heads), vmem(heads), vmem(heads), vmem(heads), vmem(heads, F32), vmem(heads, F32),
            vmem(heads, F32), vmem(heads), vmem((2, local, tokens)), vmem((tokens, tokens)),
            vmem((2, local, local // 2)), vmem((2, local, local // 2)), vmem((own, width)), vmem((own, width)),
            vmem((own, width), F32), vmem((own, width), F32), vmem((tokens, width)), vmem((width, tokens)),
            vmem((tokens, width)), vmem((2, tokens, hidden)), vmem((2, hidden, tokens)), vmem((2, tokens, hidden)),
            vmem((2, tokens, hidden)), vmem((own, width)), vmem((own, width)), vmem((own, width), F32),
            vmem((own, width)), vmem((own, width)), vmem((own, width), F32), vmem((own, width)),
            vmem((8, width), F32),
            pltpu.SemaphoreType.DMA((40,)), pltpu.SemaphoreType.DMA((40,)), pltpu.SemaphoreType.DMA((40,)),
        ],
        compiler_params=pltpu.CompilerParams(collective_id=0, has_side_effects=True, vmem_limit_bytes=60 << 20),
    )(
        inputs, segr, segc, query_weight, key_weight, value_weight, gate_weight, out_weight, left_weight,
        right_weight, down_weight, gain_one, gain_two, cotangent,
    )
    kept, (joined, ow, dres, block, gain) = results[:16], results[16:]

    first_order, second_order = (0, 1, 2), (0, 2, 1)
    unit_shapes = (
        ((2, hidden, width), 1, first_order),
        ((2, width, hidden), 0, second_order),
        ((2, width, hidden), 0, first_order),
        ((2, local, width), 0, second_order),
        ((2, width, local), 0, first_order),
        ((2, width, local), 0, second_order),
        ((2, width, local), 0, second_order),
        ((2, width, local), 0, second_order),
    )
    received = []
    for full, axis, _ in unit_shapes:
        def cut(parts, full=full, axis=axis):
            return tuple(n // parts if d == 1 + axis else n for d, n in enumerate(full))

        received += [vmem(cut(2 << k)) for k in range(PIECE_BITS)]
        received += [vmem(cut(1 << PIECE_BITS))] * extras
        received += [vmem(cut(1 << PIECE_BITS)[1:])] * 2
    stages = len(unit_shapes) * (2 * PIECE_BITS + extras + 1) + bits + 2 + 8
    results = pl.pallas_call(
        functools.partial(backward_kernel, dp_size, extras, unit_shapes),
        out_shape=[shape(full[1:], BF) for full, _, _ in unit_shapes]
        + [shape((own, width), BF), shape((8, width), F32)],
        in_specs=[ANY] * 26 + [INNER] * 3,
        out_specs=[ANY] * (len(unit_shapes) + 2),
        scratch_shapes=[vmem(full) for full, _, _ in unit_shapes]
        + received
        + [
            vmem((width, tokens)), vmem((2, local, tokens)), vmem((2, hidden, tokens)),
            vmem((2, tokens, hidden)), vmem((2, tokens, hidden)), vmem((tokens, width)), vmem(heads), vmem(heads),
            vmem(heads), vmem(heads), vmem(heads), vmem(heads, F32), vmem(heads, F32), vmem(heads, F32),
            vmem((2, local, local // 2)), vmem((2, 4, width, local)), vmem((2, local, width)), vmem((own, width), F32),
            vmem((bits + 3, 8, width), F32), vmem((bits + 2, 8, width), F32), vmem((own, width)),
            vmem((tokens, width)), vmem(heads), vmem((2, 4, tokens, local)), vmem((tokens, tokens)),
            vmem((tokens, tokens)), vmem((tokens, local), F32), vmem((tokens, local), F32),
            vmem((tokens, local), F32), vmem((2, local, local // 2)), vmem((2, local, local // 2)),
            vmem((own, width)), vmem((own, width)), vmem((own, width), F32), vmem((own, width)),
            pltpu.SemaphoreType.DMA((stages,)), pltpu.SemaphoreType.DMA((stages,)), pltpu.SemaphoreType.DMA((48,)),
        ],
        compiler_params=pltpu.CompilerParams(collective_id=1, has_side_effects=True, vmem_limit_bytes=63 << 20),
    )(
        *kept, query_weight, key_weight, value_weight, gate_weight, joined, out_weight, ow, dres, gain, inputs,
        segr, segc, gain_one,
    )
    down, left, right, out, query, key, value, gate, block_grad, gains = results
    wide = [a.astype(F32) for a in (query, key, value, gate, out, left, right, down)]
    return (block, block_grad, *wide, gains[1], gains[0])


def solution(mesh):
    row, column = P("tensor", None), P(None, "tensor")
    tokens = P(("dp", "tensor"), None)
    return jax.shard_map(
        functools.partial(per_device, mesh.shape["dp"]),
        mesh=mesh,
        in_specs=(
            tokens, P("dp", None), column, column, column, column, row, column, column, row, P(), P(), tokens,
        ),
        out_specs=(tokens, tokens, column, column, column, column, row, column, column, row, P(), P()),
        check_vma=False,
    )
```

```python
import functools
import itertools

import jax
import jax.numpy as jnp
from jax import lax
from jax.experimental import pallas as pl
from jax.experimental.pallas import tpu as pltpu
from jax.sharding import PartitionSpec as P

EPS = 1e-05
HEAD = 64
BF = jnp.bfloat16
F32 = jnp.float32
MESH = pl.DeviceIdType.MESH
ANY = pl.BlockSpec(memory_space=pl.ANY)
INNER = pl.BlockSpec(memory_space=pltpu.VMEM)
PIECE_BITS = 3


def dot(a, b):
    return lax.dot_general(a, b, (((1,), (0,)), ((), ())), preferred_element_type=F32)


def dot_t(a, b):
    return lax.dot_general(a, b, (((1,), (1,)), ((), ())), preferred_element_type=F32)


class Place:
    def __init__(self, dp_size):
        self.i = lax.axis_index("dp")
        self.t = lax.axis_index("tensor")
        self.half = lax.rem(self.t, 2)
        self.pair = self.t // 2
        self.bits = dp_size.bit_length() - 1
        self.mate = {"tensor": self.t + 1 - 2 * self.half}
        self.twin = {"tensor": self.t + 2 - 4 * self.pair}

    def bit(self, b):
        return lax.rem(self.i // (1 << b), 2)

    def over(self, b):
        return {"dp": self.i + (1 << b) * (1 - 2 * self.bit(b))}

    def greet(self):
        barrier = pltpu.get_barrier_semaphore()
        peers = [self.mate, self.twin] + [self.over(b) for b in range(self.bits)]
        for peer in peers:
            pl.semaphore_signal(barrier, inc=1, device_id=peer, device_id_type=MESH)

        def all_here():
            pl.semaphore_wait(barrier, len(peers))

        return all_here


class Links:
    def __init__(self, send_sem, recv_sem):
        self.send_sem, self.recv_sem, self.count, self.open = send_sem, recv_sem, 0, []

    def start(self, source, target, peer):
        copy = pltpu.make_async_remote_copy(
            src_ref=source,
            dst_ref=target,
            send_sem=self.send_sem.at[self.count],
            recv_sem=self.recv_sem.at[self.count],
            device_id=peer,
            device_id_type=MESH,
        )
        self.count += 1
        copy.start()
        self.open.append(copy)
        return copy

    def settle(self, *copies):
        for copy in copies:
            copy.wait_send()
        self.open = [other for other in self.open if all(other is not copy for copy in copies)]

    def finish(self):
        self.settle(*self.open)


class Moves:
    def __init__(self, sem):
        self.sem, self.count, self.open = sem, 0, []

    def start(self, source, target):
        copy = pltpu.make_async_copy(source, target, self.sem.at[self.count])
        self.count += 1
        copy.start()
        self.open.append(copy)
        return copy

    def wait(self, copy):
        copy.wait()
        self.open = [other for other in self.open if other is not copy]

    def finish(self):
        for copy in list(self.open):
            self.wait(copy)


def part(ref, lead, axis, first, count):
    window = pl.ds(first, count)
    return ref.at[lead + ((window, slice(None)) if axis == 0 else (slice(None), window))]


def piece_of(place, order):
    total = 0
    for b in order:
        total = 2 * total + place.bit(b)
    return total


class Gather:
    def __init__(self, place, links, ref, lead, axis, order):
        self.place, self.links, self.ref, self.lead, self.axis, self.order = place, links, ref, lead, axis, order
        self.size = ref.shape[len(ref.shape) - 2 + axis] // (1 << len(order))
        self.piece = piece_of(place, order)
        self.copy, self.stage, self.sent = None, 0, []

    def block(self, shard, width):
        first = (self.piece // width) * (width * self.size)
        return part(self.ref, (shard,) + self.lead, self.axis, pl.multiple_of(first, self.size), width * self.size)

    def begin(self):
        self.copy = self.links.start(self.block(0, 1), self.block(1, 1), self.place.twin)
        self.sent.append(self.copy)

    def advance(self):
        self.copy.wait_recv()
        if self.stage < len(self.order):
            block = self.block(1, 1 << self.stage)
            self.copy = self.links.start(block, block, self.place.over(self.order[-1 - self.stage]))
            self.sent.append(self.copy)
        self.stage += 1


def rows_loop(count, size, body):
    def step(k, carry):
        body(pl.multiple_of(k * size, size))
        return carry

    lax.fori_loop(0, count // size, step, 0)


def softplus_and_slope(values):
    tail = jnp.exp(-jnp.abs(values))
    soft = jnp.maximum(values, 0.0) + jnp.log1p(tail)
    slope = jnp.where(values >= 0, 1.0, tail) / (1.0 + tail)
    return soft, slope


def sigmoid(values):
    tail = jnp.exp(-jnp.abs(values))
    return jnp.where(values >= 0, 1.0, tail) / (1.0 + tail)


def head_of(shape, axis):
    return lax.broadcasted_iota(jnp.int32, shape, axis) // HEAD


def same_head(width):
    return head_of((width, width), 0) == head_of((width, width), 1)


def head_mean(values):
    ones = jnp.where(same_head(values.shape[-1]), 1.0 / HEAD, 0.0).astype(BF)
    return dot(values.astype(BF), ones)


def fold(state):
    width = state.shape[-1]
    state = jnp.where(same_head(width), state, 0.0)
    return (state[:, : width // 2] + state[:, width // 2 :]).astype(BF)


def unfold(state):
    both = jnp.concatenate((state, state), axis=1)
    return jnp.where(same_head(both.shape[-1]), both, jnp.zeros_like(both))


def only_head(values, head):
    return jnp.where(head_of(values.shape, 1) == head, values, jnp.zeros_like(values))


class Reduce:
    def __init__(self, place, links, moves, grad, axis, order, halves, credits, twin_recv, out):
        self.place, self.links, self.moves = place, links, moves
        self.grad, self.axis, self.order = grad, axis, order
        self.halves, self.twin_recv, self.out = halves, twin_recv, out
        self.extra = credits
        self.size = grad.shape[1 + axis] // (1 << len(order))
        self.piece = piece_of(place, order)
        self.stage, self.copy, self.local = 0, None, None
        self.steps = len(order) + len(self.extra) + 1 + len(order)

    def first_of(self, width):
        return pl.multiple_of((self.piece // width) * (width * self.size), self.size)

    def grad_part(self, lead, first, width):
        return part(self.grad, lead, self.axis, pl.multiple_of(first, self.size), width * self.size)

    def out_part(self, width):
        return part(self.out, (), self.axis, self.first_of(width), width * self.size)

    def begin(self):
        shards, folds = (slice(None),), len(self.order)
        k = self.stage
        if k < folds:
            width = 1 << (folds - 1 - k)
            bit = self.place.bit(self.order[k])
            away = self.first_of(width) + (1 - 2 * bit) * (width * self.size)
            self.copy = self.links.start(
                self.grad_part(shards, away, width), self.halves[k], self.place.over(self.order[k])
            )
            return
        k -= folds
        if k < len(self.extra):
            peer = self.place.over(folds + k)
            pl.semaphore_signal(self.extra[k], inc=1, device_id=peer, device_id_type=MESH)
            pl.semaphore_wait(self.extra[k], 1)
            source = self.grad_part(shards, self.first_of(1), 1)
            self.copy = self.links.start(source, self.halves[-1], peer)
            return
        k -= len(self.extra)
        if k == 0:
            source = self.grad_part((1,), self.first_of(1), 1)
            self.copy = self.links.start(source, self.twin_recv, self.place.twin)
            return
        k -= 1
        block = self.out_part(1 << k)
        source = self.grad_part((0,), self.first_of(1), 1) if k == 0 else block
        self.copy = self.links.start(source, block, self.place.over(self.order[folds - 1 - k]))
        if k == 0:
            self.local = self.moves.start(source, block)

    def add(self, recv, width):
        rows, chunk = recv.shape[-2], 32
        first = self.first_of(width)

        def body(at):
            for shard in range(recv.shape[0] if len(recv.shape) == 3 else 1):
                if self.axis == 0:
                    where = (shard, pl.ds(pl.multiple_of(first + at, chunk), chunk), slice(None))
                else:
                    where = (shard, pl.ds(at, chunk), pl.ds(first, width * self.size))
                came = recv[(shard,) * (len(recv.shape) - 2) + (pl.ds(at, chunk), slice(None))]
                self.grad[where] = self.grad[where] + came

        rows_loop(rows, chunk, body)

    def advance(self):
        if self.stage >= self.steps:
            return
        folds = len(self.order)
        self.copy.wait_recv()
        k = self.stage
        if k < folds:
            self.add(self.halves[k], 1 << (folds - 1 - k))
        elif k < folds + len(self.extra):
            self.links.settle(self.copy)
            self.add(self.halves[-1], 1)
        elif k == folds + len(self.extra):
            self.add(self.twin_recv, 1)
        elif self.local is not None:
            self.moves.wait(self.local)
            self.local = None
        self.stage += 1
        if self.stage < self.steps:
            self.begin()

    def over(self):
        return self.stage >= self.steps


def marks_of(place, segr_ref, segc, tokens):
    offset = pl.multiple_of(place.pair * tokens, tokens)
    across = segr_ref[:, pl.ds(offset, tokens)].astype(F32)
    segc[...] = jnp.broadcast_to(across, (8, tokens)).T[:, :1]
    return across, segr_ref[:, tokens - 1 : tokens].astype(F32)


def doc_mask(across, segc, mask_ref, tokens, later):
    def body(first):
        at = first + lax.broadcasted_iota(jnp.int32, (64, tokens), 0)
        col = lax.broadcasted_iota(jnp.int32, (64, tokens), 1)
        order = col >= at if later else col <= at
        same = segc[pl.ds(first, 64), :] == across
        mask_ref[pl.ds(first, 64), :] = jnp.where(same & order, 1.0, 0.0).astype(BF)

    rows_loop(tokens, 64, body)


def layer_kernel(
    dp_size, extras, hidden, pad,
    x_hbm, segr_ref, wq, wk, wv, wz, wo, wl, wr, wd, g1_ref, g2_ref, cot_hbm,
    down_out, left_out, right_out, ow_out, query_out, key_out, value_out, gate_out, block_out, grad_out, gains_out,
    x_ref, segc, normed, normed_t, joined, ow, lrw, dw, qp, kp, vl, sq, sk, hn, rr, sz, gated, mask, mask_t,
    state_send, state_recv, meet_send, meet_recv, trade_send, trade_recv, back_send, back_recv,
    resid, own_sum, second, cot, hid, dres, dm, djoined, dq, dk, dv, gains, gains_recv,
    grad_d, grad_l, grad_r, grad_o,
    *rest,
):
    *received, send_sem, recv_sem, move_sem, free_sem, credit_sem = rest
    received, tickets = list(received), itertools.count()
    place = Place(dp_size)
    links, moves = Links(send_sem, recv_sem), Moves(move_sem)
    own, width = x_ref.shape
    tokens = 2 * own
    local = qp.shape[-1]
    mine = pl.multiple_of(place.half * own, own)
    theirs = pl.multiple_of((1 - place.half) * own, own)
    lw, rw = lrw.at[:, :hidden, :], lrw.at[:, hidden:, :]
    product, dleft, dright = (slice(n * pad, n * pad + hidden) for n in range(3))
    dres_all = normed

    all_here = place.greet()
    x_in = moves.start(x_hbm, x_ref)
    joined_in = [moves.start(w, joined.at[0, j]) for j, w in enumerate((wq, wk, wv, wz))]
    ow_in = moves.start(wo, ow.at[0])
    ffn_in = [moves.start(w, v.at[0]) for w, v in ((wl, lw), (wr, rw), (wd, dw))]
    cot_in = moves.start(cot_hbm, cot.at[pl.ds(mine, own), :])
    moves.wait(x_in)

    def first_norm(first):
        values = x_ref[pl.ds(first, 32), :].astype(F32)
        scale = lax.rsqrt(jnp.mean(values * values, axis=-1, keepdims=True) + EPS)
        normed[pl.ds(mine + first, 32), :] = (values * scale * g1_ref[...]).astype(BF)

    rows_loop(own, 32, first_norm)
    for copy in joined_in:
        moves.wait(copy)
    all_here()
    block = normed.at[pl.ds(mine, own), :]
    normed_copy = links.start(block, block, place.mate)
    first_order, second_order = (0, 1, 2), (0, 2, 1)
    join_a = Gather(place, links, joined, (pl.ds(0, 2),), 0, first_order)
    join_b = Gather(place, links, joined, (pl.ds(2, 2),), 0, second_order)
    gather_o = Gather(place, links, ow, (), 1, second_order)
    gather_l = Gather(place, links, lw, (), 1, first_order)
    gather_r = Gather(place, links, rw, (), 1, second_order)
    gather_d = Gather(place, links, dw, (), 1, first_order)
    join_a.begin()
    join_b.begin()
    moves.wait(ow_in)
    gather_o.begin()

    def advance(*units):
        for unit in units:
            unit.advance()

    def project(shard, first, which):
        rows = normed[pl.ds(first, own), :]
        at = pl.ds(first, own)
        for j in which:
            raw = dot(rows, joined[shard, j])
            if j == 2:
                vl[shard, at, :] = raw.astype(BF)
            elif j == 3:
                sz[shard, at, :] = sigmoid(raw).astype(BF)
            else:
                soft, slope = softplus_and_slope(raw)
                (qp, kp)[j][shard, at, :] = soft.astype(BF)
                (sq, sk)[j][shard, at, :] = slope.astype(BF)

    project(0, mine, (1, 2, 0, 3))
    for copy in ffn_in:
        moves.wait(copy)
    gather_l.begin()
    gather_r.begin()
    gather_d.begin()
    across, last = marks_of(place, segr_ref, segc, tokens)
    doc_mask(across, segc, mask, tokens, False)
    moves.wait(cot_in)
    normed_copy.wait_recv()
    cot_block = cot.at[pl.ds(mine, own), :]
    cot_copy = links.start(cot_block, cot_block, place.mate)
    project(0, theirs, (1, 2))
    near = segc[...] == last
    state_copy = [None, None]

    def send_state(shard):
        keys = jnp.where(near, kp[shard].astype(F32), 0.0).astype(BF)
        state_send[shard] = fold(dot(keys.T, vl[shard]))
        state_copy[shard] = links.start(state_send.at[shard], state_recv.at[1 - shard], place.twin)

    send_state(0)
    project(0, theirs, (0, 3))
    advance(join_a, join_b, gather_o)

    def mix(shard):
        def one(head, carry):
            for r in range(2):
                seen = (r + 1) * own
                at = slice(r * own, (r + 1) * own)
                raw = dot_t(only_head(qp[shard, at, :], head), kp[shard, :seen, :])
                scores = raw.astype(BF) * mask[at, :seen]
                dq[at, :] += dot(scores, only_head(vl[shard, :seen, :], head))
            return carry

        dq[...] = jnp.zeros(dq.shape, F32)
        lax.fori_loop(0, local // HEAD, one, 0)

    first_half, second_half = place.pair == 0, place.pair == 1

    def open_gate(shard):
        state_copy[1 - shard].wait_recv()
        query = jnp.where(near & second_half, qp[shard].astype(F32), 0.0).astype(BF)
        mixed = dq[...] + dot(query, unfold(state_recv[shard]))
        scale = lax.rsqrt(head_mean(mixed * mixed) + EPS)
        norm = mixed * scale
        rr[shard] = scale.astype(BF)
        hn[shard] = norm.astype(BF)
        gated[shard] = (norm * sz[shard].astype(F32)).astype(BF)

    mix(0)
    advance(join_a, join_b, gather_o, gather_l)
    advance(join_a, join_b, gather_o, gather_r, gather_l)
    advance(join_a, join_b, gather_o)
    for first in (mine, theirs):
        project(1, first, (1, 2))
    send_state(1)
    open_gate(0)
    advance(gather_d, gather_r, gather_l)
    for first in (mine, theirs):
        project(1, first, (0, 3))
    advance(gather_d, gather_r, gather_l)
    mix(1)
    advance(gather_d, gather_r)
    open_gate(1)

    def branch(first):
        at = pl.ds(first, own)
        return dot(gated[0, at, :], ow[0]) + dot(gated[1, at, :], ow[1])

    trade_send[...] = branch(theirs).astype(BF)
    branch_copy = links.start(trade_send, trade_recv, place.mate)
    own_sum[...] = branch(mine)
    advance(gather_d)
    for c in range(0, width, 256):
        normed_t[c : c + 256, :] = normed[:, c : c + 256].T
    doc_mask(across, segc, mask_t, tokens, True)
    branch_copy.wait_recv()

    def second_norm(first):
        at = pl.ds(first, 32)
        values = x_ref[at, :].astype(F32) + own_sum[at, :] + trade_recv[at, :].astype(F32)
        resid[at, :] = values
        scale = lax.rsqrt(jnp.mean(values * values, axis=-1, keepdims=True) + EPS)
        second[pl.ds(mine + first, 32), :] = (values * scale * g2_ref[...]).astype(BF)

    rows_loop(own, 32, second_norm)
    block = second.at[pl.ds(mine, own), :]
    second_copy = links.start(block, block, place.mate)
    cot_copy.wait_recv()

    def hidden_grad(first):
        at = pl.ds(first, own)

        def one(shard, carry):
            hid[shard, at, dleft] = dot_t(cot[at, :], dw[shard]).astype(BF)
            return carry

        lax.fori_loop(0, 2, one, 0)

    def unit_rows(first):
        at = pl.ds(first, own)

        def one(shard, carry):
            left = dot_t(second[at, :], lw[shard])
            right = dot_t(second[at, :], rw[shard])
            grad = hid[shard, at, dleft].astype(F32)
            hid[shard, at, product] = (left * right).astype(BF)
            hid[shard, at, dleft] = (grad * right).astype(BF)
            hid[shard, at, dright] = (grad * left).astype(BF)
            return carry

        lax.fori_loop(0, 2, one, 0)

    hidden_grad(mine)
    unit_rows(mine)
    hidden_grad(theirs)
    second_copy.wait_recv()
    unit_rows(theirs)

    def back(first):
        at = pl.ds(first, own)
        return (
            dot(hid[0, at, dleft], lw[0])
            + dot(hid[0, at, dright], rw[0])
            + dot(hid[1, at, dleft], lw[1])
            + dot(hid[1, at, dright], rw[1])
        )

    def ffn(first):
        at = pl.ds(first, own)
        return dot(hid[0, at, product], dw[0]) + dot(hid[1, at, product], dw[1])

    back_send[...] = back(theirs).astype(BF)
    back_copy = links.start(back_send, back_recv, place.mate)
    own_sum[...] = back(mine)

    def make_unit(grad, axis, order, out, first_half_ref=None):
        folds = len(order)
        halves = [received.pop(0) for _ in range(folds - (first_half_ref is not None))]
        if first_half_ref is not None:
            halves = [first_half_ref] + halves
        credits = [credit_sem.at[next(tickets)] for _ in range(extras)]
        return Reduce(place, links, moves, grad, axis, order, halves, credits, received.pop(0), out)

    def split_units(grad, out):
        rows = grad.shape[1] // 2
        return [
            make_unit(grad.at[:, n * rows : (n + 1) * rows, :], 1, order, out.at[n * rows : (n + 1) * rows, :])
            for n, order in enumerate((first_order, second_order))
        ]

    down_units, left_units, right_units = (
        split_units(g, o) for g, o in ((grad_d, down_out), (grad_l, left_out), (grad_r, right_out))
    )
    ow_units = split_units(grad_o, ow_out)
    joined_units = [
        make_unit(
            lrw.at[:, :width, j * local : (j + 1) * local], 0, order, out,
            hid.at[:, : width // 2, j * local : (j + 1) * local],
        )
        for j, (order, out) in enumerate(
            zip(
                (first_order, second_order, first_order, second_order),
                (query_out, key_out, value_out, gate_out),
            )
        )
    ]
    live = []

    def launch(*units):
        for unit in units:
            unit.begin()
            live.append(unit)

    def step_all():
        for unit in live:
            unit.advance()

    def hidden_outer(units, grad, left, right):
        def one(shard, carry):
            for c in range(0, hidden, 256):
                high = min(c + 256, hidden)
                grad[shard, c:high, :] = dot(hid[shard, :, left.start + c : left.start + high].T, right[...]).astype(BF)
            return carry

        lax.fori_loop(0, 2, one, 0)
        launch(*units)

    hidden_outer(down_units, grad_d, product, cot)
    hidden_outer(left_units, grad_l, dleft, second)
    advance(*down_units)
    back_copy.wait_recv()

    gains[0] = jnp.zeros(gains.shape[1:], F32)

    def residual_back(first):
        at = pl.ds(first, 32)
        values = resid[at, :]
        scale = lax.rsqrt(jnp.mean(values * values, axis=-1, keepdims=True) + EPS)
        grad = own_sum[at, :] + back_recv[at, :].astype(F32)
        gains[0, 0:1, :] += jnp.sum(grad * values * scale, axis=0, keepdims=True)
        weighted = grad * g2_ref[...]
        inner = jnp.mean(weighted * values, axis=-1, keepdims=True)
        upstream = cot[pl.ds(mine + first, 32), :].astype(F32)
        total = upstream + scale * weighted - values * (scale * scale * scale * inner)
        dres[at, :] = total
        dres_all[pl.ds(mine + first, 32), :] = total.astype(BF)

    links.settle(normed_copy)
    rows_loop(own, 32, residual_back)
    block = dres_all.at[pl.ds(mine, own), :]
    dres_copy = links.start(block, block, place.mate)
    hidden_outer(right_units, grad_r, dright, second)
    advance(*left_units)
    links.settle(back_copy)
    back_send[...] = ffn(theirs).astype(BF)

    def add_ffn(first):
        resid[...] += ffn(first)

    add_ffn(mine)
    advance(*right_units)
    pl.semaphore_signal(free_sem, inc=1, device_id=place.over(0), device_id_type=MESH)
    advance(*down_units)
    dres_copy.wait_recv()
    ffn_copy = links.start(back_send, back_recv, place.mate)

    def gate_back(shard, carry):
        grad = dot_t(dres_all[...], ow[shard])
        opened, norm = sz[shard].astype(F32), hn[shard].astype(F32)
        djoined[shard, 3] = (grad * norm * opened * (1.0 - opened)).astype(BF)
        inner = grad * opened
        dm[shard] = (rr[shard].astype(F32) * (inner - norm * head_mean(inner * norm))).astype(BF)
        return carry

    lax.fori_loop(0, 2, gate_back, 0)
    meets = []
    for shard in range(2):
        query = jnp.where(near, qp[shard].astype(F32), 0.0).astype(BF)
        meet_send[shard] = fold(dot(query.T, dm[shard]))
        meets.append(links.start(meet_send.at[shard], meet_recv.at[1 - shard], place.twin))

    def out_outer(shard, carry):
        grad_o[shard] = dot(gated[shard].T, dres_all[...]).astype(BF)
        return carry

    lax.fori_loop(0, 2, out_outer, 0)
    launch(*ow_units)
    gathers = (join_a, join_b, gather_o, gather_l, gather_r, gather_d)
    for unit in gathers:
        links.settle(*unit.sent)
    pl.semaphore_wait(free_sem, 1)

    def project_back(j):
        def body(first):
            def one(shard, carry):
                part_grad = dot(normed_t[pl.ds(first, 256), :], djoined[shard, j])
                lrw[shard, pl.ds(first, 256), j * local : (j + 1) * local] = part_grad.astype(BF)
                return carry

            lax.fori_loop(0, 2, one, 0)

        rows_loop(width, 256, body)
        launch(joined_units[j])

    project_back(3)
    step_all()

    def mix_back(shard):
        dq[...] = jnp.where(near & second_half, dot_t(dm[shard], unfold(state_recv[shard])), 0.0)
        dk[...] = jnp.zeros(dk.shape, F32)
        dv[...] = jnp.zeros(dv.shape, F32)

        def one(head, carry):
            for r in range(2):
                seen = (r + 1) * own
                at = slice(r * own, (r + 1) * own)
                grad_r, query_r = dm[shard, at, :], qp[shard, at, :]
                grad_h, query_h = only_head(grad_r, head), only_head(query_r, head)
                keys_h = only_head(kp[shard, :seen, :], head)
                vals_h = only_head(vl[shard, :seen, :], head)
                ds = dot_t(grad_r, vals_h).astype(BF) * mask[at, :seen]
                dq[at, :] += dot(ds, keys_h)
                st = dot_t(keys_h, query_r).astype(BF) * mask_t[:seen, at]
                dv[:seen, :] += dot(st, grad_h)
                dst = dot_t(vals_h, grad_r).astype(BF) * mask_t[:seen, at]
                dk[:seen, :] += dot(dst, query_h)
            return carry

        lax.fori_loop(0, local // HEAD, one, 0)

    for shard in range(2):
        mix_back(shard)
        if shard == 0:
            step_all()
        meets[1 - shard].wait_recv()
        meet = unfold(meet_recv[shard])
        marks = near & first_half
        djoined[shard, 2] = (dv[...] + jnp.where(marks, dot(kp[shard], meet), 0.0)).astype(BF)
        from_meet = jnp.where(marks, dot_t(vl[shard], meet), 0.0)
        djoined[shard, 1] = ((dk[...] + from_meet) * sk[shard].astype(F32)).astype(BF)
        djoined[shard, 0] = (dq[...] * sq[shard].astype(F32)).astype(BF)

    project_back(0)
    project_back(1)
    project_back(2)
    step_all()

    def normed_back(first):
        at = pl.ds(first, own)
        own_sum[...] = jnp.zeros(own_sum.shape, F32)

        def one(k, carry):
            own_sum[...] += dot_t(djoined[k // 4, lax.rem(k, 4), at, :], joined[k // 4, lax.rem(k, 4)])
            return carry

        lax.fori_loop(0, 8, one, 0)

    links.settle(branch_copy)
    normed_back(theirs)
    trade_send[...] = own_sum[...].astype(BF)
    trade_copy = links.start(trade_send, trade_recv, place.mate)
    step_all()
    normed_back(mine)
    ffn_copy.wait_recv()
    links.settle(ffn_copy)

    def finish_out(first):
        at = pl.ds(first, 32)
        back_send[at, :] = (resid[at, :] + back_recv[at, :].astype(F32)).astype(BF)

    rows_loop(own, 32, finish_out)
    moves.start(back_send, block_out)
    step_all()
    trade_copy.wait_recv()
    links.settle(trade_copy)

    def finish_grad(first):
        at = pl.ds(first, 32)
        values = x_ref[at, :].astype(F32)
        scale = lax.rsqrt(jnp.mean(values * values, axis=-1, keepdims=True) + EPS)
        grad = own_sum[at, :] + trade_recv[at, :].astype(F32)
        gains[0, 1:2, :] += jnp.sum(grad * values * scale, axis=0, keepdims=True)
        weighted = grad * g1_ref[...]
        inner = jnp.mean(weighted * values, axis=-1, keepdims=True)
        trade_send[at, :] = (dres[at, :] + scale * weighted - values * (scale * scale * scale * inner)).astype(BF)

    rows_loop(own, 32, finish_grad)
    moves.start(trade_send, grad_out)

    peers = [place.over(b) for b in range(place.bits)] + [place.mate, place.twin]
    for n, peer in enumerate(peers):
        copy = links.start(gains.at[n], gains_recv.at[n], peer)
        step_all()
        copy.wait_recv()
        gains[n + 1] = gains[n] + gains_recv[n]
    moves.start(gains.at[len(peers)], gains_out)
    while not all(unit.over() for unit in live):
        step_all()
    moves.finish()
    links.finish()


def widen_kernel(count, passed, *refs):
    sources, refs = refs[: count + passed], refs[count + passed :]
    targets, refs = refs[: count + passed], refs[count + passed :]
    narrow, wide, (in_sem, out_sem) = refs[:count], refs[count : 2 * count], refs[2 * count :]
    loads = [pltpu.make_async_copy(sources[n], narrow[n], in_sem.at[n]) for n in range(count)]
    stores = [pltpu.make_async_copy(wide[n], targets[n], out_sem.at[n]) for n in range(count)]
    stores += [
        pltpu.make_async_copy(sources[n], targets[n], out_sem.at[n]) for n in range(count, count + passed)
    ]
    for copy in loads + stores[count:]:
        copy.start()
    for n in range(count):
        loads[n].wait()

        def body(first, n=n):
            wide[n][pl.ds(first, 64), :] = narrow[n][pl.ds(first, 64), :].astype(F32)

        rows_loop(narrow[n].shape[0], 64, body)
        stores[n].start()
    for copy in stores:
        copy.wait()


def vmem(shape, dtype=BF):
    return pltpu.VMEM(shape, dtype)


def per_device(
    dp_size,
    inputs, segments, query_weight, key_weight, value_weight, gate_weight, out_weight, left_weight, right_weight,
    down_weight, norm_first, norm_second, cotangent,
):
    own, width = inputs.shape
    tokens = 2 * own
    local = query_weight.shape[1]
    hidden = left_weight.shape[1]
    pad = -(-hidden // 128) * 128
    bits = dp_size.bit_length() - 1
    extras = bits - PIECE_BITS
    shape = jax.ShapeDtypeStruct
    heads, state = (2, tokens, local), (2, local, local // 2)
    grads = [(hidden, width)] * 3 + [(local, width)] + [(width, local)] * 4

    def buffers(rows, columns, axis, first):
        def cut(parts):
            return (2, rows // parts, columns) if axis == 0 else (2, rows, columns // parts)

        eighth = cut(1 << PIECE_BITS)
        kept = [vmem(cut(2 << k)) for k in range(first, PIECE_BITS)]
        return kept + [vmem(eighth[1:])]

    received = []
    for rows in (hidden // 2,) * 6 + (local // 2,) * 2:
        received += buffers(rows, width, 1, 0)
    for _ in range(4):
        received += buffers(width, local, 0, 1)
    copies = 12 * (2 * PIECE_BITS + extras + 1) + 6 * (PIECE_BITS + 1) + bits + 16
    results = pl.pallas_call(
        functools.partial(layer_kernel, dp_size, extras, hidden, pad),
        out_shape=[shape(full, BF) for full in grads]
        + [shape((own, width), BF), shape((own, width), BF), shape((8, width), F32)],
        in_specs=[ANY, INNER] + [ANY] * 8 + [INNER, INNER, ANY],
        out_specs=[ANY] * 11,
        scratch_shapes=[
            vmem((own, width)), vmem((tokens, 1), F32), vmem((tokens, width)), vmem((width, tokens)),
            vmem((2, 4, width, local)), vmem((2, local, width)), vmem((2, 2 * hidden, width)),
            vmem((2, hidden, width)),
        ]
        + [vmem(heads)] * 9
        + [vmem((tokens, tokens))] * 2
        + [vmem(state)] * 4
        + [vmem((own, width))] * 4
        + [vmem((own, width), F32)] * 2
        + [
            vmem((tokens, width)), vmem((tokens, width)), vmem((2, tokens, 3 * pad)), vmem((own, width), F32),
            vmem(heads), vmem((2, 4, tokens, local)),
        ]
        + [vmem((tokens, local), F32)] * 3
        + [vmem((bits + 3, 8, width), F32), vmem((bits + 2, 8, width), F32)]
        + [vmem((2, hidden, width))] * 3
        + [vmem((2, local, width))]
        + received
        + [pltpu.SemaphoreType.DMA((copies,))] * 2
        + [
            pltpu.SemaphoreType.DMA((40,)), pltpu.SemaphoreType.REGULAR,
            pltpu.SemaphoreType.REGULAR((max(1, 12 * extras),)),
        ],
        compiler_params=pltpu.CompilerParams(collective_id=0, has_side_effects=True, vmem_limit_bytes=63 << 20),
    )(
        inputs, segments, query_weight, key_weight, value_weight, gate_weight, out_weight, left_weight.T,
        right_weight.T, down_weight, norm_first.reshape(1, -1), norm_second.reshape(1, -1), cotangent,
    )
    count, passed = len(grads), 3
    wide = pl.pallas_call(
        functools.partial(widen_kernel, count, passed),
        out_shape=[shape(full, F32) for full in grads] + [shape(r.shape, r.dtype) for r in results[count:]],
        in_specs=[ANY] * (count + passed),
        out_specs=[ANY] * (count + passed),
        scratch_shapes=[vmem(full) for full in grads]
        + [vmem(full, F32) for full in grads]
        + [pltpu.SemaphoreType.DMA((count,)), pltpu.SemaphoreType.DMA((count + passed,))],
        compiler_params=pltpu.CompilerParams(vmem_limit_bytes=48 << 20),
    )(*results)
    down, left, right, out, query, key, value, gate, block, block_grad, gains = wide
    return (
        block, block_grad, query, key, value, gate, out, left.T, right.T, down, gains[1], gains[0],
    )


def solution(mesh):
    row, column = P("tensor", None), P(None, "tensor")
    tokens = P(("dp", "tensor"), None)
    return jax.shard_map(
        functools.partial(per_device, mesh.shape["dp"]),
        mesh=mesh,
        in_specs=(
            tokens, P("dp", None), column, column, column, column, row, column, column, row, P(), P(), tokens,
        ),
        out_specs=(tokens, tokens, column, column, column, column, row, column, column, row, P(), P()),
        check_vma=False,
    )
```

```python
import functools
import itertools

import jax
import jax.numpy as jnp
from jax import lax
from jax.experimental import pallas as pl
from jax.experimental.pallas import tpu as pltpu
from jax.sharding import PartitionSpec as P

EPS = 1e-05
HEAD = 64
BF = jnp.bfloat16
F32 = jnp.float32
MESH = pl.DeviceIdType.MESH
ANY = pl.BlockSpec(memory_space=pl.ANY)
INNER = pl.BlockSpec(memory_space=pltpu.VMEM)
PIECE_BITS = 3


def dot(a, b):
    return lax.dot_general(a, b, (((1,), (0,)), ((), ())), preferred_element_type=F32)


def dot_t(a, b):
    return lax.dot_general(a, b, (((1,), (1,)), ((), ())), preferred_element_type=F32)


class Place:
    def __init__(self, dp_size):
        self.i = lax.axis_index("dp")
        self.t = lax.axis_index("tensor")
        self.half = lax.rem(self.t, 2)
        self.pair = self.t // 2
        self.bits = dp_size.bit_length() - 1
        self.rows = [{"dp": lax.rem(self.i + k, dp_size)} for k in range(1, dp_size)]
        self.columns = [{"tensor": lax.rem(self.t + k, 4)} for k in range(1, 4)]
        self.mate = {"tensor": self.t + 1 - 2 * self.half}
        self.twin = {"tensor": self.t + 2 - 4 * self.pair}

    def bit(self, b):
        return lax.rem(self.i // (1 << b), 2)

    def over(self, b):
        return {"dp": self.i + (1 << b) * (1 - 2 * self.bit(b))}

    def greet(self):
        barrier = pltpu.get_barrier_semaphore()
        peers = self.rows + self.columns
        for peer in peers:
            pl.semaphore_signal(barrier, inc=1, device_id=peer, device_id_type=MESH)

        def all_here():
            pl.semaphore_wait(barrier, len(peers))

        return all_here


class Links:
    def __init__(self, send_sem, recv_sem):
        self.send_sem, self.recv_sem, self.count, self.open = send_sem, recv_sem, 0, []

    def start(self, source, target, peer):
        copy = pltpu.make_async_remote_copy(
            src_ref=source,
            dst_ref=target,
            send_sem=self.send_sem.at[self.count],
            recv_sem=self.recv_sem.at[self.count],
            device_id=peer,
            device_id_type=MESH,
        )
        self.count += 1
        copy.start()
        self.open.append(copy)
        return copy

    def settle(self, *copies):
        for copy in copies:
            copy.wait_send()
        self.open = [other for other in self.open if all(other is not copy for copy in copies)]

    def finish(self):
        self.settle(*self.open)


class Moves:
    def __init__(self, sem):
        self.sem, self.count, self.open = sem, 0, []

    def start(self, source, target):
        copy = pltpu.make_async_copy(source, target, self.sem.at[self.count])
        self.count += 1
        copy.start()
        self.open.append(copy)
        return copy

    def wait(self, copy):
        copy.wait()
        self.open = [other for other in self.open if other is not copy]

    def finish(self):
        for copy in list(self.open):
            self.wait(copy)


def part(ref, lead, axis, first, count):
    window = pl.ds(first, count)
    return ref.at[lead + ((window, slice(None)) if axis == 0 else (slice(None), window))]


def piece_of(place, order):
    total = 0
    for b in order:
        total = 2 * total + place.bit(b)
    return total


class Gather:
    def __init__(self, place, links, ref, lead, axis, order):
        self.place, self.links, self.ref, self.lead, self.axis, self.order = place, links, ref, lead, axis, order
        self.size = ref.shape[len(ref.shape) - 2 + axis] // (1 << len(order))
        self.piece = piece_of(place, order)
        self.copy, self.stage, self.sent = None, 0, []

    def block(self, shard, width):
        first = (self.piece // width) * (width * self.size)
        return part(self.ref, (shard,) + self.lead, self.axis, pl.multiple_of(first, self.size), width * self.size)

    def begin(self):
        self.copy = self.links.start(self.block(0, 1), self.block(1, 1), self.place.twin)
        self.sent.append(self.copy)

    def advance(self):
        self.copy.wait_recv()
        if self.stage < len(self.order):
            block = self.block(1, 1 << self.stage)
            self.copy = self.links.start(block, block, self.place.over(self.order[-1 - self.stage]))
            self.sent.append(self.copy)
        self.stage += 1


def rows_loop(count, size, body):
    def step(k, carry):
        body(pl.multiple_of(k * size, size))
        return carry

    lax.fori_loop(0, count // size, step, 0)


def softplus_and_slope(values):
    tail = jnp.exp(-jnp.abs(values))
    soft = jnp.maximum(values, 0.0) + jnp.log1p(tail)
    slope = jnp.where(values >= 0, 1.0, tail) / (1.0 + tail)
    return soft, slope


def sigmoid(values):
    tail = jnp.exp(-jnp.abs(values))
    return jnp.where(values >= 0, 1.0, tail) / (1.0 + tail)


def head_of(shape, axis):
    return lax.broadcasted_iota(jnp.int32, shape, axis) // HEAD


def same_head(width):
    return head_of((width, width), 0) == head_of((width, width), 1)


def head_mean(values):
    ones = jnp.where(same_head(values.shape[-1]), 1.0 / HEAD, 0.0).astype(BF)
    return dot(values.astype(BF), ones)


def fold(state):
    width = state.shape[-1]
    state = jnp.where(same_head(width), state, 0.0)
    return (state[:, : width // 2] + state[:, width // 2 :]).astype(BF)


def unfold(state):
    both = jnp.concatenate((state, state), axis=1)
    return jnp.where(same_head(both.shape[-1]), both, jnp.zeros_like(both))


def only_head(values, head):
    return jnp.where(head_of(values.shape, 1) == head, values, jnp.zeros_like(values))


class Reduce:
    def __init__(self, place, links, moves, grad, axis, order, halves, credits, twin_recv, out, other=None):
        self.place, self.links, self.moves = place, links, moves
        self.grad, self.axis, self.order = grad, axis, order
        self.halves, self.twin_recv, self.out = halves, twin_recv, out
        self.extra = credits
        self.size = grad.shape[1 + axis] // (1 << len(order))
        self.piece = piece_of(place, order)
        self.stage, self.copy, self.local = 0, None, None
        self.other, self.ends = other, out is None
        self.steps = len(order) + len(self.extra) + (0 if self.ends else 1 + len(order))

    def first_of(self, width):
        return pl.multiple_of((self.piece // width) * (width * self.size), self.size)

    def grad_part(self, lead, first, width):
        return part(self.grad, lead, self.axis, pl.multiple_of(first, self.size), width * self.size)

    def out_part(self, width):
        return part(self.out, (), self.axis, self.first_of(width), width * self.size)

    def begin(self):
        shards, folds = (slice(None),), len(self.order)
        k = self.stage
        if k < folds:
            width = 1 << (folds - 1 - k)
            bit = self.place.bit(self.order[k])
            away = self.first_of(width) + (1 - 2 * bit) * (width * self.size)
            self.copy = self.links.start(
                self.grad_part(shards, away, width), self.halves[k], self.place.over(self.order[k])
            )
            return
        k -= folds
        if k < len(self.extra):
            peer = self.place.over(folds + k)
            pl.semaphore_signal(self.extra[k], inc=1, device_id=peer, device_id_type=MESH)
            pl.semaphore_wait(self.extra[k], 1)
            source = self.grad_part(shards, self.first_of(1), 1)
            self.copy = self.links.start(source, self.halves[-1], peer)
            return
        k -= len(self.extra)
        if k == 0:
            if self.other is not None:
                while not self.other.over():
                    self.other.advance()
                self.copy = self.other.copy
            else:
                source = self.grad_part((self.grad.shape[0] - 1,), self.first_of(1), 1)
                self.copy = self.links.start(source, self.twin_recv, self.place.twin)
            return
        k -= 1
        block = self.out_part(1 << k)
        source = self.grad_part((0,), self.first_of(1), 1) if k == 0 else block
        self.copy = self.links.start(source, block, self.place.over(self.order[folds - 1 - k]))
        if k == 0:
            self.local = self.moves.start(source, block)

    def add(self, recv, width):
        rows, chunk = recv.shape[-2], 32
        first = self.first_of(width)

        def body(at):
            for shard in range(recv.shape[0] if len(recv.shape) == 3 else 1):
                if self.axis == 0:
                    where = (shard, pl.ds(pl.multiple_of(first + at, chunk), chunk), slice(None))
                else:
                    where = (shard, pl.ds(at, chunk), pl.ds(first, width * self.size))
                came = recv[(shard,) * (len(recv.shape) - 2) + (pl.ds(at, chunk), slice(None))]
                self.grad[where] = self.grad[where] + came

        rows_loop(rows, chunk, body)

    def advance(self):
        if self.stage >= self.steps:
            return
        folds = len(self.order)
        self.copy.wait_recv()
        k = self.stage
        if k < folds:
            self.add(self.halves[k], 1 << (folds - 1 - k))
        elif k < folds + len(self.extra):
            self.links.settle(self.copy)
            self.add(self.halves[-1], 1)
        elif k == folds + len(self.extra):
            self.add(self.twin_recv, 1)
        elif self.local is not None:
            self.moves.wait(self.local)
            self.local = None
        self.stage += 1
        if self.stage < self.steps or self.ends:
            self.begin()

    def over(self):
        return self.stage >= self.steps


def marks_of(place, segr_ref, segc, tokens):
    offset = pl.multiple_of(place.pair * tokens, tokens)
    across = segr_ref[:, pl.ds(offset, tokens)].astype(F32)
    segc[...] = jnp.broadcast_to(across, (8, tokens)).T[:, :1]
    return across, segr_ref[:, tokens - 1 : tokens].astype(F32)


def doc_mask(across, segc, mask_ref, tokens, later):
    def body(first):
        at = first + lax.broadcasted_iota(jnp.int32, (64, tokens), 0)
        col = lax.broadcasted_iota(jnp.int32, (64, tokens), 1)
        order = col >= at if later else col <= at
        same = segc[pl.ds(first, 64), :] == across
        mask_ref[pl.ds(first, 64), :] = jnp.where(same & order, 1.0, 0.0).astype(BF)

    rows_loop(tokens, 64, body)


def layer_kernel(
    dp_size, extras, hidden, pad,
    x_hbm, segr_ref, wq, wk, wv, wz, wo, wl, wr, wd, g1_ref, g2_ref, cot_hbm,
    down_out, left_out, right_out, ow_out, query_out, key_out, value_out, gate_out, block_out, grad_out, gains_out,
    x_ref, segc, normed, normed_t, joined, ow, lrw, dw, qp, kp, vl, sq, sk, hn, rr, sz, gated, mask, mask_t,
    state_send, state_recv, meet_send, meet_recv, trade_send, trade_recv, back_send, back_recv,
    resid, own_sum, second, cot, hid, dres, dm, djoined, dq, dk, dv, gains, gains_recv,
    grad_d, grad_l, grad_r, grad_o,
    *rest,
):
    *received, send_sem, recv_sem, move_sem, free_sem, credit_sem = rest
    received, tickets = list(received), itertools.count()
    place = Place(dp_size)
    links, moves = Links(send_sem, recv_sem), Moves(move_sem)
    own, width = x_ref.shape
    tokens = 2 * own
    local = qp.shape[-1]
    mine = pl.multiple_of(place.half * own, own)
    theirs = pl.multiple_of((1 - place.half) * own, own)
    lw, rw = lrw.at[:, :hidden, :], lrw.at[:, hidden:, :]
    product, dleft, dright = (slice(n * pad, n * pad + hidden) for n in range(3))
    dres_all = normed

    all_here = place.greet()
    x_in = moves.start(x_hbm, x_ref)
    joined_in = [moves.start(w, joined.at[0, j]) for j, w in enumerate((wq, wk, wv, wz))]
    ow_in = moves.start(wo, ow.at[0])
    ffn_in = [moves.start(w, v.at[0]) for w, v in ((wl, lw), (wr, rw), (wd, dw))]
    cot_in = moves.start(cot_hbm, cot.at[pl.ds(mine, own), :])
    moves.wait(x_in)

    def first_norm(first):
        values = x_ref[pl.ds(first, 32), :].astype(F32)
        scale = lax.rsqrt(jnp.mean(values * values, axis=-1, keepdims=True) + EPS)
        normed[pl.ds(mine + first, 32), :] = (values * scale * g1_ref[...]).astype(BF)

    rows_loop(own, 32, first_norm)
    for copy in joined_in:
        moves.wait(copy)
    all_here()
    block = normed.at[pl.ds(mine, own), :]
    normed_copy = links.start(block, block, place.mate)
    first_order, second_order = (0, 1, 2), (0, 2, 1)
    join_a = Gather(place, links, joined, (pl.ds(0, 2),), 0, first_order)
    join_b = Gather(place, links, joined, (pl.ds(2, 2),), 0, second_order)
    gather_o = Gather(place, links, ow, (), 1, second_order)
    gather_l = Gather(place, links, lw, (), 1, first_order)
    gather_r = Gather(place, links, rw, (), 1, second_order)
    gather_d = Gather(place, links, dw, (), 1, first_order)
    join_a.begin()
    join_b.begin()
    moves.wait(ow_in)
    gather_o.begin()

    def advance(*units):
        for unit in units:
            unit.advance()

    def project(shard, first, which):
        rows = normed[pl.ds(first, own), :]
        at = pl.ds(first, own)
        for j in which:
            raw = dot(rows, joined[shard, j])
            if j == 2:
                vl[shard, at, :] = raw.astype(BF)
            elif j == 3:
                sz[shard, at, :] = sigmoid(raw).astype(BF)
            else:
                soft, slope = softplus_and_slope(raw)
                (qp, kp)[j][shard, at, :] = soft.astype(BF)
                (sq, sk)[j][shard, at, :] = slope.astype(BF)

    project(0, mine, (1, 2, 0, 3))
    across, last = marks_of(place, segr_ref, segc, tokens)
    doc_mask(across, segc, mask, tokens, False)
    near = segc[...] == last
    state_copy = [None, None]

    def send_state(shard):
        keys = jnp.where(near, kp[shard].astype(F32), 0.0).astype(BF)
        state_send[shard] = fold(dot(keys.T, vl[shard]))
        state_copy[shard] = links.start(state_send.at[shard], state_recv.at[1 - shard], place.twin)

    attention = (join_a, join_b, gather_o)
    normed_copy.wait_recv()
    advance(*attention)
    for copy in ffn_in:
        moves.wait(copy)
    gather_l.begin()
    gather_r.begin()
    gather_d.begin()
    project(0, theirs, (1, 2))
    send_state(0)
    advance(*attention)
    moves.wait(cot_in)
    cot_block = cot.at[pl.ds(mine, own), :]
    cot_copy = links.start(cot_block, cot_block, place.mate)
    project(0, theirs, (0, 3))

    def mix(shard, total):
        def one(head, carry):
            for r in range(2):
                seen = (r + 1) * own
                at = slice(r * own, (r + 1) * own)
                raw = dot_t(only_head(qp[shard, at, :], head), kp[shard, :seen, :])
                scores = raw.astype(BF) * mask[at, :seen]
                total[at, :] += dot(scores, only_head(vl[shard, :seen, :], head))
            return carry

        total[...] = jnp.zeros(total.shape, F32)
        lax.fori_loop(0, local // HEAD, one, 0)

    first_half, second_half = place.pair == 0, place.pair == 1

    def open_gate(shard, total):
        state_copy[1 - shard].wait_recv()
        query = jnp.where(near & second_half, qp[shard].astype(F32), 0.0).astype(BF)
        mixed = total[...] + dot(query, unfold(state_recv[shard]))
        scale = lax.rsqrt(head_mean(mixed * mixed) + EPS)
        norm = mixed * scale
        rr[shard] = scale.astype(BF)
        hn[shard] = norm.astype(BF)
        gated[shard] = (norm * sz[shard].astype(F32)).astype(BF)

    mix(0, dk)
    advance(*attention)
    advance(gather_l)
    advance(*attention)
    for first in (mine, theirs):
        project(1, first, (1, 2))
    send_state(1)
    advance(gather_r)
    for first in (mine, theirs):
        project(1, first, (0, 3))
    advance(gather_l, gather_d)
    mix(1, dq)
    advance(gather_r, gather_l)
    open_gate(1, dq)
    open_gate(0, dk)

    def branch(first, count=own):
        at = pl.ds(first, count)
        return dot(gated[0, at, :], ow[0]) + dot(gated[1, at, :], ow[1])

    part_rows = own // 2
    parts = [slice(0, part_rows), slice(part_rows, own)]

    def halved(partial_sum, send, recv):
        copies = []
        for rows in parts:
            send[rows, :] = partial_sum(pl.multiple_of(theirs + rows.start, part_rows), part_rows).astype(BF)
            copies.append(links.start(send.at[rows, :], recv.at[rows, :], place.mate))
        return copies

    def share(ref):
        def after(n):
            block = ref.at[pl.ds(pl.multiple_of(mine + n * part_rows, part_rows), part_rows), :]
            return links.start(block, block, place.mate)

        return after

    branch_copies = halved(branch, trade_send, trade_recv)
    own_sum[...] = branch(mine)
    advance(gather_d, gather_r)
    for c in range(0, width, 256):
        normed_t[c : c + 256, :] = normed[:, c : c + 256].T
    doc_mask(across, segc, mask_t, tokens, True)
    advance(gather_d, gather_l, gather_r)

    def second_norm(first):
        at = pl.ds(first, 32)
        values = x_ref[at, :].astype(F32) + own_sum[at, :] + trade_recv[at, :].astype(F32)
        resid[at, :] = values
        scale = lax.rsqrt(jnp.mean(values * values, axis=-1, keepdims=True) + EPS)
        second[pl.ds(mine + first, 32), :] = (values * scale * g2_ref[...]).astype(BF)

    second_copies = []
    for n, copy in enumerate(branch_copies):
        copy.wait_recv()
        rows_loop(part_rows, 32, lambda first, n=n: second_norm(pl.multiple_of(n * part_rows + first, 32)))
        second_copies.append(share(second)(n))
    cot_copy.wait_recv()
    advance(gather_d)

    def hidden_grad(first):
        at = pl.ds(first, own)

        def one(shard, carry):
            hid[shard, at, dleft] = dot_t(cot[at, :], dw[shard]).astype(BF)
            return carry

        lax.fori_loop(0, 2, one, 0)

    def unit_rows(first):
        at = pl.ds(first, own)

        def one(shard, carry):
            left = dot_t(second[at, :], lw[shard])
            right = dot_t(second[at, :], rw[shard])
            grad = hid[shard, at, dleft].astype(F32)
            hid[shard, at, product] = (left * right).astype(BF)
            hid[shard, at, dleft] = (grad * right).astype(BF)
            hid[shard, at, dright] = (grad * left).astype(BF)
            return carry

        lax.fori_loop(0, 2, one, 0)

    hidden_grad(mine)
    unit_rows(mine)
    hidden_grad(theirs)
    for copy in second_copies:
        copy.wait_recv()
    unit_rows(theirs)

    def back(first, count=own):
        at = pl.ds(first, count)
        return (
            dot(hid[0, at, dleft], lw[0])
            + dot(hid[0, at, dright], rw[0])
            + dot(hid[1, at, dleft], lw[1])
            + dot(hid[1, at, dright], rw[1])
        )

    def ffn(first):
        at = pl.ds(first, own)
        return dot(hid[0, at, product], dw[0]) + dot(hid[1, at, product], dw[1])

    back_copies = halved(back, back_send, back_recv)
    own_sum[...] = back(mine)

    def make_unit(grad, axis, order, out, first_half_ref=None, twin_recv=None, other=None):
        folds = len(order)
        halves = [received.pop(0) for _ in range(folds - (first_half_ref is not None))]
        if first_half_ref is not None:
            halves = [first_half_ref] + halves
        credits = [credit_sem.at[next(tickets)] for _ in range(extras)]
        twin_recv = received.pop(0) if twin_recv is None else twin_recv
        return Reduce(place, links, moves, grad, axis, order, halves, credits, twin_recv, out, other)

    def split_units(grad, out):
        rows = grad.shape[1] // 2
        return [
            make_unit(grad.at[:, n * rows : (n + 1) * rows, :], 1, order, out.at[n * rows : (n + 1) * rows, :])
            for n, order in enumerate((first_order, second_order))
        ]

    down_units, left_units, right_units = (
        split_units(g, o) for g, o in ((grad_d, down_out), (grad_l, left_out), (grad_r, right_out))
    )
    ow_units = split_units(grad_o, ow_out)
    joined_units = []
    for j, (order, out) in enumerate(
        zip((first_order, second_order, first_order, second_order), (query_out, key_out, value_out, gate_out))
    ):
        columns = slice(j * local, (j + 1) * local)
        grad, landing = lrw.at[:, :width, columns], hid.at[:, : width // 2, columns]
        if j == 3:
            joined_units.append(make_unit(grad, 0, order, out, landing))
            continue
        away = make_unit(grad.at[1:2], 0, order, None, landing.at[1:2])
        near_unit = make_unit(grad.at[0:1], 0, order, out, landing.at[0:1], away.twin_recv, away)
        joined_units.append((near_unit, away))
    live = []

    def launch(*units):
        for unit in units:
            unit.begin()
            live.append(unit)

    def step_all():
        for unit in live:
            unit.advance()

    def hidden_outer(units, grad, left, right):
        def one(shard, carry):
            for c in range(0, hidden, 256):
                high = min(c + 256, hidden)
                grad[shard, c:high, :] = dot(hid[shard, :, left.start + c : left.start + high].T, right[...]).astype(BF)
            return carry

        lax.fori_loop(0, 2, one, 0)
        launch(*units)

    hidden_outer(down_units, grad_d, product, cot)
    hidden_outer(left_units, grad_l, dleft, second)
    advance(*down_units)
    hidden_outer(right_units, grad_r, dright, second)
    advance(*left_units)
    pl.semaphore_signal(free_sem, inc=1, device_id=place.over(0), device_id_type=MESH)
    gains[0] = jnp.zeros(gains.shape[1:], F32)

    def residual_back(first):
        at = pl.ds(first, 32)
        values = resid[at, :]
        scale = lax.rsqrt(jnp.mean(values * values, axis=-1, keepdims=True) + EPS)
        grad = own_sum[at, :] + back_recv[at, :].astype(F32)
        gains[0, 0:1, :] += jnp.sum(grad * values * scale, axis=0, keepdims=True)
        weighted = grad * g2_ref[...]
        inner = jnp.mean(weighted * values, axis=-1, keepdims=True)
        upstream = cot[pl.ds(mine + first, 32), :].astype(F32)
        total = upstream + scale * weighted - values * (scale * scale * scale * inner)
        dres[at, :] = total
        dres_all[pl.ds(mine + first, 32), :] = total.astype(BF)

    links.settle(normed_copy)
    dres_copies = []
    for n, copy in enumerate(back_copies):
        copy.wait_recv()
        rows_loop(part_rows, 32, lambda first, n=n: residual_back(pl.multiple_of(n * part_rows + first, 32)))
        dres_copies.append(share(dres_all)(n))
    advance(*right_units)
    links.settle(*back_copies)
    back_send[...] = ffn(theirs).astype(BF)

    def add_ffn(first):
        resid[...] += ffn(first)

    add_ffn(mine)
    advance(*down_units)
    for copy in dres_copies:
        copy.wait_recv()
    ffn_copy = links.start(back_send, back_recv, place.mate)

    def gate_back(shard, carry):
        grad = dot_t(dres_all[...], ow[shard])
        opened, norm = sz[shard].astype(F32), hn[shard].astype(F32)
        djoined[shard, 3] = (grad * norm * opened * (1.0 - opened)).astype(BF)
        inner = grad * opened
        dm[shard] = (rr[shard].astype(F32) * (inner - norm * head_mean(inner * norm))).astype(BF)
        return carry

    lax.fori_loop(0, 2, gate_back, 0)
    meets = []
    for shard in range(2):
        query = jnp.where(near, qp[shard].astype(F32), 0.0).astype(BF)
        meet_send[shard] = fold(dot(query.T, dm[shard]))
        meets.append(links.start(meet_send.at[shard], meet_recv.at[1 - shard], place.twin))

    def out_outer(shard, carry):
        grad_o[shard] = dot(gated[shard].T, dres_all[...]).astype(BF)
        return carry

    lax.fori_loop(0, 2, out_outer, 0)
    launch(*ow_units)
    gathers = (join_a, join_b, gather_o, gather_l, gather_r, gather_d)
    for unit in gathers:
        links.settle(*unit.sent)
    pl.semaphore_wait(free_sem, 1)

    def project_back(j, shard):
        def body(first):
            part_grad = dot(normed_t[pl.ds(first, 256), :], djoined[shard, j])
            lrw[shard, pl.ds(first, 256), j * local : (j + 1) * local] = part_grad.astype(BF)

        rows_loop(width, 256, body)

    project_back(3, 0)
    project_back(3, 1)
    launch(joined_units[3])
    step_all()

    def mix_back(shard):
        dq[...] = jnp.where(near & second_half, dot_t(dm[shard], unfold(state_recv[shard])), 0.0)
        dk[...] = jnp.zeros(dk.shape, F32)
        dv[...] = jnp.zeros(dv.shape, F32)

        def one(head, carry):
            for r in range(2):
                seen = (r + 1) * own
                at = slice(r * own, (r + 1) * own)
                grad_r, query_r = dm[shard, at, :], qp[shard, at, :]
                grad_h, query_h = only_head(grad_r, head), only_head(query_r, head)
                keys_h = only_head(kp[shard, :seen, :], head)
                vals_h = only_head(vl[shard, :seen, :], head)
                ds = dot_t(grad_r, vals_h).astype(BF) * mask[at, :seen]
                dq[at, :] += dot(ds, keys_h)
                st = dot_t(keys_h, query_r).astype(BF) * mask_t[:seen, at]
                dv[:seen, :] += dot(st, grad_h)
                dst = dot_t(vals_h, grad_r).astype(BF) * mask_t[:seen, at]
                dk[:seen, :] += dot(dst, query_h)
            return carry

        lax.fori_loop(0, local // HEAD, one, 0)

    for shard in (1, 0):
        mix_back(shard)
        meets[1 - shard].wait_recv()
        meet = unfold(meet_recv[shard])
        marks = near & first_half
        djoined[shard, 2] = (dv[...] + jnp.where(marks, dot(kp[shard], meet), 0.0)).astype(BF)
        from_meet = jnp.where(marks, dot_t(vl[shard], meet), 0.0)
        djoined[shard, 1] = ((dk[...] + from_meet) * sk[shard].astype(F32)).astype(BF)
        djoined[shard, 0] = (dq[...] * sq[shard].astype(F32)).astype(BF)
        if shard == 1:
            step_all()
        for j in range(3):
            project_back(j, shard)
            launch(joined_units[j][shard])

    def normed_back(first):
        at = pl.ds(first, own)
        own_sum[...] = jnp.zeros(own_sum.shape, F32)

        def one(k, carry):
            own_sum[...] += dot_t(djoined[k // 4, lax.rem(k, 4), at, :], joined[k // 4, lax.rem(k, 4)])
            return carry

        lax.fori_loop(0, 8, one, 0)

    links.settle(*branch_copies)
    normed_back(theirs)
    trade_send[...] = own_sum[...].astype(BF)
    trade_copy = links.start(trade_send, trade_recv, place.mate)
    step_all()
    normed_back(mine)
    ffn_copy.wait_recv()
    links.settle(ffn_copy)

    def finish_out(first):
        at = pl.ds(first, 32)
        back_send[at, :] = (resid[at, :] + back_recv[at, :].astype(F32)).astype(BF)

    rows_loop(own, 32, finish_out)
    moves.start(back_send, block_out)
    step_all()
    trade_copy.wait_recv()
    links.settle(trade_copy)

    def finish_grad(first):
        at = pl.ds(first, 32)
        values = x_ref[at, :].astype(F32)
        scale = lax.rsqrt(jnp.mean(values * values, axis=-1, keepdims=True) + EPS)
        grad = own_sum[at, :] + trade_recv[at, :].astype(F32)
        gains[0, 1:2, :] += jnp.sum(grad * values * scale, axis=0, keepdims=True)
        weighted = grad * g1_ref[...]
        inner = jnp.mean(weighted * values, axis=-1, keepdims=True)
        trade_send[at, :] = (dres[at, :] + scale * weighted - values * (scale * scale * scale * inner)).astype(BF)

    rows_loop(own, 32, finish_grad)
    moves.start(trade_send, grad_out)

    first = 0
    for n, peers in enumerate((place.rows, place.columns)):
        copies = [links.start(gains.at[n], gains_recv.at[first + k], peer) for k, peer in enumerate(peers)]
        step_all()
        for copy in copies:
            copy.wait_recv()
        gains[n + 1] = gains[n] + jnp.sum(gains_recv[first : first + len(peers)], axis=0)
        first += len(peers)
    moves.start(gains.at[2], gains_out)
    while not all(unit.over() for unit in live):
        step_all()
    moves.finish()
    links.finish()


def widen_kernel(count, passed, *refs):
    sources, refs = refs[: count + passed], refs[count + passed :]
    targets, refs = refs[: count + passed], refs[count + passed :]
    total = count + passed
    narrow, wide, (in_sem, out_sem) = refs[:total], refs[total : total + count], refs[total + count :]
    loads = [pltpu.make_async_copy(sources[n], narrow[n], in_sem.at[n]) for n in range(total)]
    results = list(wide) + list(narrow[count:])
    stores = [pltpu.make_async_copy(results[n], targets[n], out_sem.at[n]) for n in range(total)]
    for copy in loads:
        copy.start()
    for n in range(count):
        loads[n].wait()

        def body(first, n=n):
            wide[n][pl.ds(first, 64), :] = narrow[n][pl.ds(first, 64), :].astype(F32)

        rows_loop(narrow[n].shape[0], 64, body)
        stores[n].start()
    for n in range(count, total):
        loads[n].wait()
        stores[n].start()
    for copy in stores:
        copy.wait()


def vmem(shape, dtype=BF):
    return pltpu.VMEM(shape, dtype)


def per_device(
    dp_size,
    inputs, segments, query_weight, key_weight, value_weight, gate_weight, out_weight, left_weight, right_weight,
    down_weight, norm_first, norm_second, cotangent,
):
    own, width = inputs.shape
    tokens = 2 * own
    local = query_weight.shape[1]
    hidden = left_weight.shape[1]
    pad = -(-hidden // 128) * 128
    bits = dp_size.bit_length() - 1
    extras = bits - PIECE_BITS
    shape = jax.ShapeDtypeStruct
    heads, state = (2, tokens, local), (2, local, local // 2)
    grads = [(hidden, width)] * 3 + [(local, width)] + [(width, local)] * 4

    def buffers(rows, columns, axis, first, shards=2):
        def cut(parts):
            return (shards, rows // parts, columns) if axis == 0 else (shards, rows, columns // parts)

        eighth = cut(1 << PIECE_BITS)
        kept = [vmem(cut(2 << k)) for k in range(first, PIECE_BITS)]
        return kept + [vmem(eighth[1:])]

    received = []
    for rows in (hidden // 2,) * 6 + (local // 2,) * 2:
        received += buffers(rows, width, 1, 0)
    for _ in range(3):
        away = buffers(width, local, 0, 1, 1)
        received += away + away[:-1]
    received += buffers(width, local, 0, 1)
    copies = 15 * (2 * PIECE_BITS + extras + 1) + 6 * (PIECE_BITS + 1) + dp_size + 20
    results = pl.pallas_call(
        functools.partial(layer_kernel, dp_size, extras, hidden, pad),
        out_shape=[shape(full, BF) for full in grads]
        + [shape((own, width), BF), shape((own, width), BF), shape((2, width), F32)],
        in_specs=[ANY, INNER] + [ANY] * 8 + [INNER, INNER, ANY],
        out_specs=[ANY] * 11,
        scratch_shapes=[
            vmem((own, width)), vmem((tokens, 1), F32), vmem((tokens, width)), vmem((width, tokens)),
            vmem((2, 4, width, local)), vmem((2, local, width)), vmem((2, 2 * hidden, width)),
            vmem((2, hidden, width)),
        ]
        + [vmem(heads)] * 9
        + [vmem((tokens, tokens))] * 2
        + [vmem(state)] * 4
        + [vmem((own, width))] * 4
        + [vmem((own, width), F32)] * 2
        + [
            vmem((tokens, width)), vmem((tokens, width)), vmem((2, tokens, 3 * pad)), vmem((own, width), F32),
            vmem(heads), vmem((2, 4, tokens, local)),
        ]
        + [vmem((tokens, local), F32)] * 3
        + [vmem((3, 2, width), F32), vmem((dp_size + 2, 2, width), F32)]
        + [vmem((2, hidden, width))] * 3
        + [vmem((2, local, width))]
        + received
        + [pltpu.SemaphoreType.DMA((copies,))] * 2
        + [
            pltpu.SemaphoreType.DMA((40,)), pltpu.SemaphoreType.REGULAR,
            pltpu.SemaphoreType.REGULAR((max(1, 15 * extras),)),
        ],
        compiler_params=pltpu.CompilerParams(collective_id=0, has_side_effects=True, vmem_limit_bytes=63 << 20),
    )(
        inputs, segments, query_weight, key_weight, value_weight, gate_weight, out_weight, left_weight.T,
        right_weight.T, down_weight, norm_first.reshape(1, -1), norm_second.reshape(1, -1), cotangent,
    )
    count, passed = len(grads), 3
    wide = pl.pallas_call(
        functools.partial(widen_kernel, count, passed),
        out_shape=[shape(full, F32) for full in grads] + [shape(r.shape, r.dtype) for r in results[count:]],
        in_specs=[ANY] * (count + passed),
        out_specs=[ANY] * (count + passed),
        scratch_shapes=[vmem(r.shape, r.dtype) for r in results]
        + [vmem(full, F32) for full in grads]
        + [pltpu.SemaphoreType.DMA((count + passed,))] * 2,
        compiler_params=pltpu.CompilerParams(vmem_limit_bytes=62 << 20),
    )(*results)
    down, left, right, out, query, key, value, gate, block, block_grad, gains = wide
    return (
        block, block_grad, query, key, value, gate, out, left.T, right.T, down, gains[1], gains[0],
    )


def solution(mesh):
    row, column = P("tensor", None), P(None, "tensor")
    tokens = P(("dp", "tensor"), None)
    return jax.shard_map(
        functools.partial(per_device, mesh.shape["dp"]),
        mesh=mesh,
        in_specs=(
            tokens, P("dp", None), column, column, column, column, row, column, column, row, P(), P(), tokens,
        ),
        out_specs=(tokens, tokens, column, column, column, column, row, column, column, row, P(), P()),
        check_vma=False,
    )
```

```python
import functools
import itertools

import jax
import jax.numpy as jnp
from jax import lax
from jax.experimental import pallas as pl
from jax.experimental.pallas import tpu as pltpu
from jax.sharding import PartitionSpec as P

EPS = 1e-05
HEAD = 64
BF = jnp.bfloat16
F32 = jnp.float32
MESH = pl.DeviceIdType.MESH
ANY = pl.BlockSpec(memory_space=pl.ANY)
INNER = pl.BlockSpec(memory_space=pltpu.VMEM)
PIECE_BITS = 3


def dot(a, b):
    return lax.dot_general(a, b, (((1,), (0,)), ((), ())), preferred_element_type=F32)


def dot_t(a, b):
    return lax.dot_general(a, b, (((1,), (1,)), ((), ())), preferred_element_type=F32)


class Place:
    def __init__(self, dp_size):
        self.i = lax.axis_index("dp")
        self.t = lax.axis_index("tensor")
        self.half = lax.rem(self.t, 2)
        self.pair = self.t // 2
        self.bits = dp_size.bit_length() - 1
        self.rows = [{"dp": lax.rem(self.i + k, dp_size)} for k in range(1, dp_size)]
        self.columns = [{"tensor": lax.rem(self.t + k, 4)} for k in range(1, 4)]
        self.mate = {"tensor": self.t + 1 - 2 * self.half}
        self.twin = {"tensor": self.t + 2 - 4 * self.pair}

    def bit(self, b):
        return lax.rem(self.i // (1 << b), 2)

    def over(self, b):
        return {"dp": self.i + (1 << b) * (1 - 2 * self.bit(b))}

    def greet(self):
        barrier = pltpu.get_barrier_semaphore()
        peers = self.rows + self.columns
        for peer in peers:
            pl.semaphore_signal(barrier, inc=1, device_id=peer, device_id_type=MESH)

        def all_here():
            pl.semaphore_wait(barrier, len(peers))

        return all_here


class Links:
    def __init__(self, send_sem, recv_sem):
        self.send_sem, self.recv_sem, self.count, self.open = send_sem, recv_sem, 0, []

    def start(self, source, target, peer):
        copy = pltpu.make_async_remote_copy(
            src_ref=source,
            dst_ref=target,
            send_sem=self.send_sem.at[self.count],
            recv_sem=self.recv_sem.at[self.count],
            device_id=peer,
            device_id_type=MESH,
        )
        self.count += 1
        copy.start()
        self.open.append(copy)
        return copy

    def settle(self, *copies):
        for copy in copies:
            copy.wait_send()
        self.open = [other for other in self.open if all(other is not copy for copy in copies)]

    def finish(self):
        self.settle(*self.open)


class Moves:
    def __init__(self, sem):
        self.sem, self.count, self.open = sem, 0, []

    def start(self, source, target):
        copy = pltpu.make_async_copy(source, target, self.sem.at[self.count])
        self.count += 1
        copy.start()
        self.open.append(copy)
        return copy

    def wait(self, copy):
        copy.wait()
        self.open = [other for other in self.open if other is not copy]

    def finish(self):
        for copy in list(self.open):
            self.wait(copy)


def part(ref, lead, axis, first, count):
    window = pl.ds(first, count)
    return ref.at[lead + ((window, slice(None)) if axis == 0 else (slice(None), window))]


def piece_of(place, order):
    total = 0
    for b in order:
        total = 2 * total + place.bit(b)
    return total


class Gather:
    def __init__(self, place, links, ref, lead, axis, order):
        self.place, self.links, self.ref, self.lead, self.axis, self.order = place, links, ref, lead, axis, order
        self.size = ref.shape[len(ref.shape) - 2 + axis] // (1 << len(order))
        self.piece = piece_of(place, order)
        self.copy, self.stage, self.sent = None, 0, []

    def block(self, shard, width):
        first = (self.piece // width) * (width * self.size)
        return part(self.ref, (shard,) + self.lead, self.axis, pl.multiple_of(first, self.size), width * self.size)

    def begin(self):
        self.copy = self.links.start(self.block(0, 1), self.block(1, 1), self.place.twin)
        self.sent.append(self.copy)

    def advance(self):
        self.copy.wait_recv()
        if self.stage < len(self.order):
            block = self.block(1, 1 << self.stage)
            self.copy = self.links.start(block, block, self.place.over(self.order[-1 - self.stage]))
            self.sent.append(self.copy)
        self.stage += 1


def rows_loop(count, size, body):
    def step(k, carry):
        body(pl.multiple_of(k * size, size))
        return carry

    lax.fori_loop(0, count // size, step, 0)


def softplus_and_slope(values):
    tail = jnp.exp(-jnp.abs(values))
    soft = jnp.maximum(values, 0.0) + jnp.log1p(tail)
    slope = jnp.where(values >= 0, 1.0, tail) / (1.0 + tail)
    return soft, slope


def sigmoid(values):
    tail = jnp.exp(-jnp.abs(values))
    return jnp.where(values >= 0, 1.0, tail) / (1.0 + tail)


def head_of(shape, axis):
    return lax.broadcasted_iota(jnp.int32, shape, axis) // HEAD


def same_head(width):
    return head_of((width, width), 0) == head_of((width, width), 1)


def head_mean(values):
    ones = jnp.where(same_head(values.shape[-1]), 1.0 / HEAD, 0.0).astype(BF)
    return dot(values.astype(BF), ones)


def fold(state):
    width = state.shape[-1]
    state = jnp.where(same_head(width), state, 0.0)
    return (state[:, : width // 2] + state[:, width // 2 :]).astype(BF)


def unfold(state):
    both = jnp.concatenate((state, state), axis=1)
    return jnp.where(same_head(both.shape[-1]), both, jnp.zeros_like(both))


def only_head(values, head):
    return jnp.where(head_of(values.shape, 1) == head, values, jnp.zeros_like(values))


class Reduce:
    def __init__(self, place, links, moves, grad, axis, order, halves, credits, twin_recv, out, other=None):
        self.place, self.links, self.moves = place, links, moves
        self.grad, self.axis, self.order = grad, axis, order
        self.halves, self.twin_recv, self.out = halves, twin_recv, out
        self.extra = credits
        self.size = grad.shape[1 + axis] // (1 << len(order))
        self.piece = piece_of(place, order)
        self.stage, self.copy, self.local = 0, None, None
        self.other, self.ends = other, out is None
        self.steps = len(order) + len(self.extra) + (0 if self.ends else 1 + len(order))

    def first_of(self, width):
        return pl.multiple_of((self.piece // width) * (width * self.size), self.size)

    def grad_part(self, lead, first, width):
        return part(self.grad, lead, self.axis, pl.multiple_of(first, self.size), width * self.size)

    def out_part(self, width):
        return part(self.out, (), self.axis, self.first_of(width), width * self.size)

    def begin(self):
        shards, folds = (slice(None),), len(self.order)
        k = self.stage
        if k < folds:
            width = 1 << (folds - 1 - k)
            bit = self.place.bit(self.order[k])
            away = self.first_of(width) + (1 - 2 * bit) * (width * self.size)
            self.copy = self.links.start(
                self.grad_part(shards, away, width), self.halves[k], self.place.over(self.order[k])
            )
            return
        k -= folds
        if k < len(self.extra):
            peer = self.place.over(folds + k)
            pl.semaphore_signal(self.extra[k], inc=1, device_id=peer, device_id_type=MESH)
            pl.semaphore_wait(self.extra[k], 1)
            source = self.grad_part(shards, self.first_of(1), 1)
            self.copy = self.links.start(source, self.halves[-1], peer)
            return
        k -= len(self.extra)
        if k == 0:
            if self.other is not None:
                while not self.other.over():
                    self.other.advance()
                self.copy = self.other.copy
            else:
                source = self.grad_part((self.grad.shape[0] - 1,), self.first_of(1), 1)
                self.copy = self.links.start(source, self.twin_recv, self.place.twin)
            return
        k -= 1
        block = self.out_part(1 << k)
        source = self.grad_part((0,), self.first_of(1), 1) if k == 0 else block
        self.copy = self.links.start(source, block, self.place.over(self.order[folds - 1 - k]))
        if k == 0:
            self.local = self.moves.start(source, block)

    def add(self, recv, width):
        rows, chunk = recv.shape[-2], 32
        first = self.first_of(width)

        def body(at):
            for shard in range(recv.shape[0] if len(recv.shape) == 3 else 1):
                if self.axis == 0:
                    where = (shard, pl.ds(pl.multiple_of(first + at, chunk), chunk), slice(None))
                else:
                    where = (shard, pl.ds(at, chunk), pl.ds(first, width * self.size))
                came = recv[(shard,) * (len(recv.shape) - 2) + (pl.ds(at, chunk), slice(None))]
                self.grad[where] = self.grad[where] + came

        rows_loop(rows, chunk, body)

    def advance(self):
        if self.stage >= self.steps:
            return
        folds = len(self.order)
        self.copy.wait_recv()
        k = self.stage
        if k < folds:
            self.add(self.halves[k], 1 << (folds - 1 - k))
        elif k < folds + len(self.extra):
            self.links.settle(self.copy)
            self.add(self.halves[-1], 1)
        elif k == folds + len(self.extra):
            self.add(self.twin_recv, 1)
        elif self.local is not None:
            self.moves.wait(self.local)
            self.local = None
        self.stage += 1
        if self.stage < self.steps or self.ends:
            self.begin()

    def over(self):
        return self.stage >= self.steps


def marks_of(place, segr_ref, segc, tokens):
    offset = pl.multiple_of(place.pair * tokens, tokens)
    across = segr_ref[:, pl.ds(offset, tokens)].astype(F32)
    segc[...] = jnp.broadcast_to(across, (8, tokens)).T[:, :1]
    return across, segr_ref[:, tokens - 1 : tokens].astype(F32)


def doc_mask(across, segc, mask_ref, tokens, later):
    def body(first):
        at = first + lax.broadcasted_iota(jnp.int32, (64, tokens), 0)
        col = lax.broadcasted_iota(jnp.int32, (64, tokens), 1)
        order = col >= at if later else col <= at
        same = segc[pl.ds(first, 64), :] == across
        mask_ref[pl.ds(first, 64), :] = jnp.where(same & order, 1.0, 0.0).astype(BF)

    rows_loop(tokens, 64, body)


def layer_kernel(
    dp_size, extras, hidden, pad,
    x_hbm, segr_ref, wq, wk, wv, wz, wo, wl, wr, wd, g1_ref, g2_ref, cot_hbm,
    down_out, left_out, right_out, ow_out, query_out, key_out, value_out, gate_out, block_out, grad_out, gains_out,
    x_ref, segc, normed, normed_t, joined, ow, lrw, dw, qp, kp, vl, sq, sk, hn, rr, sz, gated, mask, mask_t,
    state_send, state_recv, meet_send, meet_recv, trade_send, trade_recv, back_send, back_recv,
    resid, own_sum, second, cot, hid, dres, dm, djoined, dq, dk, dv, gains, gains_recv,
    grad_d, grad_l, grad_r, grad_o,
    *rest,
):
    *received, send_sem, recv_sem, move_sem, free_sem, credit_sem = rest
    received, tickets = list(received), itertools.count()
    place = Place(dp_size)
    links, moves = Links(send_sem, recv_sem), Moves(move_sem)
    own, width = x_ref.shape
    tokens = 2 * own
    local = qp.shape[-1]
    mine = pl.multiple_of(place.half * own, own)
    theirs = pl.multiple_of((1 - place.half) * own, own)
    lw, rw = lrw.at[:, :hidden, :], lrw.at[:, hidden:, :]
    product, dleft, dright = (slice(n * pad, n * pad + hidden) for n in range(3))
    dres_all = normed

    all_here = place.greet()
    x_in = moves.start(x_hbm, x_ref)
    joined_in = [moves.start(w, joined.at[0, j]) for j, w in enumerate((wq, wk, wv, wz))]
    ow_in = moves.start(wo, ow.at[0])
    ffn_in = [moves.start(w, v.at[0]) for w, v in ((wl, lw), (wr, rw), (wd, dw))]
    cot_in = moves.start(cot_hbm, cot.at[pl.ds(mine, own), :])
    moves.wait(x_in)

    def first_norm(first):
        values = x_ref[pl.ds(first, 32), :].astype(F32)
        scale = lax.rsqrt(jnp.mean(values * values, axis=-1, keepdims=True) + EPS)
        normed[pl.ds(mine + first, 32), :] = (values * scale * g1_ref[...]).astype(BF)

    rows_loop(own, 32, first_norm)
    for copy in joined_in:
        moves.wait(copy)
    all_here()
    block = normed.at[pl.ds(mine, own), :]
    normed_copy = links.start(block, block, place.mate)
    first_order, second_order = (0, 1, 2), (0, 2, 1)
    join_a = Gather(place, links, joined, (pl.ds(0, 2),), 0, first_order)
    join_b = Gather(place, links, joined, (pl.ds(2, 2),), 0, second_order)
    gather_o = Gather(place, links, ow, (), 1, second_order)
    gather_l = Gather(place, links, lw, (), 1, first_order)
    gather_r = Gather(place, links, rw, (), 1, second_order)
    gather_d = Gather(place, links, dw, (), 1, first_order)
    join_a.begin()
    join_b.begin()
    moves.wait(ow_in)
    gather_o.begin()

    def advance(*units):
        for unit in units:
            unit.advance()

    def project(shard, first, which):
        rows = normed[pl.ds(first, own), :]
        at = pl.ds(first, own)
        for j in which:
            raw = dot(rows, joined[shard, j])
            if j == 2:
                vl[shard, at, :] = raw.astype(BF)
            elif j == 3:
                sz[shard, at, :] = sigmoid(raw).astype(BF)
            else:
                soft, slope = softplus_and_slope(raw)
                (qp, kp)[j][shard, at, :] = soft.astype(BF)
                (sq, sk)[j][shard, at, :] = slope.astype(BF)

    project(0, mine, (1, 2, 0, 3))
    across, last = marks_of(place, segr_ref, segc, tokens)
    doc_mask(across, segc, mask, tokens, False)
    near = segc[...] == last
    state_copy = [None, None]

    def send_state(shard):
        keys = jnp.where(near, kp[shard].astype(F32), 0.0).astype(BF)
        state_send[shard] = fold(dot(keys.T, vl[shard]))
        state_copy[shard] = links.start(state_send.at[shard], state_recv.at[1 - shard], place.twin)

    attention = (join_a, join_b, gather_o)
    normed_copy.wait_recv()
    advance(*attention)
    for copy in ffn_in:
        moves.wait(copy)
    gather_l.begin()
    gather_r.begin()
    gather_d.begin()
    project(0, theirs, (1, 2))
    send_state(0)
    advance(*attention)
    moves.wait(cot_in)
    cot_block = cot.at[pl.ds(mine, own), :]
    cot_copy = links.start(cot_block, cot_block, place.mate)
    project(0, theirs, (0, 3))

    def mix(shard, total):
        def one(head, carry):
            for r in range(2):
                seen = (r + 1) * own
                at = slice(r * own, (r + 1) * own)
                raw = dot_t(only_head(qp[shard, at, :], head), kp[shard, :seen, :])
                scores = raw.astype(BF) * mask[at, :seen]
                total[at, :] += dot(scores, only_head(vl[shard, :seen, :], head))
            return carry

        total[...] = jnp.zeros(total.shape, F32)
        lax.fori_loop(0, local // HEAD, one, 0)

    first_half, second_half = place.pair == 0, place.pair == 1

    def open_gate(shard, total):
        state_copy[1 - shard].wait_recv()
        query = jnp.where(near & second_half, qp[shard].astype(F32), 0.0).astype(BF)
        mixed = total[...] + dot(query, unfold(state_recv[shard]))
        scale = lax.rsqrt(head_mean(mixed * mixed) + EPS)
        norm = mixed * scale
        rr[shard] = scale.astype(BF)
        hn[shard] = norm.astype(BF)
        gated[shard] = (norm * sz[shard].astype(F32)).astype(BF)

    mix(0, dk)
    advance(*attention)
    advance(gather_l)
    advance(*attention)
    for first in (mine, theirs):
        project(1, first, (1, 2))
    send_state(1)
    advance(gather_r)
    for first in (mine, theirs):
        project(1, first, (0, 3))
    advance(gather_l)
    mix(1, dq)
    advance(gather_r)
    open_gate(1, dq)
    open_gate(0, dk)

    def branch(first, count=own):
        at = pl.ds(first, count)
        return dot(gated[0, at, :], ow[0]) + dot(gated[1, at, :], ow[1])

    part_rows = own // 2
    parts = [slice(0, part_rows), slice(part_rows, own)]

    def halved(partial_sum, send, recv):
        copies = []
        for rows in parts:
            send[rows, :] = partial_sum(pl.multiple_of(theirs + rows.start, part_rows), part_rows).astype(BF)
            copies.append(links.start(send.at[rows, :], recv.at[rows, :], place.mate))
        return copies

    def share(ref):
        def after(n):
            block = ref.at[pl.ds(pl.multiple_of(mine + n * part_rows, part_rows), part_rows), :]
            return links.start(block, block, place.mate)

        return after

    branch_copies = halved(branch, trade_send, trade_recv)
    advance(gather_d, gather_l)
    own_sum[...] = branch(mine)
    advance(gather_r, gather_d)
    for c in range(0, width, 256):
        normed_t[c : c + 256, :] = normed[:, c : c + 256].T
    doc_mask(across, segc, mask_t, tokens, True)
    advance(gather_d, gather_l, gather_r)

    def second_norm(first):
        at = pl.ds(first, 32)
        values = x_ref[at, :].astype(F32) + own_sum[at, :] + trade_recv[at, :].astype(F32)
        resid[at, :] = values
        scale = lax.rsqrt(jnp.mean(values * values, axis=-1, keepdims=True) + EPS)
        second[pl.ds(mine + first, 32), :] = (values * scale * g2_ref[...]).astype(BF)

    second_copies = []
    for n, copy in enumerate(branch_copies):
        copy.wait_recv()
        rows_loop(part_rows, 32, lambda first, n=n: second_norm(pl.multiple_of(n * part_rows + first, 32)))
        second_copies.append(share(second)(n))
    cot_copy.wait_recv()
    advance(gather_d)

    def hidden_grad(first):
        at = pl.ds(first, own)

        def one(shard, carry):
            hid[shard, at, dleft] = dot_t(cot[at, :], dw[shard]).astype(BF)
            return carry

        lax.fori_loop(0, 2, one, 0)

    def unit_rows(first):
        at = pl.ds(first, own)

        def one(shard, carry):
            left = dot_t(second[at, :], lw[shard])
            right = dot_t(second[at, :], rw[shard])
            grad = hid[shard, at, dleft].astype(F32)
            hid[shard, at, product] = (left * right).astype(BF)
            hid[shard, at, dleft] = (grad * right).astype(BF)
            hid[shard, at, dright] = (grad * left).astype(BF)
            return carry

        lax.fori_loop(0, 2, one, 0)

    hidden_grad(mine)
    unit_rows(mine)
    hidden_grad(theirs)
    for copy in second_copies:
        copy.wait_recv()
    unit_rows(theirs)

    def back(first, count=own):
        at = pl.ds(first, count)
        return (
            dot(hid[0, at, dleft], lw[0])
            + dot(hid[0, at, dright], rw[0])
            + dot(hid[1, at, dleft], lw[1])
            + dot(hid[1, at, dright], rw[1])
        )

    def ffn(first):
        at = pl.ds(first, own)
        return dot(hid[0, at, product], dw[0]) + dot(hid[1, at, product], dw[1])

    back_copies = halved(back, back_send, back_recv)
    own_sum[...] = back(mine)

    def make_unit(grad, axis, order, out, first_half_ref=None, twin_recv=None, other=None):
        folds = len(order)
        halves = [received.pop(0) for _ in range(folds - (first_half_ref is not None))]
        if first_half_ref is not None:
            halves = [first_half_ref] + halves
        credits = [credit_sem.at[next(tickets)] for _ in range(extras)]
        twin_recv = received.pop(0) if twin_recv is None else twin_recv
        return Reduce(place, links, moves, grad, axis, order, halves, credits, twin_recv, out, other)

    def split_units(grad, out):
        rows = grad.shape[1] // 2
        return [
            make_unit(grad.at[:, n * rows : (n + 1) * rows, :], 1, order, out.at[n * rows : (n + 1) * rows, :])
            for n, order in enumerate((first_order, second_order))
        ]

    down_units, left_units, right_units = (
        split_units(g, o) for g, o in ((grad_d, down_out), (grad_l, left_out), (grad_r, right_out))
    )
    ow_units = split_units(grad_o, ow_out)
    joined_units = []
    for j, (order, out) in enumerate(
        zip((first_order, second_order, first_order, second_order), (query_out, key_out, value_out, gate_out))
    ):
        columns = slice(j * local, (j + 1) * local)
        grad, landing = lrw.at[:, :width, columns], hid.at[:, : width // 2, columns]
        if j == 3:
            joined_units.append(make_unit(grad, 0, order, out, landing))
            continue
        away = make_unit(grad.at[1:2], 0, order, None, landing.at[1:2])
        near_unit = make_unit(grad.at[0:1], 0, order, out, landing.at[0:1], away.twin_recv, away)
        joined_units.append((near_unit, away))
    live = []

    def launch(*units):
        for unit in units:
            unit.begin()
            live.append(unit)

    def step_all(late=False):
        for unit in reversed(live) if late else live:
            unit.advance()

    def hidden_outer(units, grad, left, right):
        def one(shard, carry):
            for c in range(0, hidden, 256):
                high = min(c + 256, hidden)
                grad[shard, c:high, :] = dot(hid[shard, :, left.start + c : left.start + high].T, right[...]).astype(BF)
            return carry

        lax.fori_loop(0, 2, one, 0)
        launch(*units)

    hidden_outer(down_units, grad_d, product, cot)
    hidden_outer(left_units, grad_l, dleft, second)
    advance(*down_units)
    hidden_outer(right_units, grad_r, dright, second)
    advance(*left_units)
    pl.semaphore_signal(free_sem, inc=1, device_id=place.over(0), device_id_type=MESH)
    gains[0] = jnp.zeros(gains.shape[1:], F32)

    def residual_back(first):
        at = pl.ds(first, 32)
        values = resid[at, :]
        scale = lax.rsqrt(jnp.mean(values * values, axis=-1, keepdims=True) + EPS)
        grad = own_sum[at, :] + back_recv[at, :].astype(F32)
        gains[0, 0:1, :] += jnp.sum(grad * values * scale, axis=0, keepdims=True)
        weighted = grad * g2_ref[...]
        inner = jnp.mean(weighted * values, axis=-1, keepdims=True)
        upstream = cot[pl.ds(mine + first, 32), :].astype(F32)
        total = upstream + scale * weighted - values * (scale * scale * scale * inner)
        dres[at, :] = total
        dres_all[pl.ds(mine + first, 32), :] = total.astype(BF)

    links.settle(normed_copy)
    dres_copies = []
    for n, copy in enumerate(back_copies):
        copy.wait_recv()
        rows_loop(part_rows, 32, lambda first, n=n: residual_back(pl.multiple_of(n * part_rows + first, 32)))
        dres_copies.append(share(dres_all)(n))
    advance(*right_units)
    links.settle(*back_copies)
    back_send[...] = ffn(theirs).astype(BF)

    def add_ffn(first):
        resid[...] += ffn(first)

    add_ffn(mine)
    advance(*down_units)
    for copy in dres_copies:
        copy.wait_recv()
    ffn_copy = links.start(back_send, back_recv, place.mate)

    def gate_back(shard, carry):
        grad = dot_t(dres_all[...], ow[shard])
        opened, norm = sz[shard].astype(F32), hn[shard].astype(F32)
        djoined[shard, 3] = (grad * norm * opened * (1.0 - opened)).astype(BF)
        inner = grad * opened
        dm[shard] = (rr[shard].astype(F32) * (inner - norm * head_mean(inner * norm))).astype(BF)
        return carry

    lax.fori_loop(0, 2, gate_back, 0)
    meets = []
    for shard in range(2):
        query = jnp.where(near, qp[shard].astype(F32), 0.0).astype(BF)
        meet_send[shard] = fold(dot(query.T, dm[shard]))
        meets.append(links.start(meet_send.at[shard], meet_recv.at[1 - shard], place.twin))

    def out_outer(shard, carry):
        grad_o[shard] = dot(gated[shard].T, dres_all[...]).astype(BF)
        return carry

    lax.fori_loop(0, 2, out_outer, 0)
    launch(*ow_units)
    gathers = (join_a, join_b, gather_o, gather_l, gather_r, gather_d)
    for unit in gathers:
        links.settle(*unit.sent)
    pl.semaphore_wait(free_sem, 1)

    def project_back(j, shard):
        def body(first):
            part_grad = dot(normed_t[pl.ds(first, 256), :], djoined[shard, j])
            lrw[shard, pl.ds(first, 256), j * local : (j + 1) * local] = part_grad.astype(BF)

        rows_loop(width, 256, body)

    project_back(3, 0)
    project_back(3, 1)
    launch(joined_units[3])
    step_all()

    def mix_back(shard):
        dq[...] = jnp.where(near & second_half, dot_t(dm[shard], unfold(state_recv[shard])), 0.0)
        dk[...] = jnp.zeros(dk.shape, F32)
        dv[...] = jnp.zeros(dv.shape, F32)

        def one(head, carry):
            for r in range(2):
                seen = (r + 1) * own
                at = slice(r * own, (r + 1) * own)
                grad_r, query_r = dm[shard, at, :], qp[shard, at, :]
                grad_h, query_h = only_head(grad_r, head), only_head(query_r, head)
                keys_h = only_head(kp[shard, :seen, :], head)
                vals_h = only_head(vl[shard, :seen, :], head)
                ds = dot_t(grad_r, vals_h).astype(BF) * mask[at, :seen]
                dq[at, :] += dot(ds, keys_h)
                st = dot_t(keys_h, query_r).astype(BF) * mask_t[:seen, at]
                dv[:seen, :] += dot(st, grad_h)
                dst = dot_t(vals_h, grad_r).astype(BF) * mask_t[:seen, at]
                dk[:seen, :] += dot(dst, query_h)
            return carry

        lax.fori_loop(0, local // HEAD, one, 0)

    for shard in (1, 0):
        mix_back(shard)
        meets[1 - shard].wait_recv()
        meet = unfold(meet_recv[shard])
        marks = near & first_half
        djoined[shard, 2] = (dv[...] + jnp.where(marks, dot(kp[shard], meet), 0.0)).astype(BF)
        from_meet = jnp.where(marks, dot_t(vl[shard], meet), 0.0)
        djoined[shard, 1] = ((dk[...] + from_meet) * sk[shard].astype(F32)).astype(BF)
        djoined[shard, 0] = (dq[...] * sq[shard].astype(F32)).astype(BF)
        for j in range(3):
            project_back(j, shard)
            launch(joined_units[j][shard])

    def normed_back(first):
        at = pl.ds(first, own)
        own_sum[...] = jnp.zeros(own_sum.shape, F32)

        def one(k, carry):
            own_sum[...] += dot_t(djoined[k // 4, lax.rem(k, 4), at, :], joined[k // 4, lax.rem(k, 4)])
            return carry

        lax.fori_loop(0, 8, one, 0)

    links.settle(*branch_copies)
    normed_back(theirs)
    trade_send[...] = own_sum[...].astype(BF)
    trade_copy = links.start(trade_send, trade_recv, place.mate)
    step_all(True)
    normed_back(mine)
    ffn_copy.wait_recv()
    links.settle(ffn_copy)

    def finish_out(first):
        at = pl.ds(first, 32)
        back_send[at, :] = (resid[at, :] + back_recv[at, :].astype(F32)).astype(BF)

    rows_loop(own, 32, finish_out)
    moves.start(back_send, block_out)
    step_all(True)
    trade_copy.wait_recv()
    links.settle(trade_copy)

    def finish_grad(first):
        at = pl.ds(first, 32)
        values = x_ref[at, :].astype(F32)
        scale = lax.rsqrt(jnp.mean(values * values, axis=-1, keepdims=True) + EPS)
        grad = own_sum[at, :] + trade_recv[at, :].astype(F32)
        gains[0, 1:2, :] += jnp.sum(grad * values * scale, axis=0, keepdims=True)
        weighted = grad * g1_ref[...]
        inner = jnp.mean(weighted * values, axis=-1, keepdims=True)
        trade_send[at, :] = (dres[at, :] + scale * weighted - values * (scale * scale * scale * inner)).astype(BF)

    rows_loop(own, 32, finish_grad)
    moves.start(trade_send, grad_out)

    first = 0
    for n, peers in enumerate((place.rows, place.columns)):
        copies = [links.start(gains.at[n], gains_recv.at[first + k], peer) for k, peer in enumerate(peers)]
        step_all(True)
        for copy in copies:
            copy.wait_recv()
        gains[n + 1] = gains[n] + jnp.sum(gains_recv[first : first + len(peers)], axis=0)
        first += len(peers)
    moves.start(gains.at[2], gains_out)
    while not all(unit.over() for unit in live):
        step_all(True)
    moves.finish()
    links.finish()


def widen_kernel(count, passed, *refs):
    sources, refs = refs[: count + passed], refs[count + passed :]
    targets, refs = refs[: count + passed], refs[count + passed :]
    total = count + passed
    narrow, wide, (in_sem, out_sem) = refs[:total], refs[total : total + count], refs[total + count :]
    loads = [pltpu.make_async_copy(sources[n], narrow[n], in_sem.at[n]) for n in range(total)]
    results = list(wide) + list(narrow[count:])
    stores = [pltpu.make_async_copy(results[n], targets[n], out_sem.at[n]) for n in range(total)]
    for copy in loads:
        copy.start()
    for n in range(count):
        loads[n].wait()

        def body(first, n=n):
            wide[n][pl.ds(first, 64), :] = narrow[n][pl.ds(first, 64), :].astype(F32)

        rows_loop(narrow[n].shape[0], 64, body)
        stores[n].start()
    for n in range(count, total):
        loads[n].wait()
        stores[n].start()
    for copy in stores:
        copy.wait()


def vmem(shape, dtype=BF):
    return pltpu.VMEM(shape, dtype)


def per_device(
    dp_size,
    inputs, segments, query_weight, key_weight, value_weight, gate_weight, out_weight, left_weight, right_weight,
    down_weight, norm_first, norm_second, cotangent,
):
    own, width = inputs.shape
    tokens = 2 * own
    local = query_weight.shape[1]
    hidden = left_weight.shape[1]
    pad = -(-hidden // 128) * 128
    bits = dp_size.bit_length() - 1
    extras = bits - PIECE_BITS
    shape = jax.ShapeDtypeStruct
    heads, state = (2, tokens, local), (2, local, local // 2)
    grads = [(hidden, width)] * 3 + [(local, width)] + [(width, local)] * 4

    def buffers(rows, columns, axis, first, shards=2):
        def cut(parts):
            return (shards, rows // parts, columns) if axis == 0 else (shards, rows, columns // parts)

        eighth = cut(1 << PIECE_BITS)
        kept = [vmem(cut(2 << k)) for k in range(first, PIECE_BITS)]
        return kept + [vmem(eighth[1:])]

    received = []
    for rows in (hidden // 2,) * 6 + (local // 2,) * 2:
        received += buffers(rows, width, 1, 0)
    for _ in range(3):
        away = buffers(width, local, 0, 1, 1)
        received += away + away[:-1]
    received += buffers(width, local, 0, 1)
    copies = 15 * (2 * PIECE_BITS + extras + 1) + 6 * (PIECE_BITS + 1) + dp_size + 20
    results = pl.pallas_call(
        functools.partial(layer_kernel, dp_size, extras, hidden, pad),
        out_shape=[shape(full, BF) for full in grads]
        + [shape((own, width), BF), shape((own, width), BF), shape((2, width), F32)],
        in_specs=[ANY, INNER] + [ANY] * 8 + [INNER, INNER, ANY],
        out_specs=[ANY] * 11,
        scratch_shapes=[
            vmem((own, width)), vmem((tokens, 1), F32), vmem((tokens, width)), vmem((width, tokens)),
            vmem((2, 4, width, local)), vmem((2, local, width)), vmem((2, 2 * hidden, width)),
            vmem((2, hidden, width)),
        ]
        + [vmem(heads)] * 9
        + [vmem((tokens, tokens))] * 2
        + [vmem(state)] * 4
        + [vmem((own, width))] * 4
        + [vmem((own, width), F32)] * 2
        + [
            vmem((tokens, width)), vmem((tokens, width)), vmem((2, tokens, 3 * pad)), vmem((own, width), F32),
            vmem(heads), vmem((2, 4, tokens, local)),
        ]
        + [vmem((tokens, local), F32)] * 3
        + [vmem((3, 2, width), F32), vmem((dp_size + 2, 2, width), F32)]
        + [vmem((2, hidden, width))] * 3
        + [vmem((2, local, width))]
        + received
        + [pltpu.SemaphoreType.DMA((copies,))] * 2
        + [
            pltpu.SemaphoreType.DMA((40,)), pltpu.SemaphoreType.REGULAR,
            pltpu.SemaphoreType.REGULAR((max(1, 15 * extras),)),
        ],
        compiler_params=pltpu.CompilerParams(collective_id=0, has_side_effects=True, vmem_limit_bytes=63 << 20),
    )(
        inputs, segments, query_weight, key_weight, value_weight, gate_weight, out_weight, left_weight.T,
        right_weight.T, down_weight, norm_first.reshape(1, -1), norm_second.reshape(1, -1), cotangent,
    )
    count, passed = len(grads), 3
    wide = pl.pallas_call(
        functools.partial(widen_kernel, count, passed),
        out_shape=[shape(full, F32) for full in grads] + [shape(r.shape, r.dtype) for r in results[count:]],
        in_specs=[ANY] * (count + passed),
        out_specs=[ANY] * (count + passed),
        scratch_shapes=[vmem(r.shape, r.dtype) for r in results]
        + [vmem(full, F32) for full in grads]
        + [pltpu.SemaphoreType.DMA((count + passed,))] * 2,
        compiler_params=pltpu.CompilerParams(vmem_limit_bytes=62 << 20),
    )(*results)
    down, left, right, out, query, key, value, gate, block, block_grad, gains = wide
    return (
        block, block_grad, query, key, value, gate, out, left.T, right.T, down, gains[1], gains[0],
    )


def solution(mesh):
    row, column = P("tensor", None), P(None, "tensor")
    tokens = P(("dp", "tensor"), None)
    return jax.shard_map(
        functools.partial(per_device, mesh.shape["dp"]),
        mesh=mesh,
        in_specs=(
            tokens, P("dp", None), column, column, column, column, row, column, column, row, P(), P(), tokens,
        ),
        out_specs=(tokens, tokens, column, column, column, column, row, column, column, row, P(), P()),
        check_vma=False,
    )
```

```python
import functools
import itertools

import jax
import jax.numpy as jnp
from jax import lax
from jax.experimental import pallas as pl
from jax.experimental.pallas import tpu as pltpu
from jax.sharding import PartitionSpec as P

EPS = 1e-05
HEAD = 64
BF = jnp.bfloat16
F32 = jnp.float32
MESH = pl.DeviceIdType.MESH
ANY = pl.BlockSpec(memory_space=pl.ANY)
INNER = pl.BlockSpec(memory_space=pltpu.VMEM)
PIECE_BITS = 3


def dot(a, b):
    return lax.dot_general(a, b, (((1,), (0,)), ((), ())), preferred_element_type=F32)


def dot_t(a, b):
    return lax.dot_general(a, b, (((1,), (1,)), ((), ())), preferred_element_type=F32)


class Place:
    def __init__(self, dp_size):
        self.i = lax.axis_index("dp")
        self.t = lax.axis_index("tensor")
        self.half = lax.rem(self.t, 2)
        self.pair = self.t // 2
        self.bits = dp_size.bit_length() - 1
        self.rows = [{"dp": lax.rem(self.i + k, dp_size)} for k in range(1, dp_size)]
        self.columns = [{"tensor": lax.rem(self.t + k, 4)} for k in range(1, 4)]
        self.mate = {"tensor": self.t + 1 - 2 * self.half}
        self.twin = {"tensor": self.t + 2 - 4 * self.pair}

    def bit(self, b):
        return lax.rem(self.i // (1 << b), 2)

    def over(self, b):
        return {"dp": self.i + (1 << b) * (1 - 2 * self.bit(b))}

    def greet(self):
        barrier = pltpu.get_barrier_semaphore()
        peers = self.rows + self.columns
        for peer in peers:
            pl.semaphore_signal(barrier, inc=1, device_id=peer, device_id_type=MESH)

        def all_here():
            pl.semaphore_wait(barrier, len(peers))

        return all_here


class Links:
    def __init__(self, send_sem, recv_sem):
        self.send_sem, self.recv_sem, self.count, self.open = send_sem, recv_sem, 0, []

    def start(self, source, target, peer):
        copy = pltpu.make_async_remote_copy(
            src_ref=source,
            dst_ref=target,
            send_sem=self.send_sem.at[self.count],
            recv_sem=self.recv_sem.at[self.count],
            device_id=peer,
            device_id_type=MESH,
        )
        self.count += 1
        copy.start()
        self.open.append(copy)
        return copy

    def settle(self, *copies):
        for copy in copies:
            copy.wait_send()
        self.open = [other for other in self.open if all(other is not copy for copy in copies)]

    def finish(self):
        self.settle(*self.open)


class Moves:
    def __init__(self, sem):
        self.sem, self.count, self.open = sem, 0, []

    def start(self, source, target):
        copy = pltpu.make_async_copy(source, target, self.sem.at[self.count])
        self.count += 1
        copy.start()
        self.open.append(copy)
        return copy

    def wait(self, copy):
        copy.wait()
        self.open = [other for other in self.open if other is not copy]

    def finish(self):
        for copy in list(self.open):
            self.wait(copy)


def part(ref, lead, axis, first, count):
    window = pl.ds(first, count)
    return ref.at[lead + ((window, slice(None)) if axis == 0 else (slice(None), window))]


def piece_of(place, order):
    total = 0
    for b in order:
        total = 2 * total + place.bit(b)
    return total


class Gather:
    def __init__(self, place, links, ref, lead, axis, order):
        self.place, self.links, self.ref, self.lead, self.axis, self.order = place, links, ref, lead, axis, order
        self.size = ref.shape[len(ref.shape) - 2 + axis] // (1 << len(order))
        self.piece = piece_of(place, order)
        self.copy, self.stage, self.sent = None, 0, []

    def block(self, shard, width):
        first = (self.piece // width) * (width * self.size)
        return part(self.ref, (shard,) + self.lead, self.axis, pl.multiple_of(first, self.size), width * self.size)

    def begin(self):
        self.copy = self.links.start(self.block(0, 1), self.block(1, 1), self.place.twin)
        self.sent.append(self.copy)

    def advance(self):
        self.copy.wait_recv()
        if self.stage < len(self.order):
            block = self.block(1, 1 << self.stage)
            self.copy = self.links.start(block, block, self.place.over(self.order[-1 - self.stage]))
            self.sent.append(self.copy)
        self.stage += 1


def rows_loop(count, size, body):
    def step(k, carry):
        body(pl.multiple_of(k * size, size))
        return carry

    lax.fori_loop(0, count // size, step, 0)


def softplus_and_slope(values):
    tail = jnp.exp(-jnp.abs(values))
    soft = jnp.maximum(values, 0.0) + jnp.log1p(tail)
    slope = jnp.where(values >= 0, 1.0, tail) / (1.0 + tail)
    return soft, slope


def sigmoid(values):
    tail = jnp.exp(-jnp.abs(values))
    return jnp.where(values >= 0, 1.0, tail) / (1.0 + tail)


def head_of(shape, axis):
    return lax.broadcasted_iota(jnp.int32, shape, axis) // HEAD


def same_head(width):
    return head_of((width, width), 0) == head_of((width, width), 1)


def head_mean(values):
    ones = jnp.where(same_head(values.shape[-1]), 1.0 / HEAD, 0.0).astype(BF)
    return dot(values.astype(BF), ones)


def fold(state):
    width = state.shape[-1]
    state = jnp.where(same_head(width), state, 0.0)
    return (state[:, : width // 2] + state[:, width // 2 :]).astype(BF)


def unfold(state):
    both = jnp.concatenate((state, state), axis=1)
    return jnp.where(same_head(both.shape[-1]), both, jnp.zeros_like(both))


def only_head(values, head):
    return jnp.where(head_of(values.shape, 1) == head, values, jnp.zeros_like(values))


class Reduce:
    def __init__(self, place, links, moves, grad, axis, order, halves, credits, twin_recv, out, other=None):
        self.place, self.links, self.moves = place, links, moves
        self.grad, self.axis, self.order = grad, axis, order
        self.halves, self.twin_recv, self.out = halves, twin_recv, out
        self.extra = credits
        self.size = grad.shape[1 + axis] // (1 << len(order))
        self.piece = piece_of(place, order)
        self.stage, self.copy, self.local = 0, None, None
        self.other, self.ends = other, out is None
        self.steps = len(order) + len(self.extra) + (0 if self.ends else 1 + len(order))

    def first_of(self, width):
        return pl.multiple_of((self.piece // width) * (width * self.size), self.size)

    def grad_part(self, lead, first, width):
        return part(self.grad, lead, self.axis, pl.multiple_of(first, self.size), width * self.size)

    def out_part(self, width):
        return part(self.out, (), self.axis, self.first_of(width), width * self.size)

    def begin(self):
        shards, folds = (slice(None),), len(self.order)
        k = self.stage
        if k < folds:
            width = 1 << (folds - 1 - k)
            bit = self.place.bit(self.order[k])
            away = self.first_of(width) + (1 - 2 * bit) * (width * self.size)
            self.copy = self.links.start(
                self.grad_part(shards, away, width), self.halves[k], self.place.over(self.order[k])
            )
            return
        k -= folds
        if k < len(self.extra):
            peer = self.place.over(folds + k)
            pl.semaphore_signal(self.extra[k], inc=1, device_id=peer, device_id_type=MESH)
            pl.semaphore_wait(self.extra[k], 1)
            source = self.grad_part(shards, self.first_of(1), 1)
            self.copy = self.links.start(source, self.halves[-1], peer)
            return
        k -= len(self.extra)
        if k == 0:
            if self.other is not None:
                while not self.other.over():
                    self.other.advance()
                self.copy = self.other.copy
            else:
                source = self.grad_part((self.grad.shape[0] - 1,), self.first_of(1), 1)
                self.copy = self.links.start(source, self.twin_recv, self.place.twin)
            return
        k -= 1
        block = self.out_part(1 << k)
        source = self.grad_part((0,), self.first_of(1), 1) if k == 0 else block
        self.copy = self.links.start(source, block, self.place.over(self.order[folds - 1 - k]))
        if k == 0:
            self.local = self.moves.start(source, block)

    def add(self, recv, width):
        rows, chunk = recv.shape[-2], 32
        first = self.first_of(width)

        def body(at):
            for shard in range(recv.shape[0] if len(recv.shape) == 3 else 1):
                if self.axis == 0:
                    where = (shard, pl.ds(pl.multiple_of(first + at, chunk), chunk), slice(None))
                else:
                    where = (shard, pl.ds(at, chunk), pl.ds(first, width * self.size))
                came = recv[(shard,) * (len(recv.shape) - 2) + (pl.ds(at, chunk), slice(None))]
                self.grad[where] = self.grad[where] + came

        rows_loop(rows, chunk, body)

    def advance(self):
        if self.stage >= self.steps:
            return
        folds = len(self.order)
        self.copy.wait_recv()
        k = self.stage
        if k < folds:
            self.add(self.halves[k], 1 << (folds - 1 - k))
        elif k < folds + len(self.extra):
            self.links.settle(self.copy)
            self.add(self.halves[-1], 1)
        elif k == folds + len(self.extra):
            self.add(self.twin_recv, 1)
        elif self.local is not None:
            self.moves.wait(self.local)
            self.local = None
        self.stage += 1
        if self.stage < self.steps or self.ends:
            self.begin()

    def over(self):
        return self.stage >= self.steps


def marks_of(place, segr_ref, segc, tokens):
    offset = pl.multiple_of(place.pair * tokens, tokens)
    across = segr_ref[:, pl.ds(offset, tokens)].astype(F32)
    segc[...] = jnp.broadcast_to(across, (8, tokens)).T[:, :1]
    return across, segr_ref[:, tokens - 1 : tokens].astype(F32)


def doc_mask(across, segc, mask_ref, tokens, later):
    def body(first):
        at = first + lax.broadcasted_iota(jnp.int32, (64, tokens), 0)
        col = lax.broadcasted_iota(jnp.int32, (64, tokens), 1)
        order = col >= at if later else col <= at
        same = segc[pl.ds(first, 64), :] == across
        mask_ref[pl.ds(first, 64), :] = jnp.where(same & order, 1.0, 0.0).astype(BF)

    rows_loop(tokens, 64, body)


def layer_kernel(
    dp_size, extras, hidden, pad,
    x_hbm, segr_ref, wq, wk, wv, wz, wo, wl, wr, wd, g1_ref, g2_ref, cot_hbm,
    down_out, left_out, right_out, ow_out, query_out, key_out, value_out, gate_out, block_out, grad_out, gains_out,
    x_ref, segc, normed, normed_t, joined, ow, lrw, dw, qp, kp, vl, sq, sk, hn, rr, sz, gated, mask, mask_t,
    state_send, state_recv, meet_send, meet_recv, trade_send, trade_recv, back_send, back_recv,
    resid, own_sum, second, cot, hid, dres, dm, djoined, dq, dk, dv, gains, gains_recv,
    grad_d, grad_l, grad_r, grad_o,
    *rest,
):
    *received, send_sem, recv_sem, move_sem, free_sem, credit_sem = rest
    received, tickets = list(received), itertools.count()
    place = Place(dp_size)
    links, moves = Links(send_sem, recv_sem), Moves(move_sem)
    own, width = x_ref.shape
    tokens = 2 * own
    local = qp.shape[-1]
    mine = pl.multiple_of(place.half * own, own)
    theirs = pl.multiple_of((1 - place.half) * own, own)
    lw, rw = lrw.at[:, :hidden, :], lrw.at[:, hidden:, :]
    product, dleft, dright = (slice(n * pad, n * pad + hidden) for n in range(3))
    dres_all = normed

    all_here = place.greet()
    x_in = moves.start(x_hbm, x_ref)
    joined_in = [moves.start(w, joined.at[0, j]) for j, w in enumerate((wq, wk, wv, wz))]
    ow_in = moves.start(wo, ow.at[0])
    ffn_in = [moves.start(w, v.at[0]) for w, v in ((wl, lw), (wr, rw), (wd, dw))]
    cot_in = moves.start(cot_hbm, cot.at[pl.ds(mine, own), :])
    moves.wait(x_in)

    def first_norm(first):
        values = x_ref[pl.ds(first, 32), :].astype(F32)
        scale = lax.rsqrt(jnp.mean(values * values, axis=-1, keepdims=True) + EPS)
        normed[pl.ds(mine + first, 32), :] = (values * scale * g1_ref[...]).astype(BF)

    rows_loop(own, 32, first_norm)
    for copy in joined_in:
        moves.wait(copy)
    all_here()
    block = normed.at[pl.ds(mine, own), :]
    normed_copy = links.start(block, block, place.mate)
    first_order, second_order = (0, 1, 2), (0, 2, 1)
    join_a = Gather(place, links, joined, (pl.ds(0, 2),), 0, first_order)
    join_b = Gather(place, links, joined, (pl.ds(2, 2),), 0, second_order)
    gather_o = Gather(place, links, ow, (), 1, second_order)
    gather_l = Gather(place, links, lw, (), 1, first_order)
    gather_r = Gather(place, links, rw, (), 1, second_order)
    gather_d = Gather(place, links, dw, (), 1, first_order)
    join_a.begin()
    join_b.begin()
    moves.wait(ow_in)
    gather_o.begin()

    def advance(*units):
        for unit in units:
            unit.advance()

    def project(shard, first, which):
        rows = normed[pl.ds(first, own), :]
        at = pl.ds(first, own)
        for j in which:
            raw = dot(rows, joined[shard, j])
            if j == 2:
                vl[shard, at, :] = raw.astype(BF)
            elif j == 3:
                sz[shard, at, :] = sigmoid(raw).astype(BF)
            else:
                soft, slope = softplus_and_slope(raw)
                (qp, kp)[j][shard, at, :] = soft.astype(BF)
                (sq, sk)[j][shard, at, :] = slope.astype(BF)

    project(0, mine, (1, 2, 0, 3))
    across, last = marks_of(place, segr_ref, segc, tokens)
    doc_mask(across, segc, mask, tokens, False)
    near = segc[...] == last
    edge = segc[...] == segc[own - 1 : own, :]
    halves_of = (slice(0, own), slice(own, tokens))
    state_copy = [None, None]

    def marked(values, marks):
        return jnp.where(marks, values.astype(F32), 0.0).astype(BF)

    def blocks(left, right):
        return jnp.where(same_head(local), dot(left.T, right), 0.0).astype(BF)

    def middle_state(shard):
        return blocks(marked(kp[shard, :own, :], edge[:own]), vl[shard, :own, :])

    def send_state(shard):
        keys = jnp.where(near, kp[shard].astype(F32), 0.0).astype(BF)
        state_send[shard] = fold(dot(keys.T, vl[shard]))
        state_copy[shard] = links.start(state_send.at[shard], state_recv.at[1 - shard], place.twin)

    attention = (join_a, join_b, gather_o)
    normed_copy.wait_recv()
    advance(*attention)
    for copy in ffn_in:
        moves.wait(copy)
    gather_l.begin()
    gather_r.begin()
    gather_d.begin()
    project(0, theirs, (1, 2))
    send_state(0)
    advance(*attention)
    moves.wait(cot_in)
    cot_block = cot.at[pl.ds(mine, own), :]
    cot_copy = links.start(cot_block, cot_block, place.mate)
    project(0, theirs, (0, 3))

    def mix(shard, total):
        def one(head, carry):
            for at in halves_of:
                raw = dot_t(only_head(qp[shard, at, :], head), kp[shard, at, :])
                scores = raw.astype(BF) * mask[at, at]
                total[at, :] += dot(scores, only_head(vl[shard, at, :], head))
            return carry

        total[:own, :] = jnp.zeros((own, local), F32)
        total[own:, :] = dot(marked(qp[shard, own:, :], edge[own:]), middle_state(shard))
        lax.fori_loop(0, local // HEAD, one, 0)

    first_half, second_half = place.pair == 0, place.pair == 1

    def open_gate(shard, total):
        state_copy[1 - shard].wait_recv()
        query = jnp.where(near & second_half, qp[shard].astype(F32), 0.0).astype(BF)
        mixed = total[...] + dot(query, unfold(state_recv[shard]))
        scale = lax.rsqrt(head_mean(mixed * mixed) + EPS)
        norm = mixed * scale
        rr[shard] = scale.astype(BF)
        hn[shard] = norm.astype(BF)
        gated[shard] = (norm * sz[shard].astype(F32)).astype(BF)

    mix(0, dk)
    advance(*attention)
    advance(gather_l)
    advance(*attention)
    for first in (mine, theirs):
        project(1, first, (1, 2))
    send_state(1)
    advance(gather_r)
    for first in (mine, theirs):
        project(1, first, (0, 3))
    advance(gather_l)
    mix(1, dq)
    advance(gather_r)
    open_gate(1, dq)
    open_gate(0, dk)

    def branch(first, count=own):
        at = pl.ds(first, count)
        return dot(gated[0, at, :], ow[0]) + dot(gated[1, at, :], ow[1])

    part_rows = own // 2
    parts = [slice(0, part_rows), slice(part_rows, own)]

    def halved(partial_sum, send, recv):
        copies = []
        for rows in parts:
            send[rows, :] = partial_sum(pl.multiple_of(theirs + rows.start, part_rows), part_rows).astype(BF)
            copies.append(links.start(send.at[rows, :], recv.at[rows, :], place.mate))
        return copies

    def share(ref):
        def after(n):
            block = ref.at[pl.ds(pl.multiple_of(mine + n * part_rows, part_rows), part_rows), :]
            return links.start(block, block, place.mate)

        return after

    branch_copies = halved(branch, trade_send, trade_recv)
    advance(gather_d, gather_l)
    own_sum[...] = branch(mine)
    advance(gather_r, gather_d)
    for c in range(0, width, 256):
        normed_t[c : c + 256, :] = normed[:, c : c + 256].T
    doc_mask(across, segc, mask_t, tokens, True)
    advance(gather_d, gather_l, gather_r)

    def second_norm(first):
        at = pl.ds(first, 32)
        values = x_ref[at, :].astype(F32) + own_sum[at, :] + trade_recv[at, :].astype(F32)
        resid[at, :] = values
        scale = lax.rsqrt(jnp.mean(values * values, axis=-1, keepdims=True) + EPS)
        second[pl.ds(mine + first, 32), :] = (values * scale * g2_ref[...]).astype(BF)

    second_copies = []
    for n, copy in enumerate(branch_copies):
        copy.wait_recv()
        rows_loop(part_rows, 32, lambda first, n=n: second_norm(pl.multiple_of(n * part_rows + first, 32)))
        second_copies.append(share(second)(n))
    cot_copy.wait_recv()
    advance(gather_d)

    def hidden_grad(first):
        at = pl.ds(first, own)

        def one(shard, carry):
            hid[shard, at, dleft] = dot_t(cot[at, :], dw[shard]).astype(BF)
            return carry

        lax.fori_loop(0, 2, one, 0)

    def unit_rows(first):
        at = pl.ds(first, own)

        def one(shard, carry):
            left = dot_t(second[at, :], lw[shard])
            right = dot_t(second[at, :], rw[shard])
            grad = hid[shard, at, dleft].astype(F32)
            hid[shard, at, product] = (left * right).astype(BF)
            hid[shard, at, dleft] = (grad * right).astype(BF)
            hid[shard, at, dright] = (grad * left).astype(BF)
            return carry

        lax.fori_loop(0, 2, one, 0)

    hidden_grad(mine)
    unit_rows(mine)
    hidden_grad(theirs)
    for copy in second_copies:
        copy.wait_recv()
    unit_rows(theirs)

    def back(first, count=own):
        at = pl.ds(first, count)
        return (
            dot(hid[0, at, dleft], lw[0])
            + dot(hid[0, at, dright], rw[0])
            + dot(hid[1, at, dleft], lw[1])
            + dot(hid[1, at, dright], rw[1])
        )

    def ffn(first):
        at = pl.ds(first, own)
        return dot(hid[0, at, product], dw[0]) + dot(hid[1, at, product], dw[1])

    back_copies = halved(back, back_send, back_recv)
    own_sum[...] = back(mine)

    def make_unit(grad, axis, order, out, first_half_ref=None, twin_recv=None, other=None):
        folds = len(order)
        halves = [received.pop(0) for _ in range(folds - (first_half_ref is not None))]
        if first_half_ref is not None:
            halves = [first_half_ref] + halves
        credits = [credit_sem.at[next(tickets)] for _ in range(extras)]
        twin_recv = received.pop(0) if twin_recv is None else twin_recv
        return Reduce(place, links, moves, grad, axis, order, halves, credits, twin_recv, out, other)

    def split_units(grad, out):
        rows = grad.shape[1] // 2
        return [
            make_unit(grad.at[:, n * rows : (n + 1) * rows, :], 1, order, out.at[n * rows : (n + 1) * rows, :])
            for n, order in enumerate((first_order, second_order))
        ]

    down_units, left_units, right_units = (
        split_units(g, o) for g, o in ((grad_d, down_out), (grad_l, left_out), (grad_r, right_out))
    )
    ow_units = split_units(grad_o, ow_out)
    joined_units = []
    for j, (order, out) in enumerate(
        zip((first_order, second_order, first_order, second_order), (query_out, key_out, value_out, gate_out))
    ):
        columns = slice(j * local, (j + 1) * local)
        grad, landing = lrw.at[:, :width, columns], hid.at[:, : width // 2, columns]
        if j == 3:
            joined_units.append(make_unit(grad, 0, order, out, landing))
            continue
        away = make_unit(grad.at[1:2], 0, order, None, landing.at[1:2])
        near_unit = make_unit(grad.at[0:1], 0, order, out, landing.at[0:1], away.twin_recv, away)
        joined_units.append((near_unit, away))
    live = []

    def launch(*units):
        for unit in units:
            unit.begin()
            live.append(unit)

    def step_all(late=False):
        for unit in reversed(live) if late else live:
            unit.advance()

    def hidden_outer(units, grad, left, right):
        def one(shard, carry):
            for c in range(0, hidden, 256):
                high = min(c + 256, hidden)
                grad[shard, c:high, :] = dot(hid[shard, :, left.start + c : left.start + high].T, right[...]).astype(BF)
            return carry

        lax.fori_loop(0, 2, one, 0)
        launch(*units)

    hidden_outer(down_units, grad_d, product, cot)
    hidden_outer(left_units, grad_l, dleft, second)
    advance(*down_units)
    hidden_outer(right_units, grad_r, dright, second)
    advance(*left_units)
    pl.semaphore_signal(free_sem, inc=1, device_id=place.over(0), device_id_type=MESH)
    gains[0] = jnp.zeros(gains.shape[1:], F32)

    def residual_back(first):
        at = pl.ds(first, 32)
        values = resid[at, :]
        scale = lax.rsqrt(jnp.mean(values * values, axis=-1, keepdims=True) + EPS)
        grad = own_sum[at, :] + back_recv[at, :].astype(F32)
        gains[0, 0:1, :] += jnp.sum(grad * values * scale, axis=0, keepdims=True)
        weighted = grad * g2_ref[...]
        inner = jnp.mean(weighted * values, axis=-1, keepdims=True)
        upstream = cot[pl.ds(mine + first, 32), :].astype(F32)
        total = upstream + scale * weighted - values * (scale * scale * scale * inner)
        dres[at, :] = total
        dres_all[pl.ds(mine + first, 32), :] = total.astype(BF)

    links.settle(normed_copy)
    dres_copies = []
    for n, copy in enumerate(back_copies):
        copy.wait_recv()
        rows_loop(part_rows, 32, lambda first, n=n: residual_back(pl.multiple_of(n * part_rows + first, 32)))
        dres_copies.append(share(dres_all)(n))
    advance(*right_units)
    links.settle(*back_copies)
    back_send[...] = ffn(theirs).astype(BF)

    def add_ffn(first):
        resid[...] += ffn(first)

    add_ffn(mine)
    advance(*down_units)
    for copy in dres_copies:
        copy.wait_recv()
    ffn_copy = links.start(back_send, back_recv, place.mate)

    def gate_back(shard, carry):
        grad = dot_t(dres_all[...], ow[shard])
        opened, norm = sz[shard].astype(F32), hn[shard].astype(F32)
        djoined[shard, 3] = (grad * norm * opened * (1.0 - opened)).astype(BF)
        inner = grad * opened
        dm[shard] = (rr[shard].astype(F32) * (inner - norm * head_mean(inner * norm))).astype(BF)
        return carry

    lax.fori_loop(0, 2, gate_back, 0)
    meets = []
    for shard in range(2):
        query = jnp.where(near, qp[shard].astype(F32), 0.0).astype(BF)
        meet_send[shard] = fold(dot(query.T, dm[shard]))
        meets.append(links.start(meet_send.at[shard], meet_recv.at[1 - shard], place.twin))

    def out_outer(shard, carry):
        grad_o[shard] = dot(gated[shard].T, dres_all[...]).astype(BF)
        return carry

    lax.fori_loop(0, 2, out_outer, 0)
    launch(*ow_units)
    gathers = (join_a, join_b, gather_o, gather_l, gather_r, gather_d)
    for unit in gathers:
        links.settle(*unit.sent)
    pl.semaphore_wait(free_sem, 1)

    def project_back(j, shard):
        def body(first):
            part_grad = dot(normed_t[pl.ds(first, 256), :], djoined[shard, j])
            lrw[shard, pl.ds(first, 256), j * local : (j + 1) * local] = part_grad.astype(BF)

        rows_loop(width, 256, body)

    project_back(3, 0)
    project_back(3, 1)
    launch(joined_units[3])
    step_all()

    def mix_back(shard):
        dq[...] = jnp.where(near & second_half, dot_t(dm[shard], unfold(state_recv[shard])), 0.0)
        dq[own:, :] += jnp.where(edge[own:], dot_t(dm[shard, own:, :], middle_state(shard)), 0.0)
        meeting = blocks(marked(qp[shard, own:, :], edge[own:]), dm[shard, own:, :])
        dk[:own, :] = jnp.where(edge[:own], dot_t(vl[shard, :own, :], meeting), 0.0)
        dv[:own, :] = jnp.where(edge[:own], dot(kp[shard, :own, :], meeting), 0.0)
        dk[own:, :] = jnp.zeros((own, local), F32)
        dv[own:, :] = jnp.zeros((own, local), F32)

        def one(head, carry):
            for at in halves_of:
                grad_r, query_r = dm[shard, at, :], qp[shard, at, :]
                grad_h, query_h = only_head(grad_r, head), only_head(query_r, head)
                keys_h = only_head(kp[shard, at, :], head)
                vals_h = only_head(vl[shard, at, :], head)
                ds = dot_t(grad_r, vals_h).astype(BF) * mask[at, at]
                dq[at, :] += dot(ds, keys_h)
                st = dot_t(keys_h, query_r).astype(BF) * mask_t[at, at]
                dv[at, :] += dot(st, grad_h)
                dst = dot_t(vals_h, grad_r).astype(BF) * mask_t[at, at]
                dk[at, :] += dot(dst, query_h)
            return carry

        lax.fori_loop(0, local // HEAD, one, 0)

    for shard in (1, 0):
        mix_back(shard)
        meets[1 - shard].wait_recv()
        meet = unfold(meet_recv[shard])
        marks = near & first_half
        djoined[shard, 2] = (dv[...] + jnp.where(marks, dot(kp[shard], meet), 0.0)).astype(BF)
        from_meet = jnp.where(marks, dot_t(vl[shard], meet), 0.0)
        djoined[shard, 1] = ((dk[...] + from_meet) * sk[shard].astype(F32)).astype(BF)
        djoined[shard, 0] = (dq[...] * sq[shard].astype(F32)).astype(BF)
        for j in range(3):
            project_back(j, shard)
            launch(joined_units[j][shard])

    def normed_back(first):
        at = pl.ds(first, own)
        own_sum[...] = jnp.zeros(own_sum.shape, F32)

        def one(k, carry):
            own_sum[...] += dot_t(djoined[k // 4, lax.rem(k, 4), at, :], joined[k // 4, lax.rem(k, 4)])
            return carry

        lax.fori_loop(0, 8, one, 0)

    links.settle(*branch_copies)
    normed_back(theirs)
    trade_send[...] = own_sum[...].astype(BF)
    trade_copy = links.start(trade_send, trade_recv, place.mate)
    step_all(True)
    normed_back(mine)
    ffn_copy.wait_recv()
    links.settle(ffn_copy)

    def finish_out(first):
        at = pl.ds(first, 32)
        back_send[at, :] = (resid[at, :] + back_recv[at, :].astype(F32)).astype(BF)

    rows_loop(own, 32, finish_out)
    moves.start(back_send, block_out)
    step_all(True)
    trade_copy.wait_recv()
    links.settle(trade_copy)

    def finish_grad(first):
        at = pl.ds(first, 32)
        values = x_ref[at, :].astype(F32)
        scale = lax.rsqrt(jnp.mean(values * values, axis=-1, keepdims=True) + EPS)
        grad = own_sum[at, :] + trade_recv[at, :].astype(F32)
        gains[0, 1:2, :] += jnp.sum(grad * values * scale, axis=0, keepdims=True)
        weighted = grad * g1_ref[...]
        inner = jnp.mean(weighted * values, axis=-1, keepdims=True)
        trade_send[at, :] = (dres[at, :] + scale * weighted - values * (scale * scale * scale * inner)).astype(BF)

    rows_loop(own, 32, finish_grad)
    moves.start(trade_send, grad_out)

    first = 0
    for n, peers in enumerate((place.rows, place.columns)):
        copies = [links.start(gains.at[n], gains_recv.at[first + k], peer) for k, peer in enumerate(peers)]
        step_all(True)
        for copy in copies:
            copy.wait_recv()
        gains[n + 1] = gains[n] + jnp.sum(gains_recv[first : first + len(peers)], axis=0)
        first += len(peers)
    moves.start(gains.at[2], gains_out)
    while not all(unit.over() for unit in live):
        step_all(True)
    moves.finish()
    links.finish()


def widen_kernel(count, passed, *refs):
    sources, refs = refs[: count + passed], refs[count + passed :]
    targets, refs = refs[: count + passed], refs[count + passed :]
    total = count + passed
    narrow, wide, (in_sem, out_sem) = refs[:total], refs[total : total + count], refs[total + count :]
    loads = [pltpu.make_async_copy(sources[n], narrow[n], in_sem.at[n]) for n in range(total)]
    results = list(wide) + list(narrow[count:])
    stores = [pltpu.make_async_copy(results[n], targets[n], out_sem.at[n]) for n in range(total)]
    for copy in loads:
        copy.start()
    for n in range(count):
        loads[n].wait()

        def body(first, n=n):
            wide[n][pl.ds(first, 64), :] = narrow[n][pl.ds(first, 64), :].astype(F32)

        rows_loop(narrow[n].shape[0], 64, body)
        stores[n].start()
    for n in range(count, total):
        loads[n].wait()
        stores[n].start()
    for copy in stores:
        copy.wait()


def vmem(shape, dtype=BF):
    return pltpu.VMEM(shape, dtype)


def per_device(
    dp_size,
    inputs, segments, query_weight, key_weight, value_weight, gate_weight, out_weight, left_weight, right_weight,
    down_weight, norm_first, norm_second, cotangent,
):
    own, width = inputs.shape
    tokens = 2 * own
    local = query_weight.shape[1]
    hidden = left_weight.shape[1]
    pad = -(-hidden // 128) * 128
    bits = dp_size.bit_length() - 1
    extras = bits - PIECE_BITS
    shape = jax.ShapeDtypeStruct
    heads, state = (2, tokens, local), (2, local, local // 2)
    grads = [(hidden, width)] * 3 + [(local, width)] + [(width, local)] * 4

    def buffers(rows, columns, axis, first, shards=2):
        def cut(parts):
            return (shards, rows // parts, columns) if axis == 0 else (shards, rows, columns // parts)

        eighth = cut(1 << PIECE_BITS)
        kept = [vmem(cut(2 << k)) for k in range(first, PIECE_BITS)]
        return kept + [vmem(eighth[1:])]

    received = []
    for rows in (hidden // 2,) * 6 + (local // 2,) * 2:
        received += buffers(rows, width, 1, 0)
    for _ in range(3):
        away = buffers(width, local, 0, 1, 1)
        received += away + away[:-1]
    received += buffers(width, local, 0, 1)
    copies = 15 * (2 * PIECE_BITS + extras + 1) + 6 * (PIECE_BITS + 1) + dp_size + 20
    results = pl.pallas_call(
        functools.partial(layer_kernel, dp_size, extras, hidden, pad),
        out_shape=[shape(full, BF) for full in grads]
        + [shape((own, width), BF), shape((own, width), BF), shape((2, width), F32)],
        in_specs=[ANY, INNER] + [ANY] * 8 + [INNER, INNER, ANY],
        out_specs=[ANY] * 11,
        scratch_shapes=[
            vmem((own, width)), vmem((tokens, 1), F32), vmem((tokens, width)), vmem((width, tokens)),
            vmem((2, 4, width, local)), vmem((2, local, width)), vmem((2, 2 * hidden, width)),
            vmem((2, hidden, width)),
        ]
        + [vmem(heads)] * 9
        + [vmem((tokens, tokens))] * 2
        + [vmem(state)] * 4
        + [vmem((own, width))] * 4
        + [vmem((own, width), F32)] * 2
        + [
            vmem((tokens, width)), vmem((tokens, width)), vmem((2, tokens, 3 * pad)), vmem((own, width), F32),
            vmem(heads), vmem((2, 4, tokens, local)),
        ]
        + [vmem((tokens, local), F32)] * 3
        + [vmem((3, 2, width), F32), vmem((dp_size + 2, 2, width), F32)]
        + [vmem((2, hidden, width))] * 3
        + [vmem((2, local, width))]
        + received
        + [pltpu.SemaphoreType.DMA((copies,))] * 2
        + [
            pltpu.SemaphoreType.DMA((40,)), pltpu.SemaphoreType.REGULAR,
            pltpu.SemaphoreType.REGULAR((max(1, 15 * extras),)),
        ],
        compiler_params=pltpu.CompilerParams(collective_id=0, has_side_effects=True, vmem_limit_bytes=63 << 20),
    )(
        inputs, segments, query_weight, key_weight, value_weight, gate_weight, out_weight, left_weight.T,
        right_weight.T, down_weight, norm_first.reshape(1, -1), norm_second.reshape(1, -1), cotangent,
    )
    count, passed = len(grads), 3
    wide = pl.pallas_call(
        functools.partial(widen_kernel, count, passed),
        out_shape=[shape(full, F32) for full in grads] + [shape(r.shape, r.dtype) for r in results[count:]],
        in_specs=[ANY] * (count + passed),
        out_specs=[ANY] * (count + passed),
        scratch_shapes=[vmem(r.shape, r.dtype) for r in results]
        + [vmem(full, F32) for full in grads]
        + [pltpu.SemaphoreType.DMA((count + passed,))] * 2,
        compiler_params=pltpu.CompilerParams(vmem_limit_bytes=62 << 20),
    )(*results)
    down, left, right, out, query, key, value, gate, block, block_grad, gains = wide
    return (
        block, block_grad, query, key, value, gate, out, left.T, right.T, down, gains[1], gains[0],
    )


def solution(mesh):
    row, column = P("tensor", None), P(None, "tensor")
    tokens = P(("dp", "tensor"), None)
    return jax.shard_map(
        functools.partial(per_device, mesh.shape["dp"]),
        mesh=mesh,
        in_specs=(
            tokens, P("dp", None), column, column, column, column, row, column, column, row, P(), P(), tokens,
        ),
        out_specs=(tokens, tokens, column, column, column, column, row, column, column, row, P(), P()),
        check_vma=False,
    )
```

```python
import functools
import itertools

import jax
import jax.numpy as jnp
from jax import lax
from jax.experimental import pallas as pl
from jax.experimental.pallas import tpu as pltpu
from jax.sharding import PartitionSpec as P

EPS = 1e-05
HEAD = 64
BF = jnp.bfloat16
F32 = jnp.float32
MESH = pl.DeviceIdType.MESH
ANY = pl.BlockSpec(memory_space=pl.ANY)
INNER = pl.BlockSpec(memory_space=pltpu.VMEM)
PIECE_BITS = 3


def dot(a, b):
    return lax.dot_general(a, b, (((1,), (0,)), ((), ())), preferred_element_type=F32)


def dot_t(a, b):
    return lax.dot_general(a, b, (((1,), (1,)), ((), ())), preferred_element_type=F32)


class Place:
    def __init__(self, dp_size):
        self.i = lax.axis_index("dp")
        self.t = lax.axis_index("tensor")
        self.half = lax.rem(self.t, 2)
        self.pair = self.t // 2
        self.bits = dp_size.bit_length() - 1
        self.rows = [{"dp": lax.rem(self.i + k, dp_size)} for k in range(1, dp_size)]
        self.columns = [{"tensor": lax.rem(self.t + k, 4)} for k in range(1, 4)]
        self.mate = {"tensor": self.t + 1 - 2 * self.half}
        self.twin = {"tensor": self.t + 2 - 4 * self.pair}

    def bit(self, b):
        return lax.rem(self.i // (1 << b), 2)

    def over(self, b):
        return {"dp": self.i + (1 << b) * (1 - 2 * self.bit(b))}

    def greet(self):
        barrier = pltpu.get_barrier_semaphore()
        peers = self.rows + self.columns
        for peer in peers:
            pl.semaphore_signal(barrier, inc=1, device_id=peer, device_id_type=MESH)

        def all_here():
            pl.semaphore_wait(barrier, len(peers))

        return all_here


class Links:
    def __init__(self, send_sem, recv_sem):
        self.send_sem, self.recv_sem, self.count, self.open = send_sem, recv_sem, 0, []

    def start(self, source, target, peer):
        copy = pltpu.make_async_remote_copy(
            src_ref=source,
            dst_ref=target,
            send_sem=self.send_sem.at[self.count],
            recv_sem=self.recv_sem.at[self.count],
            device_id=peer,
            device_id_type=MESH,
        )
        self.count += 1
        copy.start()
        self.open.append(copy)
        return copy

    def settle(self, *copies):
        for copy in copies:
            copy.wait_send()
        self.open = [other for other in self.open if all(other is not copy for copy in copies)]

    def finish(self):
        self.settle(*self.open)


class Moves:
    def __init__(self, sem):
        self.sem, self.count, self.open = sem, 0, []

    def start(self, source, target):
        copy = pltpu.make_async_copy(source, target, self.sem.at[self.count])
        self.count += 1
        copy.start()
        self.open.append(copy)
        return copy

    def wait(self, copy):
        copy.wait()
        self.open = [other for other in self.open if other is not copy]

    def finish(self):
        for copy in list(self.open):
            self.wait(copy)


def part(ref, lead, axis, first, count):
    window = pl.ds(first, count)
    return ref.at[lead + ((window, slice(None)) if axis == 0 else (slice(None), window))]


def piece_of(place, order):
    total = 0
    for b in order:
        total = 2 * total + place.bit(b)
    return total


class Gather:
    def __init__(self, place, links, ref, lead, axis, order):
        self.place, self.links, self.ref, self.lead, self.axis, self.order = place, links, ref, lead, axis, order
        self.size = ref.shape[len(ref.shape) - 2 + axis] // (1 << len(order))
        self.piece = piece_of(place, order)
        self.copy, self.stage, self.sent = None, 0, []

    def block(self, shard, width):
        first = (self.piece // width) * (width * self.size)
        return part(self.ref, (shard,) + self.lead, self.axis, pl.multiple_of(first, self.size), width * self.size)

    def begin(self):
        self.copy = self.links.start(self.block(0, 1), self.block(1, 1), self.place.twin)
        self.sent.append(self.copy)

    def advance(self):
        self.copy.wait_recv()
        if self.stage < len(self.order):
            block = self.block(1, 1 << self.stage)
            self.copy = self.links.start(block, block, self.place.over(self.order[-1 - self.stage]))
            self.sent.append(self.copy)
        self.stage += 1


def rows_loop(count, size, body):
    def step(k, carry):
        body(pl.multiple_of(k * size, size))
        return carry

    lax.fori_loop(0, count // size, step, 0)


def softplus_and_slope(values):
    tail = jnp.exp(-jnp.abs(values))
    soft = jnp.maximum(values, 0.0) + jnp.log1p(tail)
    slope = jnp.where(values >= 0, 1.0, tail) / (1.0 + tail)
    return soft, slope


def sigmoid(values):
    tail = jnp.exp(-jnp.abs(values))
    return jnp.where(values >= 0, 1.0, tail) / (1.0 + tail)


def head_of(shape, axis):
    return lax.broadcasted_iota(jnp.int32, shape, axis) // HEAD


def same_head(width):
    return head_of((width, width), 0) == head_of((width, width), 1)


def head_mean(values):
    ones = jnp.where(same_head(values.shape[-1]), 1.0 / HEAD, 0.0).astype(BF)
    return dot(values.astype(BF), ones)


def fold(state):
    width = state.shape[-1]
    state = jnp.where(same_head(width), state, 0.0)
    return (state[:, : width // 2] + state[:, width // 2 :]).astype(BF)


def unfold(state):
    both = jnp.concatenate((state, state), axis=1)
    return jnp.where(same_head(both.shape[-1]), both, jnp.zeros_like(both))


def only_head(values, head):
    return jnp.where(head_of(values.shape, 1) == head, values, jnp.zeros_like(values))


class Reduce:
    def __init__(self, place, links, moves, grad, axis, order, halves, credits, twin_recv, out, other=None):
        self.place, self.links, self.moves = place, links, moves
        self.grad, self.axis, self.order = grad, axis, order
        self.halves, self.twin_recv, self.out = halves, twin_recv, out
        self.extra = credits
        self.size = grad.shape[1 + axis] // (1 << len(order))
        self.piece = piece_of(place, order)
        self.stage, self.copy, self.local = 0, None, None
        self.other, self.ends = other, out is None
        self.steps = len(order) + len(self.extra) + (0 if self.ends else 1 + len(order))

    def first_of(self, width):
        return pl.multiple_of((self.piece // width) * (width * self.size), self.size)

    def grad_part(self, lead, first, width):
        return part(self.grad, lead, self.axis, pl.multiple_of(first, self.size), width * self.size)

    def out_part(self, width):
        return part(self.out, (), self.axis, self.first_of(width), width * self.size)

    def begin(self):
        shards, folds = (slice(None),), len(self.order)
        k = self.stage
        if k < folds:
            width = 1 << (folds - 1 - k)
            bit = self.place.bit(self.order[k])
            away = self.first_of(width) + (1 - 2 * bit) * (width * self.size)
            self.copy = self.links.start(
                self.grad_part(shards, away, width), self.halves[k], self.place.over(self.order[k])
            )
            return
        k -= folds
        if k < len(self.extra):
            peer = self.place.over(folds + k)
            pl.semaphore_signal(self.extra[k], inc=1, device_id=peer, device_id_type=MESH)
            pl.semaphore_wait(self.extra[k], 1)
            source = self.grad_part(shards, self.first_of(1), 1)
            self.copy = self.links.start(source, self.halves[-1], peer)
            return
        k -= len(self.extra)
        if k == 0:
            if self.other is not None:
                while not self.other.over():
                    self.other.advance()
                self.copy = self.other.copy
            else:
                source = self.grad_part((self.grad.shape[0] - 1,), self.first_of(1), 1)
                self.copy = self.links.start(source, self.twin_recv, self.place.twin)
            return
        k -= 1
        block = self.out_part(1 << k)
        source = self.grad_part((0,), self.first_of(1), 1) if k == 0 else block
        self.copy = self.links.start(source, block, self.place.over(self.order[folds - 1 - k]))
        if k == 0:
            self.local = self.moves.start(source, block)

    def add(self, recv, width):
        rows, chunk = recv.shape[-2], 32
        first = self.first_of(width)

        def body(at):
            for shard in range(recv.shape[0] if len(recv.shape) == 3 else 1):
                if self.axis == 0:
                    where = (shard, pl.ds(pl.multiple_of(first + at, chunk), chunk), slice(None))
                else:
                    where = (shard, pl.ds(at, chunk), pl.ds(first, width * self.size))
                came = recv[(shard,) * (len(recv.shape) - 2) + (pl.ds(at, chunk), slice(None))]
                self.grad[where] = self.grad[where] + came

        rows_loop(rows, chunk, body)

    def advance(self):
        if self.stage >= self.steps:
            return
        folds = len(self.order)
        self.copy.wait_recv()
        k = self.stage
        if k < folds:
            self.add(self.halves[k], 1 << (folds - 1 - k))
        elif k < folds + len(self.extra):
            self.links.settle(self.copy)
            self.add(self.halves[-1], 1)
        elif k == folds + len(self.extra):
            self.add(self.twin_recv, 1)
        elif self.local is not None:
            self.moves.wait(self.local)
            self.local = None
        self.stage += 1
        if self.stage < self.steps or self.ends:
            self.begin()

    def over(self):
        return self.stage >= self.steps


def marks_of(place, segr_ref, segc, tokens):
    offset = pl.multiple_of(place.pair * tokens, tokens)
    across = segr_ref[:, pl.ds(offset, tokens)].astype(F32)
    segc[...] = jnp.broadcast_to(across, (8, tokens)).T[:, :1]
    return across, segr_ref[:, tokens - 1 : tokens].astype(F32)


def doc_mask(across, segc, mask_ref, tokens, later):
    def body(first):
        at = first + lax.broadcasted_iota(jnp.int32, (64, tokens), 0)
        col = lax.broadcasted_iota(jnp.int32, (64, tokens), 1)
        order = col >= at if later else col <= at
        same = segc[pl.ds(first, 64), :] == across
        mask_ref[pl.ds(first, 64), :] = jnp.where(same & order, 1.0, 0.0).astype(BF)

    rows_loop(tokens, 64, body)


def layer_kernel(
    dp_size, extras, hidden, pad,
    x_hbm, segr_ref, wq, wk, wv, wz, wo, wl, wr, wd, g1_ref, g2_ref, cot_hbm,
    down_out, left_out, right_out, ow_out, query_out, key_out, value_out, gate_out, block_out, grad_out, gains_out,
    x_ref, segc, normed, normed_t, joined, ow, lrw, dw, qp, kp, vl, sq, sk, hn, rr, sz, gated, mask, mask_t,
    state_send, state_recv, meet_send, meet_recv, trade_send, trade_recv, back_send, back_recv,
    resid, own_sum, second, cot, hid, dres, dm, djoined, dq, dk, dv, gains, gains_recv,
    grad_d, grad_l, grad_r, grad_o,
    *rest,
):
    *received, send_sem, recv_sem, move_sem, free_sem, credit_sem = rest
    received, tickets = list(received), itertools.count()
    place = Place(dp_size)
    links, moves = Links(send_sem, recv_sem), Moves(move_sem)
    own, width = x_ref.shape
    tokens = 2 * own
    local = qp.shape[-1]
    mine = pl.multiple_of(place.half * own, own)
    theirs = pl.multiple_of((1 - place.half) * own, own)
    lw, rw = lrw.at[:, :hidden, :], lrw.at[:, hidden:, :]
    product, dleft, dright = (slice(n * pad, n * pad + hidden) for n in range(3))
    dres_all = normed

    all_here = place.greet()
    x_in = moves.start(x_hbm, x_ref)
    joined_in = [moves.start(w, joined.at[0, j]) for j, w in enumerate((wq, wk, wv, wz))]
    ow_in = moves.start(wo, ow.at[0])
    ffn_in = [moves.start(w, v.at[0]) for w, v in ((wl, lw), (wr, rw), (wd, dw))]
    cot_in = moves.start(cot_hbm, cot.at[pl.ds(mine, own), :])
    moves.wait(x_in)

    def first_norm(first):
        values = x_ref[pl.ds(first, 32), :].astype(F32)
        scale = lax.rsqrt(jnp.mean(values * values, axis=-1, keepdims=True) + EPS)
        normed[pl.ds(mine + first, 32), :] = (values * scale * g1_ref[...]).astype(BF)

    rows_loop(own, 32, first_norm)
    for copy in joined_in:
        moves.wait(copy)
    all_here()
    block = normed.at[pl.ds(mine, own), :]
    normed_copy = links.start(block, block, place.mate)
    first_order, second_order = (0, 1, 2), (0, 2, 1)
    join_a = Gather(place, links, joined, (pl.ds(0, 2),), 0, first_order)
    join_b = Gather(place, links, joined, (pl.ds(2, 2),), 0, second_order)
    gather_o = Gather(place, links, ow, (), 1, second_order)
    gather_l = Gather(place, links, lw, (), 1, first_order)
    gather_r = Gather(place, links, rw, (), 1, second_order)
    gather_d = Gather(place, links, dw, (), 1, first_order)
    join_a.begin()
    join_b.begin()
    moves.wait(ow_in)
    gather_o.begin()

    def advance(*units):
        for unit in units:
            unit.advance()

    def project(shard, first, which):
        rows = normed[pl.ds(first, own), :]
        at = pl.ds(first, own)
        for j in which:
            raw = dot(rows, joined[shard, j])
            if j == 2:
                vl[shard, at, :] = raw.astype(BF)
            elif j == 3:
                sz[shard, at, :] = sigmoid(raw).astype(BF)
            else:
                soft, slope = softplus_and_slope(raw)
                (qp, kp)[j][shard, at, :] = soft.astype(BF)
                (sq, sk)[j][shard, at, :] = slope.astype(BF)

    project(0, mine, (1, 2, 0, 3))
    across, last = marks_of(place, segr_ref, segc, tokens)
    doc_mask(across, segc, mask, tokens, False)
    near = segc[...] == last
    edge = segc[...] == segc[own - 1 : own, :]
    halves_of = (slice(0, own), slice(own, tokens))
    state_copy = [None, None]

    def marked(values, marks):
        return jnp.where(marks, values.astype(F32), 0.0).astype(BF)

    def blocks(left, right):
        return jnp.where(same_head(local), dot(left.T, right), 0.0).astype(BF)

    def middle_state(shard):
        return blocks(marked(kp[shard, :own, :], edge[:own]), vl[shard, :own, :])

    def send_state(shard):
        keys = jnp.where(near, kp[shard].astype(F32), 0.0).astype(BF)
        state_send[shard] = fold(dot(keys.T, vl[shard]))
        state_copy[shard] = links.start(state_send.at[shard], state_recv.at[1 - shard], place.twin)

    attention = (join_a, join_b, gather_o)
    normed_copy.wait_recv()
    advance(*attention)
    for copy in ffn_in:
        moves.wait(copy)
    gather_l.begin()
    gather_r.begin()
    gather_d.begin()
    project(0, theirs, (1, 2))
    send_state(0)
    advance(*attention)
    moves.wait(cot_in)
    cot_block = cot.at[pl.ds(mine, own), :]
    cot_copy = links.start(cot_block, cot_block, place.mate)
    project(0, theirs, (0, 3))

    def mix(shard, total):
        def one(head, carry):
            for at in halves_of:
                raw = dot_t(only_head(qp[shard, at, :], head), kp[shard, at, :])
                scores = raw.astype(BF) * mask[at, at]
                total[at, :] += dot(scores, only_head(vl[shard, at, :], head))
            return carry

        total[:own, :] = jnp.zeros((own, local), F32)
        total[own:, :] = dot(marked(qp[shard, own:, :], edge[own:]), middle_state(shard))
        lax.fori_loop(0, local // HEAD, one, 0)

    first_half, second_half = place.pair == 0, place.pair == 1

    def open_gate(shard, total):
        state_copy[1 - shard].wait_recv()
        query = jnp.where(near & second_half, qp[shard].astype(F32), 0.0).astype(BF)
        mixed = total[...] + dot(query, unfold(state_recv[shard]))
        scale = lax.rsqrt(head_mean(mixed * mixed) + EPS)
        norm = mixed * scale
        rr[shard] = scale.astype(BF)
        hn[shard] = norm.astype(BF)
        gated[shard] = (norm * sz[shard].astype(F32)).astype(BF)

    mix(0, dk)
    advance(*attention)
    advance(gather_l)
    advance(*attention)
    for first in (mine, theirs):
        project(1, first, (1, 2))
    send_state(1)
    advance(gather_r)
    for first in (mine, theirs):
        project(1, first, (0, 3))
    advance(gather_l)
    mix(1, dq)
    advance(gather_r)
    open_gate(1, dq)
    open_gate(0, dk)

    def branch(first, count=own):
        at = pl.ds(first, count)
        return dot(gated[0, at, :], ow[0]) + dot(gated[1, at, :], ow[1])

    part_rows = own // 2
    parts = [slice(0, part_rows), slice(part_rows, own)]

    def halved(partial_sum, send, recv):
        copies = []
        for rows in parts:
            send[rows, :] = partial_sum(pl.multiple_of(theirs + rows.start, part_rows), part_rows).astype(BF)
            copies.append(links.start(send.at[rows, :], recv.at[rows, :], place.mate))
        return copies

    def share(ref):
        def after(n):
            block = ref.at[pl.ds(pl.multiple_of(mine + n * part_rows, part_rows), part_rows), :]
            return links.start(block, block, place.mate)

        return after

    branch_copies = halved(branch, trade_send, trade_recv)
    advance(gather_d, gather_l)
    own_sum[...] = branch(mine)
    advance(gather_r, gather_d)
    for c in range(0, width, 256):
        normed_t[c : c + 256, :] = normed[:, c : c + 256].T
    doc_mask(across, segc, mask_t, tokens, True)
    advance(gather_d, gather_l, gather_r)

    def second_norm(first):
        at = pl.ds(first, 32)
        values = x_ref[at, :].astype(F32) + own_sum[at, :] + trade_recv[at, :].astype(F32)
        resid[at, :] = values
        scale = lax.rsqrt(jnp.mean(values * values, axis=-1, keepdims=True) + EPS)
        second[pl.ds(mine + first, 32), :] = (values * scale * g2_ref[...]).astype(BF)

    second_copies = []
    for n, copy in enumerate(branch_copies):
        copy.wait_recv()
        rows_loop(part_rows, 32, lambda first, n=n: second_norm(pl.multiple_of(n * part_rows + first, 32)))
        second_copies.append(share(second)(n))
    cot_copy.wait_recv()
    advance(gather_d)

    def hidden_grad(first):
        at = pl.ds(first, own)

        def one(shard, carry):
            hid[shard, at, dleft] = dot_t(cot[at, :], dw[shard]).astype(BF)
            return carry

        lax.fori_loop(0, 2, one, 0)

    def unit_rows(first):
        at = pl.ds(first, own)

        def one(shard, carry):
            left = dot_t(second[at, :], lw[shard])
            right = dot_t(second[at, :], rw[shard])
            grad = hid[shard, at, dleft].astype(F32)
            hid[shard, at, product] = (left * right).astype(BF)
            hid[shard, at, dleft] = (grad * right).astype(BF)
            hid[shard, at, dright] = (grad * left).astype(BF)
            return carry

        lax.fori_loop(0, 2, one, 0)

    hidden_grad(mine)
    unit_rows(mine)
    hidden_grad(theirs)
    for copy in second_copies:
        copy.wait_recv()
    unit_rows(theirs)

    def back(first, count=own):
        at = pl.ds(first, count)
        return (
            dot(hid[0, at, dleft], lw[0])
            + dot(hid[0, at, dright], rw[0])
            + dot(hid[1, at, dleft], lw[1])
            + dot(hid[1, at, dright], rw[1])
        )

    def ffn(first):
        at = pl.ds(first, own)
        return dot(hid[0, at, product], dw[0]) + dot(hid[1, at, product], dw[1])

    back_copies = halved(back, back_send, back_recv)
    own_sum[...] = back(mine)

    def make_unit(grad, axis, order, out, first_half_ref=None, twin_recv=None, other=None):
        folds = len(order)
        halves = [received.pop(0) for _ in range(folds - (first_half_ref is not None))]
        if first_half_ref is not None:
            halves = [first_half_ref] + halves
        credits = [credit_sem.at[next(tickets)] for _ in range(extras)]
        twin_recv = received.pop(0) if twin_recv is None else twin_recv
        return Reduce(place, links, moves, grad, axis, order, halves, credits, twin_recv, out, other)

    def split_units(grad, out):
        rows = grad.shape[1] // 2
        return [
            make_unit(grad.at[:, n * rows : (n + 1) * rows, :], 1, order, out.at[n * rows : (n + 1) * rows, :])
            for n, order in enumerate((first_order, second_order))
        ]

    down_units, left_units, right_units = (
        split_units(g, o) for g, o in ((grad_d, down_out), (grad_l, left_out), (grad_r, right_out))
    )
    ow_units = split_units(grad_o, ow_out)
    joined_units = []
    for j, (order, out) in enumerate(
        zip((first_order, second_order, first_order, second_order), (query_out, key_out, value_out, gate_out))
    ):
        columns = slice(j * local, (j + 1) * local)
        grad, landing = lrw.at[:, :width, columns], hid.at[:, : width // 2, columns]
        if j == 3:
            joined_units.append(make_unit(grad, 0, order, out, landing))
            continue
        away = make_unit(grad.at[1:2], 0, order, None, landing.at[1:2])
        near_unit = make_unit(grad.at[0:1], 0, order, out, landing.at[0:1], away.twin_recv, away)
        joined_units.append((near_unit, away))
    live = []

    def launch(*units):
        for unit in units:
            unit.begin()
            live.append(unit)

    def step_all(late=False):
        for unit in live[:6] + live[:5:-1] if late else live:
            unit.advance()

    def hidden_outer(units, grad, left, right):
        def one(shard, carry):
            for c in range(0, hidden, 256):
                high = min(c + 256, hidden)
                grad[shard, c:high, :] = dot(hid[shard, :, left.start + c : left.start + high].T, right[...]).astype(BF)
            return carry

        lax.fori_loop(0, 2, one, 0)
        launch(*units)

    hidden_outer(down_units, grad_d, product, cot)
    hidden_outer(left_units, grad_l, dleft, second)
    advance(*down_units)
    hidden_outer(right_units, grad_r, dright, second)
    advance(*left_units)
    pl.semaphore_signal(free_sem, inc=1, device_id=place.over(0), device_id_type=MESH)
    gains[0] = jnp.zeros(gains.shape[1:], F32)

    def residual_back(first):
        at = pl.ds(first, 32)
        values = resid[at, :]
        scale = lax.rsqrt(jnp.mean(values * values, axis=-1, keepdims=True) + EPS)
        grad = own_sum[at, :] + back_recv[at, :].astype(F32)
        gains[0, 0:1, :] += jnp.sum(grad * values * scale, axis=0, keepdims=True)
        weighted = grad * g2_ref[...]
        inner = jnp.mean(weighted * values, axis=-1, keepdims=True)
        upstream = cot[pl.ds(mine + first, 32), :].astype(F32)
        total = upstream + scale * weighted - values * (scale * scale * scale * inner)
        dres[at, :] = total
        dres_all[pl.ds(mine + first, 32), :] = total.astype(BF)

    links.settle(normed_copy)
    dres_copies = []
    for n, copy in enumerate(back_copies):
        copy.wait_recv()
        rows_loop(part_rows, 32, lambda first, n=n: residual_back(pl.multiple_of(n * part_rows + first, 32)))
        dres_copies.append(share(dres_all)(n))
    advance(*right_units)
    links.settle(*back_copies)
    back_send[...] = ffn(theirs).astype(BF)

    def add_ffn(first):
        resid[...] += ffn(first)

    add_ffn(mine)
    advance(*down_units)
    for copy in dres_copies:
        copy.wait_recv()
    ffn_copy = links.start(back_send, back_recv, place.mate)

    def gate_back(shard, carry):
        grad = dot_t(dres_all[...], ow[shard])
        opened, norm = sz[shard].astype(F32), hn[shard].astype(F32)
        djoined[shard, 3] = (grad * norm * opened * (1.0 - opened)).astype(BF)
        inner = grad * opened
        dm[shard] = (rr[shard].astype(F32) * (inner - norm * head_mean(inner * norm))).astype(BF)
        return carry

    lax.fori_loop(0, 2, gate_back, 0)
    meets = []
    for shard in range(2):
        query = jnp.where(near, qp[shard].astype(F32), 0.0).astype(BF)
        meet_send[shard] = fold(dot(query.T, dm[shard]))
        meets.append(links.start(meet_send.at[shard], meet_recv.at[1 - shard], place.twin))

    def out_outer(shard, carry):
        grad_o[shard] = dot(gated[shard].T, dres_all[...]).astype(BF)
        return carry

    lax.fori_loop(0, 2, out_outer, 0)
    launch(*ow_units)
    gathers = (join_a, join_b, gather_o, gather_l, gather_r, gather_d)
    for unit in gathers:
        links.settle(*unit.sent)
    pl.semaphore_wait(free_sem, 1)

    def project_back(j, shard):
        def body(first):
            part_grad = dot(normed_t[pl.ds(first, 256), :], djoined[shard, j])
            lrw[shard, pl.ds(first, 256), j * local : (j + 1) * local] = part_grad.astype(BF)

        rows_loop(width, 256, body)

    project_back(3, 0)
    project_back(3, 1)
    launch(joined_units[3])
    step_all()

    def mix_back(shard):
        dq[...] = jnp.where(near & second_half, dot_t(dm[shard], unfold(state_recv[shard])), 0.0)
        dq[own:, :] += jnp.where(edge[own:], dot_t(dm[shard, own:, :], middle_state(shard)), 0.0)
        meeting = blocks(marked(qp[shard, own:, :], edge[own:]), dm[shard, own:, :])
        dk[:own, :] = jnp.where(edge[:own], dot_t(vl[shard, :own, :], meeting), 0.0)
        dv[:own, :] = jnp.where(edge[:own], dot(kp[shard, :own, :], meeting), 0.0)
        dk[own:, :] = jnp.zeros((own, local), F32)
        dv[own:, :] = jnp.zeros((own, local), F32)

        def one(head, carry):
            for at in halves_of:
                grad_r, query_r = dm[shard, at, :], qp[shard, at, :]
                grad_h, query_h = only_head(grad_r, head), only_head(query_r, head)
                keys_h = only_head(kp[shard, at, :], head)
                vals_h = only_head(vl[shard, at, :], head)
                ds = dot_t(grad_r, vals_h).astype(BF) * mask[at, at]
                dq[at, :] += dot(ds, keys_h)
                st = dot_t(keys_h, query_r).astype(BF) * mask_t[at, at]
                dv[at, :] += dot(st, grad_h)
                dst = dot_t(vals_h, grad_r).astype(BF) * mask_t[at, at]
                dk[at, :] += dot(dst, query_h)
            return carry

        lax.fori_loop(0, local // HEAD, one, 0)

    for shard in (1, 0):
        mix_back(shard)
        meets[1 - shard].wait_recv()
        meet = unfold(meet_recv[shard])
        marks = near & first_half
        djoined[shard, 2] = (dv[...] + jnp.where(marks, dot(kp[shard], meet), 0.0)).astype(BF)
        from_meet = jnp.where(marks, dot_t(vl[shard], meet), 0.0)
        djoined[shard, 1] = ((dk[...] + from_meet) * sk[shard].astype(F32)).astype(BF)
        djoined[shard, 0] = (dq[...] * sq[shard].astype(F32)).astype(BF)
        for j in range(3):
            project_back(j, shard)
            launch(joined_units[j][shard])

    def normed_back(first):
        at = pl.ds(first, own)
        own_sum[...] = jnp.zeros(own_sum.shape, F32)

        def one(k, carry):
            own_sum[...] += dot_t(djoined[k // 4, lax.rem(k, 4), at, :], joined[k // 4, lax.rem(k, 4)])
            return carry

        lax.fori_loop(0, 8, one, 0)

    links.settle(*branch_copies)
    normed_back(theirs)
    trade_send[...] = own_sum[...].astype(BF)
    trade_copy = links.start(trade_send, trade_recv, place.mate)
    step_all(True)
    normed_back(mine)
    ffn_copy.wait_recv()
    links.settle(ffn_copy)

    def finish_out(first):
        at = pl.ds(first, 32)
        back_send[at, :] = (resid[at, :] + back_recv[at, :].astype(F32)).astype(BF)

    rows_loop(own, 32, finish_out)
    moves.start(back_send, block_out)
    step_all(True)
    trade_copy.wait_recv()
    links.settle(trade_copy)

    def finish_grad(first):
        at = pl.ds(first, 32)
        values = x_ref[at, :].astype(F32)
        scale = lax.rsqrt(jnp.mean(values * values, axis=-1, keepdims=True) + EPS)
        grad = own_sum[at, :] + trade_recv[at, :].astype(F32)
        gains[0, 1:2, :] += jnp.sum(grad * values * scale, axis=0, keepdims=True)
        weighted = grad * g1_ref[...]
        inner = jnp.mean(weighted * values, axis=-1, keepdims=True)
        trade_send[at, :] = (dres[at, :] + scale * weighted - values * (scale * scale * scale * inner)).astype(BF)

    rows_loop(own, 32, finish_grad)
    moves.start(trade_send, grad_out)

    first = 0
    for n, peers in enumerate((place.rows, place.columns)):
        copies = [links.start(gains.at[n], gains_recv.at[first + k], peer) for k, peer in enumerate(peers)]
        step_all(True)
        for copy in copies:
            copy.wait_recv()
        gains[n + 1] = gains[n] + jnp.sum(gains_recv[first : first + len(peers)], axis=0)
        first += len(peers)
    moves.start(gains.at[2], gains_out)
    while not all(unit.over() for unit in live):
        step_all(True)
    moves.finish()
    links.finish()


def widen_kernel(count, passed, *refs):
    sources, refs = refs[: count + passed], refs[count + passed :]
    targets, refs = refs[: count + passed], refs[count + passed :]
    total = count + passed
    narrow, wide, (in_sem, out_sem) = refs[:total], refs[total : total + count], refs[total + count :]
    loads = [pltpu.make_async_copy(sources[n], narrow[n], in_sem.at[n]) for n in range(total)]
    results = list(wide) + list(narrow[count:])
    stores = [pltpu.make_async_copy(results[n], targets[n], out_sem.at[n]) for n in range(total)]
    for copy in loads:
        copy.start()
    for n in range(count):
        loads[n].wait()

        def body(first, n=n):
            wide[n][pl.ds(first, 64), :] = narrow[n][pl.ds(first, 64), :].astype(F32)

        rows_loop(narrow[n].shape[0], 64, body)
        stores[n].start()
    for n in range(count, total):
        loads[n].wait()
        stores[n].start()
    for copy in stores:
        copy.wait()


def vmem(shape, dtype=BF):
    return pltpu.VMEM(shape, dtype)


def per_device(
    dp_size,
    inputs, segments, query_weight, key_weight, value_weight, gate_weight, out_weight, left_weight, right_weight,
    down_weight, norm_first, norm_second, cotangent,
):
    own, width = inputs.shape
    tokens = 2 * own
    local = query_weight.shape[1]
    hidden = left_weight.shape[1]
    pad = -(-hidden // 128) * 128
    bits = dp_size.bit_length() - 1
    extras = bits - PIECE_BITS
    shape = jax.ShapeDtypeStruct
    heads, state = (2, tokens, local), (2, local, local // 2)
    grads = [(hidden, width)] * 3 + [(local, width)] + [(width, local)] * 4

    def buffers(rows, columns, axis, first, shards=2):
        def cut(parts):
            return (shards, rows // parts, columns) if axis == 0 else (shards, rows, columns // parts)

        eighth = cut(1 << PIECE_BITS)
        kept = [vmem(cut(2 << k)) for k in range(first, PIECE_BITS)]
        return kept + [vmem(eighth[1:])]

    received = []
    for rows in (hidden // 2,) * 6 + (local // 2,) * 2:
        received += buffers(rows, width, 1, 0)
    for _ in range(3):
        away = buffers(width, local, 0, 1, 1)
        received += away + away[:-1]
    received += buffers(width, local, 0, 1)
    copies = 15 * (2 * PIECE_BITS + extras + 1) + 6 * (PIECE_BITS + 1) + dp_size + 20
    results = pl.pallas_call(
        functools.partial(layer_kernel, dp_size, extras, hidden, pad),
        out_shape=[shape(full, BF) for full in grads]
        + [shape((own, width), BF), shape((own, width), BF), shape((2, width), F32)],
        in_specs=[ANY, INNER] + [ANY] * 8 + [INNER, INNER, ANY],
        out_specs=[ANY] * 11,
        scratch_shapes=[
            vmem((own, width)), vmem((tokens, 1), F32), vmem((tokens, width)), vmem((width, tokens)),
            vmem((2, 4, width, local)), vmem((2, local, width)), vmem((2, 2 * hidden, width)),
            vmem((2, hidden, width)),
        ]
        + [vmem(heads)] * 9
        + [vmem((tokens, tokens))] * 2
        + [vmem(state)] * 4
        + [vmem((own, width))] * 4
        + [vmem((own, width), F32)] * 2
        + [
            vmem((tokens, width)), vmem((tokens, width)), vmem((2, tokens, 3 * pad)), vmem((own, width), F32),
            vmem(heads), vmem((2, 4, tokens, local)),
        ]
        + [vmem((tokens, local), F32)] * 3
        + [vmem((3, 2, width), F32), vmem((dp_size + 2, 2, width), F32)]
        + [vmem((2, hidden, width))] * 3
        + [vmem((2, local, width))]
        + received
        + [pltpu.SemaphoreType.DMA((copies,))] * 2
        + [
            pltpu.SemaphoreType.DMA((40,)), pltpu.SemaphoreType.REGULAR,
            pltpu.SemaphoreType.REGULAR((max(1, 15 * extras),)),
        ],
        compiler_params=pltpu.CompilerParams(collective_id=0, has_side_effects=True, vmem_limit_bytes=63 << 20),
    )(
        inputs, segments, query_weight, key_weight, value_weight, gate_weight, out_weight, left_weight.T,
        right_weight.T, down_weight, norm_first.reshape(1, -1), norm_second.reshape(1, -1), cotangent,
    )
    count, passed = len(grads), 3
    wide = pl.pallas_call(
        functools.partial(widen_kernel, count, passed),
        out_shape=[shape(full, F32) for full in grads] + [shape(r.shape, r.dtype) for r in results[count:]],
        in_specs=[ANY] * (count + passed),
        out_specs=[ANY] * (count + passed),
        scratch_shapes=[vmem(r.shape, r.dtype) for r in results]
        + [vmem(full, F32) for full in grads]
        + [pltpu.SemaphoreType.DMA((count + passed,))] * 2,
        compiler_params=pltpu.CompilerParams(vmem_limit_bytes=62 << 20),
    )(*results)
    down, left, right, out, query, key, value, gate, block, block_grad, gains = wide
    return (
        block, block_grad, query, key, value, gate, out, left.T, right.T, down, gains[1], gains[0],
    )


def solution(mesh):
    row, column = P("tensor", None), P(None, "tensor")
    tokens = P(("dp", "tensor"), None)
    return jax.shard_map(
        functools.partial(per_device, mesh.shape["dp"]),
        mesh=mesh,
        in_specs=(
            tokens, P("dp", None), column, column, column, column, row, column, column, row, P(), P(), tokens,
        ),
        out_specs=(tokens, tokens, column, column, column, column, row, column, column, row, P(), P()),
        check_vma=False,
    )
```
